32 devices in a mesh: dp: 8 (over z, y), frame: 4 (over x, core).
Axes of the slice: x: 2, y: 2, z: 4, core: 2. Of those that a mesh axis runs over, the one named last changes fastest.
Arguments:
- mel_frames: bfloat16 [16, 3008, 80], P('dp', 'frame'), may hold values from -6 to 6
- window_count: int32 [8], P('dp'), may hold values from 1 to 2, as said below
- stem_weight: bfloat16 [3, 80, 512], replicated, may hold values from -0.375 to 0.375
- stem_bias: float32 [512], replicated, may hold values from -1.5 to 1.5
- reduce_weight: bfloat16 [3, 512, 512], replicated, may hold values from -0.15625 to 0.15625
- reduce_bias: float32 [512], replicated, may hold values from -1.5 to 1.5
- first_gain: float32 [512], replicated, may hold values from 0.5 to 1.5
- first_shift: float32 [512], replicated, may hold values from -1.5 to 1.5
- query_weight: bfloat16 [512, 512], replicated, may hold values from -0.25 to 0.25
- query_bias: float32 [512], replicated, may hold values from -1.5 to 1.5
- key_weight: bfloat16 [512, 512], replicated, may hold values from -0.25 to 0.25
- value_weight: bfloat16 [512, 512], replicated, may hold values from -0.25 to 0.25
- value_bias: float32 [512], replicated, may hold values from -1.5 to 1.5
- output_weight: bfloat16 [512, 512], replicated, may hold values from -4 to 4
- output_bias: float32 [512], replicated, may hold values from -1.5 to 1.5
- second_gain: float32 [512], replicated, may hold values from 0.5 to 1.5
- second_shift: float32 [512], replicated, may hold values from -1.5 to 1.5
- hidden_weight: bfloat16 [512, 2048], replicated, may hold values from -0.25 to 0.25
- hidden_bias: float32 [2048], replicated, may hold values from -1.5 to 1.5
- return_weight: bfloat16 [2048, 512], replicated, may hold values from -0.125 to 0.125
- return_bias: float32 [512], replicated, may hold values from -1.5 to 1.5
- cotangent: bfloat16 [16, 1504, 512], P('dp', 'frame'), may hold values from -6 to 6
Outputs:
- layer_output: bfloat16 [16, 1504, 512], P('dp', 'frame')
- mel_gradient: float32 [16, 3008, 80], P('dp', 'frame')
- stem_weight_gradient: float32 [3, 80, 512], replicated
- stem_bias_gradient: float32 [512], replicated
- reduce_weight_gradient: float32 [3, 512, 512], replicated
- reduce_bias_gradient: float32 [512], replicated
- first_gain_gradient: float32 [512], replicated
- first_shift_gradient: float32 [512], replicated
- query_weight_gradient: float32 [512, 512], replicated
- query_bias_gradient: float32 [512], replicated
- key_weight_gradient: float32 [512, 512], replicated
- value_weight_gradient: float32 [512, 512], replicated
- value_bias_gradient: float32 [512], replicated
- output_weight_gradient: float32 [512, 512], replicated
- output_bias_gradient: float32 [512], replicated
- second_gain_gradient: float32 [512], replicated
- second_shift_gradient: float32 [512], replicated
- hidden_weight_gradient: float32 [512, 2048], replicated
- hidden_bias_gradient: float32 [2048], replicated
- return_weight_gradient: float32 [2048, 512], replicated
- return_bias_gradient: float32 [512], replicated
The draws below stay inside these ranges and needn't reach their ends.
Inputs may be any that keep to these rules, and one draw needn't show every extreme that they name: `window_count`: slots of a data group at or beyond its count hold no window. Some group has exactly 2 windows and some group exactly 1.
All inputs are finite; a program needn't handle non-finite values.
Results may differ from the reference program's by a relative error of at most 0.013.
Values may be sent and summed in bfloat16 or wider, within the bound.
A program may use at most 192 MiB of HBM per device.

```python
import math
import jax
import jax.numpy as jnp
from jax import lax

D = 512
HEADS = 8
FF = 2048
MELS = 80
HEAD_DIM = 64
WIN_FR = 3008
WIN_TOK = 1504
MAXW = 2
WINDOWS = 16
N_DP = 8


def draw_window_count(key, part):
    first_key = jax.random.fold_in(key, 11)
    second_key = jax.random.fold_in(key, 12)
    third_key = jax.random.fold_in(key, 13)
    counts = jax.random.randint(first_key, (N_DP,), 1, MAXW + 1)
    busiest = jax.random.randint(second_key, (), 0, N_DP)
    offset = jax.random.randint(third_key, (), 1, N_DP)
    lightest = (busiest + offset) % N_DP
    places = jnp.arange(N_DP, dtype=jnp.int32)
    counts = jnp.where(places == lightest, 1, counts)
    counts = jnp.where(places == busiest, MAXW, counts)
    return counts.astype(jnp.int32)


def level_of(stream_key, shape, cuts, low, largest):
    def one(axis_at, shards_of):
        draws = jax.random.uniform(jax.random.fold_in(jax.random.fold_in(stream_key, 6), axis_at), (shards_of,), jnp.float32, low / len(cuts), largest / len(cuts))
        return jnp.repeat(jnp.exp(draws), shape[axis_at] // shards_of).reshape((-1,) + (1,) * (len(shape) - axis_at - 1))

    loudness = one(*cuts[0])
    for cut in cuts[1:]:
        loudness = loudness * one(*cut)
    return loudness


def noise(stream_key, shape, spread, most, pieces=(), kind=jnp.bfloat16):
    entries = jax.random.normal(stream_key, shape, jnp.float32) * spread
    if len(pieces) > 0:
        entries = level_of(stream_key, shape, pieces, -0.22, 0.18) * entries
    return jnp.clip(entries, min=-most, max=most).astype(kind)


def setup_inputs(seed: int = 0) -> dict:
    streams_of = jax.random.split(jax.random.key(seed), 23)
    mel_frames = noise(streams_of[0], (WINDOWS, WIN_FR, MELS), 1.0, 6.0, ((0, 8), (1, 4)))
    window_count = draw_window_count(jax.random.fold_in(streams_of[22], 71), 0)
    stem_weight = noise(streams_of[2], (3, MELS, D), (3 * MELS) ** -0.5, 0.375)
    stem_bias = noise(streams_of[3], (D,), 0.3, 1.5, (), jnp.float32)
    reduce_weight = noise(streams_of[4], (3, D, D), (3 * D) ** -0.5, 0.15625)
    reduce_bias = noise(streams_of[5], (D,), 0.3, 1.5, (), jnp.float32)
    first_gain = jnp.clip(1.0 + 0.1 * jax.random.normal(streams_of[6], (D,), jnp.float32), 0.5, 1.5)
    first_shift = noise(streams_of[7], (D,), 0.3, 1.5, (), jnp.float32)
    query_weight = noise(streams_of[8], (D, D), D ** -0.5, 0.25)
    query_bias = noise(streams_of[9], (D,), 0.3, 1.5, (), jnp.float32)
    key_weight = noise(streams_of[10], (D, D), D ** -0.5, 0.25)
    value_weight = noise(streams_of[11], (D, D), D ** -0.5, 0.25)
    value_bias = noise(streams_of[12], (D,), 0.3, 1.5, (), jnp.float32)
    output_weight = noise(streams_of[13], (D, D), 2 ** -0.5, 4.0)
    output_bias = noise(streams_of[14], (D,), 0.3, 1.5, (), jnp.float32)
    second_gain = jnp.clip(1.0 + 0.1 * jax.random.normal(streams_of[15], (D,), jnp.float32), 0.5, 1.5)
    second_shift = noise(streams_of[16], (D,), 0.3, 1.5, (), jnp.float32)
    hidden_weight = noise(streams_of[17], (D, FF), D ** -0.5, 0.25)
    hidden_bias = noise(streams_of[18], (FF,), 0.3, 1.5, (), jnp.float32)
    return_weight = noise(streams_of[19], (FF, D), FF ** -0.5, 0.125)
    return_bias = noise(streams_of[20], (D,), 0.3, 1.5, (), jnp.float32)
    cotangent = noise(streams_of[21], (WINDOWS, WIN_TOK, D), 1.0, 6.0, ((0, 8), (1, 4)))
    return dict(mel_frames=mel_frames, window_count=window_count, stem_weight=stem_weight, stem_bias=stem_bias, reduce_weight=reduce_weight, reduce_bias=reduce_bias, first_gain=first_gain, first_shift=first_shift, query_weight=query_weight, query_bias=query_bias, key_weight=key_weight, value_weight=value_weight, value_bias=value_bias, output_weight=output_weight, output_bias=output_bias, second_gain=second_gain, second_shift=second_shift, hidden_weight=hidden_weight, hidden_bias=hidden_bias, return_weight=return_weight, return_bias=return_bias, cotangent=cotangent)


epsilon = 1e-05
highest = lax.Precision.HIGHEST

@jax.custom_vjp
def low(v):
    return lax.optimization_barrier(v.astype(jnp.bfloat16)).astype(jnp.float32)

@jax.custom_vjp
def low_back(v):
    return v

def low_keep(v):
    return (low(v), None)

def low_pass(kept, grad):
    return (grad,)

def back_keep(v):
    return (v, None)

def back_low(kept, grad):
    return (low(grad),)
low.defvjp(low_keep, low_pass)
low_back.defvjp(back_keep, back_low)

def matmul(left, right):
    return jnp.dot(left, right, precision=highest, preferred_element_type=jnp.float32)

def gelu_exact(argument):
    return jax.nn.gelu(argument, approximate=False)

def layer_norm(argument, norm_gain, norm_shift):
    centred = argument - lax.optimization_barrier(jnp.mean(argument, axis=-1, keepdims=True))
    variance = lax.optimization_barrier(jnp.mean(centred * centred, axis=-1, keepdims=True))
    return centred * lax.rsqrt(variance + epsilon) * norm_gain + norm_shift

def sinusoid(start_token, length, model_width):
    halfway = model_width // 2
    increment = math.log(10000.0) / (halfway - 1)
    inverse = jnp.exp(-increment * jnp.arange(halfway, dtype=jnp.float32))
    places = (start_token + jnp.arange(length, dtype=jnp.int32)).astype(jnp.float32)
    angles = places[:, None] * inverse[None, :]
    return jnp.concatenate([jnp.sin(angles), jnp.cos(angles)], axis=1)

def softmax_rows(scores):
    shifted = scores - lax.optimization_barrier(jnp.max(scores, axis=-1, keepdims=True))
    exponent = jnp.exp(shifted)
    return exponent / lax.optimization_barrier(jnp.sum(exponent, axis=-1, keepdims=True))

def forward(mel_window, params):
    stem_weight, stem_bias, reduce_weight, reduce_bias, first_gain, first_shift, query_weight, query_bias, key_weight, value_weight, value_bias, output_weight, output_bias, second_gain, second_shift, hidden_weight, hidden_bias, return_weight, return_bias = params
    padded = jnp.pad(mel_window, ((1, 1), (0, 0)))
    stem_columns = jnp.concatenate([padded[0:WIN_FR], padded[1:WIN_FR + 1], padded[2:WIN_FR + 2]], axis=1)
    stem_linear = low_back(matmul(stem_columns, stem_weight.reshape(3 * MELS, D)) + stem_bias)
    stem_active = low(gelu_exact(stem_linear))
    padded_active = jnp.pad(stem_active, ((1, 1), (0, 0)))
    conv_columns = jnp.concatenate([padded_active[0:WIN_FR:2], padded_active[1:WIN_FR + 1:2], padded_active[2:WIN_FR + 2:2]], axis=1)
    conv_linear = low_back(matmul(conv_columns, reduce_weight.reshape(3 * D, D)) + reduce_bias)
    stream = gelu_exact(conv_linear) + sinusoid(0, WIN_TOK, D)
    first_normed = low(layer_norm(stream, first_gain, first_shift))
    query_heads = low_back(low(matmul(first_normed, query_weight) + query_bias)).reshape(WIN_TOK, HEADS, HEAD_DIM)
    key_heads = low_back(low(matmul(first_normed, key_weight))).reshape(WIN_TOK, HEADS, HEAD_DIM)
    value_heads = low_back(low(matmul(first_normed, value_weight) + value_bias)).reshape(WIN_TOK, HEADS, HEAD_DIM)
    score_scale = HEAD_DIM ** (-0.5)
    scores = low_back(jnp.einsum('qhd,khd->hqk', query_heads, key_heads, precision=highest) * score_scale)
    attention_weights = low(softmax_rows(scores))
    attended = jnp.einsum('hqk,khd->qhd', attention_weights, value_heads, precision=highest).reshape(WIN_TOK, D)
    attended = low_back(low(attended))
    attention_branch = low_back(matmul(attended, output_weight) + output_bias)
    mixed = stream + attention_branch
    second_normed = low(layer_norm(mixed, second_gain, second_shift))
    hidden_linear = low_back(matmul(second_normed, hidden_weight) + hidden_bias)
    hidden_active = low(gelu_exact(hidden_linear))
    feed_branch = low_back(matmul(hidden_active, return_weight) + return_bias)
    return mixed + feed_branch

def reference(mel_frames, window_count, stem_weight, stem_bias, reduce_weight, reduce_bias, first_gain, first_shift, query_weight, query_bias, key_weight, value_weight, value_bias, output_weight, output_bias, second_gain, second_shift, hidden_weight, hidden_bias, return_weight, return_bias, cotangent):
    params = (stem_weight.astype(jnp.float32), stem_bias.astype(jnp.float32), reduce_weight.astype(jnp.float32), reduce_bias.astype(jnp.float32), first_gain.astype(jnp.float32), first_shift.astype(jnp.float32), query_weight.astype(jnp.float32), query_bias.astype(jnp.float32), key_weight.astype(jnp.float32), value_weight.astype(jnp.float32), value_bias.astype(jnp.float32), output_weight.astype(jnp.float32), output_bias.astype(jnp.float32), second_gain.astype(jnp.float32), second_shift.astype(jnp.float32), hidden_weight.astype(jnp.float32), hidden_bias.astype(jnp.float32), return_weight.astype(jnp.float32), return_bias.astype(jnp.float32))
    slot_numbers = jnp.arange(MAXW, dtype=jnp.int32)
    alive_mask = (slot_numbers[None, :] < window_count[:, None]).reshape(WINDOWS).astype(jnp.float32)

    def window_step(running, window_items):
        mel_window, cotangent_window, alive = window_items
        layer_window, pullback = jax.vjp(forward, mel_window.astype(jnp.float32), params)
        mel_window_grad, param_grads = pullback(cotangent_window.astype(jnp.float32))
        running = tuple((earlier + alive * fresh for earlier, fresh in zip(running, param_grads)))
        return (running, ((layer_window * alive).astype(jnp.bfloat16), mel_window_grad * alive))
    starting = tuple((jnp.zeros_like(entry) for entry in params))
    totals, (layer_output, mel_gradient) = lax.scan(window_step, starting, (mel_frames, cotangent, alive_mask))
    return (layer_output, mel_gradient, totals[0], totals[1], totals[2], totals[3], totals[4], totals[5], totals[6], totals[7], totals[8], totals[9], totals[10], totals[11], totals[12], totals[13], totals[14], totals[15], totals[16], totals[17], totals[18])
```

```python
import math

import jax
import jax.numpy as jnp
from jax import lax
from jax.sharding import PartitionSpec as P

HEADS = 8
EPS = 1e-05
F32 = jnp.float32
BF16 = jnp.bfloat16
PHI_SLOPE = 0.28
PHI_POLY = (
    0.1167294156016242,
    0.06622785593379492,
    0.27197610469464767,
    -0.24067367858721922,
    0.3920693507793772,
    -0.10632905941542621,
)


def phi_parts(v):
    size = jnp.abs(v)
    t = 1.0 / (1.0 + PHI_SLOPE * size)
    bell = jnp.exp(-0.5 * v * v)
    poly = PHI_POLY[5]
    for c in PHI_POLY[4::-1]:
        poly = poly * t + c
    tail = poly * t * bell
    cdf = jnp.where(v >= 0, 1.0 - tail, tail)
    return cdf, bell * (1.0 / math.sqrt(2.0 * math.pi))


def gelu(v):
    cdf, _ = phi_parts(v)
    return v * cdf


def gelu_slope(v):
    cdf, pdf = phi_parts(v)
    return cdf + v * pdf


def dot(left, right):
    return jnp.dot(left, right, preferred_element_type=F32)


def dot_t(left, right):
    return lax.dot_general(left, right, (((1,), (1,)), ((), ())), preferred_element_type=F32)


def outer(left, right):
    return lax.dot_general(left, right, (((0,), (0,)), ((), ())), preferred_element_type=F32)


def column_total(x):
    return jnp.sum(x.astype(F32), axis=0)


def norm_parts(x):
    centred = x - jnp.mean(x, axis=-1, keepdims=True)
    r = lax.rsqrt(jnp.mean(centred * centred, axis=-1, keepdims=True) + EPS)
    return centred * r, r


def norm_pull(xhat, r, gain, dy):
    dh = dy * gain
    inner = r * (
        dh
        - jnp.mean(dh, axis=-1, keepdims=True)
        - xhat * jnp.mean(dh * xhat, axis=-1, keepdims=True)
    )
    return inner, column_total(dy * xhat), column_total(dy)


def positions_of(first, count, width):
    half = width // 2
    step = math.log(10000.0) / (half - 1)
    rate = jnp.exp(-step * jnp.arange(half, dtype=F32))[None, :]
    fine = math.gcd(count, 16)
    coarse = count // fine
    a = (first + fine * jnp.arange(coarse, dtype=jnp.int32)).astype(F32)[:, None] * rate
    b = jnp.arange(fine, dtype=jnp.int32).astype(F32)[:, None] * rate
    sa, ca = jnp.sin(a)[:, None, :], jnp.cos(a)[:, None, :]
    sb, cb = jnp.sin(b)[None, :, :], jnp.cos(b)[None, :, :]
    both = jnp.concatenate([sa * cb + ca * sb, ca * cb - sa * sb], axis=2)
    return both.reshape(count, width)


def on_device(
    mel_frames,
    window_count,
    stem_weight,
    stem_bias,
    reduce_weight,
    reduce_bias,
    first_gain,
    first_shift,
    query_weight,
    query_bias,
    key_weight,
    value_weight,
    value_bias,
    output_weight,
    output_bias,
    second_gain,
    second_shift,
    hidden_weight,
    hidden_bias,
    return_weight,
    return_bias,
    cotangent,
):
    S, piece_frames, mels = mel_frames.shape
    piece = cotangent.shape[1]
    D = stem_weight.shape[2]
    hd = D // HEADS
    scale = hd ** (-0.5)
    F = lax.axis_size("frame")
    G = F // S
    T = S * piece
    R = -(-(T + 2) // 128) * 128
    f = lax.axis_index("frame")
    s = f // G
    r = f % G
    alive = s < window_count[0]

    def gather_window(x):
        parts = []
        out = jnp.zeros((S * x.shape[1], x.shape[2]), x.dtype)
        for t in range(S):
            part = lax.dynamic_index_in_dim(x, (f + t) % S, 0, keepdims=False)
            perm = [(p, ((p % S + t) % S) * G + p // S) for p in range(F)]
            got = lax.ppermute(part, "frame", perm)
            j = (s - t) % S
            out = lax.dynamic_update_slice(out, got, (j * x.shape[1], 0))
        return out

    def scatter_window(x):
        n = x.shape[0] // S
        out = jnp.zeros((S, n, x.shape[1]), x.dtype)
        for t in range(S):
            j = (s - t) % S
            part = lax.dynamic_slice(x, (j * n, 0), (n, x.shape[1]))
            perm = [(((p % S + t) % S) * G + p // S, p) for p in range(F)]
            got = lax.ppermute(part, "frame", perm)
            out = lax.dynamic_update_slice(out, got[None], ((f + t) % S, 0, 0))
        return out

    down = [(i, i + 1) for i in range(F) if (i + 1) % G != 0]
    up = [(i + 1, i) for i in range(F) if (i + 1) % G != 0]

    def with_halo(x):
        before = lax.ppermute(x[T - 1 : T], "frame", down)
        after = lax.ppermute(x[0:1], "frame", up)
        gap = jnp.zeros((R - T - 2, x.shape[1]), x.dtype)
        return jnp.concatenate([x, after, gap, before], axis=0)

    mel = gather_window(mel_frames.reshape(S, piece, 2 * mels))
    cot = gather_window(cotangent)
    cot = jnp.where(alive, cot, jnp.zeros_like(cot))
    mel = with_halo(mel)
    odd_before = jnp.roll(mel[:, mels:], 1, axis=0)
    even_after = jnp.roll(mel[:, :mels], -1, axis=0)
    columns = jnp.concatenate([odd_before, mel, even_after], axis=1)
    stem_matrix = stem_weight.reshape(3 * mels, D)
    gap = jnp.zeros((mels, D), BF16)
    stem_pair = jnp.concatenate(
        [
            jnp.concatenate([stem_matrix, gap], axis=0),
            jnp.concatenate([gap, stem_matrix], axis=0),
        ],
        axis=1,
    )
    stem_bias2 = jnp.concatenate([stem_bias, stem_bias])
    stem_linear = dot(columns, stem_pair) + stem_bias2
    row = lax.broadcasted_iota(jnp.int32, (R, 1), 0)
    valid = (row < T) | ((row == T) & (r < G - 1)) | ((row == R - 1) & (r > 0))
    stem_active = jnp.where(valid, gelu(stem_linear), 0.0).astype(BF16)

    odd_active_before = jnp.roll(stem_active[:, D:], 1, axis=0)[:T]
    conv_columns = jnp.concatenate([odd_active_before, stem_active[:T]], axis=1)
    reduce_matrix = reduce_weight.reshape(3 * D, D)
    conv_linear = dot(conv_columns, reduce_matrix) + reduce_bias
    stream = gelu(conv_linear) + positions_of(r * T, T, D)
    xhat1, r1 = norm_parts(stream)
    first_normed = (xhat1 * first_gain + first_shift).astype(BF16)
    query = (dot(first_normed, query_weight) + query_bias).astype(BF16)
    key = dot(first_normed, key_weight).astype(BF16)
    value = (dot(first_normed, value_weight) + value_bias).astype(BF16)
    keyval = jnp.concatenate([key, value], axis=1)
    others = []
    for t in range(1, G):
        perm = [(i, (i // G) * G + (i % G + t) % G) for i in range(F)]
        others.append(lax.ppermute(keyval, "frame", perm))
    whole = jnp.concatenate([keyval] + others, axis=0)
    tokens = whole.shape[0]
    kh = whole[:, :D].reshape(tokens, HEADS, hd)
    vh = whole[:, D:].reshape(tokens, HEADS, hd)
    qh = query.reshape(T, HEADS, hd)
    scores = jnp.einsum("qhd,khd->hqk", qh, kh, preferred_element_type=F32) * scale
    exponent = jnp.exp(scores - jnp.max(scores, axis=-1, keepdims=True))
    probs = exponent / jnp.sum(exponent, axis=-1, keepdims=True)
    weights = probs.astype(BF16)
    attended = jnp.einsum("hqk,khd->qhd", weights, vh, preferred_element_type=F32)
    attended = attended.reshape(T, D).astype(BF16)
    mixed = stream + dot(attended, output_weight) + output_bias
    xhat2, r2 = norm_parts(mixed)
    second_normed = (xhat2 * second_gain + second_shift).astype(BF16)
    hidden_linear = dot(second_normed, hidden_weight) + hidden_bias
    hidden_cdf, hidden_pdf = phi_parts(hidden_linear)
    hidden_active = (hidden_linear * hidden_cdf).astype(BF16)
    layer = mixed + dot(hidden_active, return_weight) + return_bias
    layer = jnp.where(alive, layer, 0.0).astype(BF16)
    layer_output = scatter_window(layer)

    return_bias_grad = column_total(cot)
    return_weight_grad = outer(hidden_active, cot)
    slope = hidden_cdf + hidden_linear * hidden_pdf
    hidden_grad = (slope * dot_t(cot, return_weight)).astype(BF16)
    hidden_bias_grad = column_total(hidden_grad)
    hidden_weight_grad = outer(second_normed, hidden_grad)
    inner, second_gain_grad, second_shift_grad = norm_pull(
        xhat2, r2, second_gain, dot_t(hidden_grad, hidden_weight)
    )
    mixed_grad = cot.astype(F32) + inner
    branch_grad = mixed_grad.astype(BF16)
    output_bias_grad = column_total(branch_grad)
    output_weight_grad = outer(attended, branch_grad)

    early = lax.psum(
        (
            return_weight_grad.astype(BF16),
            hidden_weight_grad.astype(BF16),
            output_weight_grad.astype(BF16),
        ),
        ("dp", "frame"),
    )

    attended_grad = dot_t(branch_grad, output_weight).astype(BF16).reshape(T, HEADS, hd)
    weight_grad = jnp.einsum("qhd,khd->hqk", attended_grad, vh, preferred_element_type=F32)
    delta = jnp.sum(weight_grad * probs, axis=-1, keepdims=True)
    score_grad = (probs * (weight_grad - delta)).astype(BF16)
    query_grad = jnp.einsum("hqk,khd->qhd", score_grad, kh, preferred_element_type=F32) * scale
    query_grad = query_grad.astype(BF16).reshape(T, D)
    key_term = jnp.einsum("hqk,qhd->khd", score_grad, qh, preferred_element_type=F32) * scale
    value_term = jnp.einsum("hqk,qhd->khd", weights, attended_grad, preferred_element_type=F32)
    terms = jnp.concatenate([key_term.reshape(tokens, D), value_term.reshape(tokens, D)], axis=1)
    total = terms[:T]
    for t in range(1, G):
        perm = [((i // G) * G + (i % G + t) % G, i) for i in range(F)]
        back = lax.ppermute(terms[t * T : (t + 1) * T], "frame", perm)
        total = total + back
    key_grad = total[:, :D].astype(BF16)
    value_grad = total[:, D:].astype(BF16)
    query_weight_grad = outer(first_normed, query_grad)
    key_weight_grad = outer(first_normed, key_grad)
    value_weight_grad = outer(first_normed, value_grad)
    query_bias_grad = column_total(query_grad)
    value_bias_grad = column_total(value_grad)
    normed_grad = (
        dot_t(query_grad, query_weight)
        + dot_t(key_grad, key_weight)
        + dot_t(value_grad, value_weight)
    )
    inner, first_gain_grad, first_shift_grad = norm_pull(xhat1, r1, first_gain, normed_grad)
    stream_grad = mixed_grad + inner
    conv_grad = (gelu_slope(conv_linear) * stream_grad).astype(BF16)
    reduce_bias_grad = column_total(conv_grad)
    reduce_matrix_grad = outer(conv_columns, conv_grad)
    conv_ext = with_halo(conv_grad)
    conv_after = jnp.roll(conv_ext, -1, axis=0)
    pair_grad = dot_t(conv_ext, reduce_matrix[D:])
    third_grad = dot_t(conv_after, reduce_matrix[:D])
    active_grad = pair_grad + jnp.concatenate([jnp.zeros_like(third_grad), third_grad], axis=1)
    stem_grad = jnp.where(valid, gelu_slope(stem_linear) * active_grad, 0.0).astype(BF16)
    own = stem_grad[:T]
    totals = column_total(own)
    stem_bias_grad = totals[:D] + totals[D:]
    pair_matrix_grad = outer(columns[:T], own)
    stem_matrix_grad = pair_matrix_grad[: 3 * mels, :D] + pair_matrix_grad[mels:, D:]
    mel_columns = dot_t(stem_grad, stem_pair)
    mel_pair = (
        mel_columns[:, mels : 3 * mels]
        + jnp.concatenate(
            [
                jnp.roll(mel_columns[:, 3 * mels :], 1, axis=0),
                jnp.roll(mel_columns[:, :mels], -1, axis=0),
            ],
            axis=1,
        )
    )[:T]
    mel_gradient = scatter_window(mel_pair).reshape(S, piece_frames, mels)

    late = lax.psum(
        (
            reduce_matrix_grad.astype(BF16),
            query_weight_grad.astype(BF16),
            key_weight_grad.astype(BF16),
            value_weight_grad.astype(BF16),
            stem_matrix_grad.astype(BF16),
        ),
        ("dp", "frame"),
    )
    small = [
        stem_bias_grad,
        reduce_bias_grad,
        first_gain_grad,
        first_shift_grad,
        query_bias_grad,
        value_bias_grad,
        output_bias_grad,
        second_gain_grad,
        second_shift_grad,
        hidden_bias_grad,
        return_bias_grad,
    ]
    sizes = [v.shape[0] for v in small]
    packed = lax.psum(jnp.concatenate(small).reshape(-1, 128), ("dp", "frame")).reshape(-1)
    small = []
    at = 0
    for n in sizes:
        small.append(packed[at : at + n])
        at += n
    return_w, hidden_w, output_w = [x.astype(F32) for x in early]
    reduce_w, query_w, key_w, value_w, stem_w = [x.astype(F32) for x in late]
    return (
        layer_output,
        mel_gradient,
        stem_w.reshape(3, mels, D),
        small[0],
        reduce_w.reshape(3, D, D),
        small[1],
        small[2],
        small[3],
        query_w,
        small[4],
        key_w,
        value_w,
        small[5],
        output_w,
        small[6],
        small[7],
        small[8],
        hidden_w,
        small[9],
        return_w,
        small[10],
    )


def solution(mesh):
    cut = P("dp", "frame", None)
    return jax.shard_map(
        on_device,
        mesh=mesh,
        in_specs=(cut, P("dp")) + (P(),) * 19 + (cut,),
        out_specs=(cut, cut) + (P(),) * 19,
        check_vma=False,
    )
```

```python
import functools
import math

import jax
import jax.numpy as jnp
from jax import lax
from jax.experimental import pallas as pl
from jax.experimental.pallas import tpu as pltpu
from jax.sharding import PartitionSpec as P

HEADS = 8
EPS = 1e-05
F32 = jnp.float32
BF16 = jnp.bfloat16
PHI_SLOPE = 0.28
PHI_POLY = (
    0.1167294156016242,
    0.06622785593379492,
    0.27197610469464767,
    -0.24067367858721922,
    0.3920693507793772,
    -0.10632905941542621,
)


def phi_parts(v):
    size = jnp.abs(v)
    t = 1.0 / (1.0 + PHI_SLOPE * size)
    bell = jnp.exp(-0.5 * v * v)
    poly = PHI_POLY[5]
    for c in PHI_POLY[4::-1]:
        poly = poly * t + c
    tail = poly * t * bell
    cdf = jnp.where(v >= 0, 1.0 - tail, tail)
    return cdf, bell * (1.0 / math.sqrt(2.0 * math.pi))


def gelu(v):
    cdf, _ = phi_parts(v)
    return v * cdf


def gelu_slope(v):
    cdf, pdf = phi_parts(v)
    return cdf + v * pdf


def dot(left, right):
    return jnp.dot(left, right, preferred_element_type=F32)


def dot_t(left, right):
    return lax.dot_general(left, right, (((1,), (1,)), ((), ())), preferred_element_type=F32)


def outer(left, right):
    return lax.dot_general(left, right, (((0,), (0,)), ((), ())), preferred_element_type=F32)


def column_total(x):
    return jnp.sum(x.astype(F32), axis=0)


def norm_parts(x):
    centred = x - jnp.mean(x, axis=-1, keepdims=True)
    r = lax.rsqrt(jnp.mean(centred * centred, axis=-1, keepdims=True) + EPS)
    return centred * r, r


def norm_pull(xhat, r, gain, dy):
    dh = dy * gain
    inner = r * (
        dh
        - jnp.mean(dh, axis=-1, keepdims=True)
        - xhat * jnp.mean(dh * xhat, axis=-1, keepdims=True)
    )
    return inner, column_total(dy * xhat), column_total(dy)


def positions_of(first, count, width):
    half = width // 2
    step = math.log(10000.0) / (half - 1)
    rate = jnp.exp(-step * jnp.arange(half, dtype=F32))[None, :]
    fine = math.gcd(count, 16)
    coarse = count // fine
    a = (first + fine * jnp.arange(coarse, dtype=jnp.int32)).astype(F32)[:, None] * rate
    b = jnp.arange(fine, dtype=jnp.int32).astype(F32)[:, None] * rate
    sa, ca = jnp.sin(a)[:, None, :], jnp.cos(a)[:, None, :]
    sb, cb = jnp.sin(b)[None, :, :], jnp.cos(b)[None, :, :]
    both = jnp.concatenate([sa * cb + ca * sb, ca * cb - sa * sb], axis=2)
    return both.reshape(count, width)


def half_mask(shape, h, hd):
    lane = lax.broadcasted_iota(jnp.int32, shape, 1)
    return (lane >= h*hd) & (lane < (h+1)*hd)

def fwd_kernel(scale, hd, q_ref, k_ref, v_ref, p_ref, o_ref, s_ref):
    per = 128//hd
    k = k_ref[...]
    vt = v_ref[...].T
    outs=[]
    for h in range(per):
        q = q_ref[...]
        q = jnp.where(half_mask(q.shape,h,hd), q, jnp.zeros_like(q))
        s_ref[h] = lax.dot_general(k, q, (((1,),(1,)),((),())), preferred_element_type=F32)
    for h in range(per):
        s = s_ref[h]
        m = jnp.max(s, axis=0, keepdims=True)
        e = jnp.exp((s - m)*scale)
        l = jnp.sum(e, axis=0, keepdims=True)
        p = (e * (1.0/l)).astype(BF16)
        p_ref[h] = p
        outs.append(jnp.dot(vt[h*hd:(h+1)*hd], p, preferred_element_type=F32))
    o_ref[...] = jnp.concatenate(outs, axis=0).T

def attn_fwd(q, k, v, scale, heads, QB):
    R, D = q.shape; N = k.shape[0]; hd = D//heads; per=128//hd; pairs=D//128
    return pl.pallas_call(
        functools.partial(fwd_kernel, scale, hd),
        grid=(pairs, R//QB),
        in_specs=[pl.BlockSpec((QB,128),lambda p,i:(i,p)),
                  pl.BlockSpec((N,128),lambda p,i:(0,p)),
                  pl.BlockSpec((N,128),lambda p,i:(0,p))],
        out_specs=[pl.BlockSpec((per,N,QB),lambda p,i:(p,0,i)),
                   pl.BlockSpec((QB,128),lambda p,i:(i,p))],
        out_shape=[jax.ShapeDtypeStruct((heads,N,R),BF16), jax.ShapeDtypeStruct((R,D),F32)],
        scratch_shapes=[pltpu.VMEM((per,N,QB),F32)],
        compiler_params=pltpu.CompilerParams(vmem_limit_bytes=60<<20),
    )(q,k,v)

def bwd_kernel(scale, hd, q_ref, do_ref, o_ref, k_ref, v_ref, p_ref, dq_ref, dk_ref, dv_ref, dp_ref, kt_ref):
    per = 128//hd
    i = pl.program_id(1)
    @pl.when(i==0)
    def _():
        kt_ref[...] = k_ref[...].T
        dk_ref[...] = jnp.zeros_like(dk_ref)
        dv_ref[...] = jnp.zeros_like(dv_ref)
    do = do_ref[...]
    q = q_ref[...]
    v = v_ref[...]
    prod = (do.astype(F32)*o_ref[...]).T
    for h in range(per):
        doh = jnp.where(half_mask(do.shape,h,hd), do, jnp.zeros_like(do))
        dp_ref[h] = lax.dot_general(v, doh, (((1,),(1,)),((),())), preferred_element_type=F32)
    dqs=[]
    for h in range(per):
        doh = jnp.where(half_mask(do.shape,h,hd), do, jnp.zeros_like(do))
        qh = jnp.where(half_mask(q.shape,h,hd), q, jnp.zeros_like(q))
        delta = jnp.sum(prod[h*hd:(h+1)*hd], axis=0, keepdims=True)
        p = p_ref[h]
        ds = (p.astype(F32)*(dp_ref[h]-delta)).astype(BF16)
        dv_ref[...] += jnp.dot(p, doh, preferred_element_type=F32)
        dk_ref[...] += jnp.dot(ds, qh, preferred_element_type=F32)
        dqs.append(jnp.dot(kt_ref[h*hd:(h+1)*hd], ds, preferred_element_type=F32))
    dq_ref[...] = (jnp.concatenate(dqs,axis=0)*scale).T.astype(BF16)
    @pl.when(i==pl.num_programs(1)-1)
    def _():
        dk_ref[...] = dk_ref[...]*scale

def attn_bwd(q, do, o, k, v, p, scale, heads, QB):
    R, D = q.shape; N = k.shape[0]; hd = D//heads; per=128//hd; pairs=D//128
    row = pl.BlockSpec((QB,128),lambda p,i:(i,p))
    key = pl.BlockSpec((N,128),lambda p,i:(0,p))
    return pl.pallas_call(
        functools.partial(bwd_kernel, scale, hd),
        grid=(pairs, R//QB),
        in_specs=[row,row,row,key,key,pl.BlockSpec((per,N,QB),lambda p,i:(p,0,i))],
        out_specs=[row,key,key],
        out_shape=[jax.ShapeDtypeStruct((R,D),BF16), jax.ShapeDtypeStruct((N,D),F32), jax.ShapeDtypeStruct((N,D),F32)],
        scratch_shapes=[pltpu.VMEM((per,N,QB),F32), pltpu.VMEM((128,N),BF16)],
        compiler_params=pltpu.CompilerParams(vmem_limit_bytes=60<<20),
    )(q,do,o,k,v,p)


def on_device(
    mel_frames,
    window_count,
    stem_weight,
    stem_bias,
    reduce_weight,
    reduce_bias,
    first_gain,
    first_shift,
    query_weight,
    query_bias,
    key_weight,
    value_weight,
    value_bias,
    output_weight,
    output_bias,
    second_gain,
    second_shift,
    hidden_weight,
    hidden_bias,
    return_weight,
    return_bias,
    cotangent,
):
    S, piece_frames, mels = mel_frames.shape
    piece = cotangent.shape[1]
    D = stem_weight.shape[2]
    hd = D // HEADS
    scale = hd ** (-0.5)
    F = lax.axis_size("frame")
    G = F // S
    T = S * piece
    R = -(-(T + 2) // 128) * 128
    f = lax.axis_index("frame")
    s = f // G
    r = f % G
    alive = s < window_count[0]

    def gather_window(x):
        parts = []
        out = jnp.zeros((S * x.shape[1], x.shape[2]), x.dtype)
        for t in range(S):
            part = lax.dynamic_index_in_dim(x, (f + t) % S, 0, keepdims=False)
            perm = [(p, ((p % S + t) % S) * G + p // S) for p in range(F)]
            got = lax.ppermute(part, "frame", perm)
            j = (s - t) % S
            out = lax.dynamic_update_slice(out, got, (j * x.shape[1], 0))
        return out

    def scatter_window(x):
        n = x.shape[0] // S
        out = jnp.zeros((S, n, x.shape[1]), x.dtype)
        for t in range(S):
            j = (s - t) % S
            part = lax.dynamic_slice(x, (j * n, 0), (n, x.shape[1]))
            perm = [(((p % S + t) % S) * G + p // S, p) for p in range(F)]
            got = lax.ppermute(part, "frame", perm)
            out = lax.dynamic_update_slice(out, got[None], ((f + t) % S, 0, 0))
        return out

    down = [(i, i + 1) for i in range(F) if (i + 1) % G != 0]
    up = [(i + 1, i) for i in range(F) if (i + 1) % G != 0]

    def with_halo(x):
        before = lax.ppermute(x[T - 1 : T], "frame", down)
        after = lax.ppermute(x[0:1], "frame", up)
        gap = jnp.zeros((R - T - 2, x.shape[1]), x.dtype)
        return jnp.concatenate([x, after, gap, before], axis=0)

    mel = gather_window(mel_frames.reshape(S, piece, 2 * mels))
    cot = gather_window(cotangent)
    cot = jnp.where(alive, cot, jnp.zeros_like(cot))
    mel = with_halo(mel)
    odd_before = jnp.roll(mel[:, mels:], 1, axis=0)
    even_after = jnp.roll(mel[:, :mels], -1, axis=0)
    columns = jnp.concatenate([odd_before, mel, even_after], axis=1)
    stem_matrix = stem_weight.reshape(3 * mels, D)
    gap = jnp.zeros((mels, D), BF16)
    stem_pair = jnp.concatenate(
        [
            jnp.concatenate([stem_matrix, gap], axis=0),
            jnp.concatenate([gap, stem_matrix], axis=0),
        ],
        axis=1,
    )
    stem_bias2 = jnp.concatenate([stem_bias, stem_bias])
    stem_linear = dot(columns, stem_pair) + stem_bias2
    row = lax.broadcasted_iota(jnp.int32, (R, 1), 0)
    valid = (row < T) | ((row == T) & (r < G - 1)) | ((row == R - 1) & (r > 0))
    stem_active = jnp.where(valid, gelu(stem_linear), 0.0).astype(BF16)

    odd_active_before = jnp.roll(stem_active[:, D:], 1, axis=0)[:T]
    conv_columns = jnp.concatenate([odd_active_before, stem_active[:T]], axis=1)
    reduce_matrix = reduce_weight.reshape(3 * D, D)
    conv_linear = dot(conv_columns, reduce_matrix) + reduce_bias
    stream = gelu(conv_linear) + positions_of(r * T, T, D)
    xhat1, r1 = norm_parts(stream)
    first_normed = (xhat1 * first_gain + first_shift).astype(BF16)
    query = (dot(first_normed, query_weight) + query_bias).astype(BF16)
    key = dot(first_normed, key_weight).astype(BF16)
    value = (dot(first_normed, value_weight) + value_bias).astype(BF16)
    keyval = jnp.concatenate([key, value], axis=1)
    others = []
    for t in range(1, G):
        perm = [(i, (i // G) * G + (i % G + t) % G) for i in range(F)]
        others.append(lax.ppermute(keyval, "frame", perm))
    whole = jnp.concatenate([keyval] + others, axis=0)
    tokens = whole.shape[0]
    key_all, value_all = whole[:, :D], whole[:, D:]
    query_ext = jnp.pad(query, ((0, R - T), (0, 0)))
    block = 256 if R % 256 == 0 else 128
    probs, attended_wide = attn_fwd(query_ext, key_all, value_all, scale, HEADS, block)
    attended = attended_wide[:T].astype(BF16)
    mixed = stream + dot(attended, output_weight) + output_bias
    xhat2, r2 = norm_parts(mixed)
    second_normed = (xhat2 * second_gain + second_shift).astype(BF16)
    hidden_linear = dot(second_normed, hidden_weight) + hidden_bias
    hidden_cdf, hidden_pdf = phi_parts(hidden_linear)
    hidden_active = (hidden_linear * hidden_cdf).astype(BF16)
    layer = mixed + dot(hidden_active, return_weight) + return_bias
    layer = jnp.where(alive, layer, 0.0).astype(BF16)
    layer_output = scatter_window(layer)

    return_bias_grad = column_total(cot)
    return_weight_grad = outer(hidden_active, cot)
    slope = hidden_cdf + hidden_linear * hidden_pdf
    hidden_grad = (slope * dot_t(cot, return_weight)).astype(BF16)
    hidden_bias_grad = column_total(hidden_grad)
    hidden_weight_grad = outer(second_normed, hidden_grad)
    inner, second_gain_grad, second_shift_grad = norm_pull(
        xhat2, r2, second_gain, dot_t(hidden_grad, hidden_weight)
    )
    mixed_grad = cot.astype(F32) + inner
    branch_grad = mixed_grad.astype(BF16)
    output_bias_grad = column_total(branch_grad)
    output_weight_grad = outer(attended, branch_grad)

    early = lax.psum(
        (
            return_weight_grad.astype(BF16),
            hidden_weight_grad.astype(BF16),
            output_weight_grad.astype(BF16),
        ),
        ("dp", "frame"),
    )

    attended_grad = jnp.pad(dot_t(branch_grad, output_weight).astype(BF16), ((0, R - T), (0, 0)))
    query_grad, key_term, value_term = attn_bwd(
        query_ext, attended_grad, attended_wide, key_all, value_all, probs, scale, HEADS, block
    )
    query_grad = query_grad[:T]
    terms = jnp.concatenate([key_term, value_term], axis=1)
    total = terms[:T]
    for t in range(1, G):
        perm = [((i // G) * G + (i % G + t) % G, i) for i in range(F)]
        back = lax.ppermute(terms[t * T : (t + 1) * T], "frame", perm)
        total = total + back
    key_grad = total[:, :D].astype(BF16)
    value_grad = total[:, D:].astype(BF16)
    query_weight_grad = outer(first_normed, query_grad)
    key_weight_grad = outer(first_normed, key_grad)
    value_weight_grad = outer(first_normed, value_grad)
    query_bias_grad = column_total(query_grad)
    value_bias_grad = column_total(value_grad)
    normed_grad = (
        dot_t(query_grad, query_weight)
        + dot_t(key_grad, key_weight)
        + dot_t(value_grad, value_weight)
    )
    inner, first_gain_grad, first_shift_grad = norm_pull(xhat1, r1, first_gain, normed_grad)
    stream_grad = mixed_grad + inner
    conv_grad = (gelu_slope(conv_linear) * stream_grad).astype(BF16)
    reduce_bias_grad = column_total(conv_grad)
    reduce_matrix_grad = outer(conv_columns, conv_grad)
    conv_ext = with_halo(conv_grad)
    conv_after = jnp.roll(conv_ext, -1, axis=0)
    pair_grad = dot_t(conv_ext, reduce_matrix[D:])
    third_grad = dot_t(conv_after, reduce_matrix[:D])
    active_grad = pair_grad + jnp.concatenate([jnp.zeros_like(third_grad), third_grad], axis=1)
    stem_grad = jnp.where(valid, gelu_slope(stem_linear) * active_grad, 0.0).astype(BF16)
    own = stem_grad[:T]
    totals = column_total(own)
    stem_bias_grad = totals[:D] + totals[D:]
    pair_matrix_grad = outer(columns[:T], own)
    stem_matrix_grad = pair_matrix_grad[: 3 * mels, :D] + pair_matrix_grad[mels:, D:]
    mel_columns = dot_t(stem_grad, stem_pair)
    mel_pair = (
        mel_columns[:, mels : 3 * mels]
        + jnp.concatenate(
            [
                jnp.roll(mel_columns[:, 3 * mels :], 1, axis=0),
                jnp.roll(mel_columns[:, :mels], -1, axis=0),
            ],
            axis=1,
        )
    )[:T]
    mel_gradient = scatter_window(mel_pair).reshape(S, piece_frames, mels)

    late = lax.psum(
        (
            reduce_matrix_grad.astype(BF16),
            query_weight_grad.astype(BF16),
            key_weight_grad.astype(BF16),
            value_weight_grad.astype(BF16),
            stem_matrix_grad.astype(BF16),
        ),
        ("dp", "frame"),
    )
    small = [
        stem_bias_grad,
        reduce_bias_grad,
        first_gain_grad,
        first_shift_grad,
        query_bias_grad,
        value_bias_grad,
        output_bias_grad,
        second_gain_grad,
        second_shift_grad,
        hidden_bias_grad,
        return_bias_grad,
    ]
    sizes = [v.shape[0] for v in small]
    packed = lax.psum(jnp.concatenate(small).reshape(-1, 128), ("dp", "frame")).reshape(-1)
    small = []
    at = 0
    for n in sizes:
        small.append(packed[at : at + n])
        at += n
    return_w, hidden_w, output_w = [x.astype(F32) for x in early]
    reduce_w, query_w, key_w, value_w, stem_w = [x.astype(F32) for x in late]
    return (
        layer_output,
        mel_gradient,
        stem_w.reshape(3, mels, D),
        small[0],
        reduce_w.reshape(3, D, D),
        small[1],
        small[2],
        small[3],
        query_w,
        small[4],
        key_w,
        value_w,
        small[5],
        output_w,
        small[6],
        small[7],
        small[8],
        hidden_w,
        small[9],
        return_w,
        small[10],
    )


def solution(mesh):
    cut = P("dp", "frame", None)
    return jax.shard_map(
        on_device,
        mesh=mesh,
        in_specs=(cut, P("dp")) + (P(),) * 19 + (cut,),
        out_specs=(cut, cut) + (P(),) * 19,
        check_vma=False,
    )
```

```python
import functools
import math

import jax
import jax.numpy as jnp
from jax import lax
from jax.experimental import pallas as pl
from jax.experimental.pallas import tpu as pltpu
from jax.sharding import PartitionSpec as P

HEADS = 8
EPS = 1e-05
F32 = jnp.float32
BF16 = jnp.bfloat16
PHI_SLOPE = 0.28
PHI_POLY = (
    0.1167294156016242,
    0.06622785593379492,
    0.27197610469464767,
    -0.24067367858721922,
    0.3920693507793772,
    -0.10632905941542621,
)


def phi_parts(v):
    size = jnp.abs(v)
    t = 1.0 / (1.0 + PHI_SLOPE * size)
    bell = jnp.exp(-0.5 * v * v)
    poly = PHI_POLY[5]
    for c in PHI_POLY[4::-1]:
        poly = poly * t + c
    tail = poly * t * bell
    cdf = jnp.where(v >= 0, 1.0 - tail, tail)
    return cdf, bell * (1.0 / math.sqrt(2.0 * math.pi))


def gelu(v):
    cdf, _ = phi_parts(v)
    return v * cdf


def gelu_slope(v):
    cdf, pdf = phi_parts(v)
    return cdf + v * pdf


def dot(left, right):
    return jnp.dot(left, right, preferred_element_type=F32)


def dot_t(left, right):
    return lax.dot_general(left, right, (((1,), (1,)), ((), ())), preferred_element_type=F32)


def outer(left, right):
    return lax.dot_general(left, right, (((0,), (0,)), ((), ())), preferred_element_type=F32)


def column_total(x):
    return jnp.sum(x.astype(F32), axis=0)


def norm_parts(x):
    centred = x - jnp.mean(x, axis=-1, keepdims=True)
    r = lax.rsqrt(jnp.mean(centred * centred, axis=-1, keepdims=True) + EPS)
    return centred * r, r


def norm_pull(xhat, r, gain, dy):
    dh = dy * gain
    inner = r * (
        dh
        - jnp.mean(dh, axis=-1, keepdims=True)
        - xhat * jnp.mean(dh * xhat, axis=-1, keepdims=True)
    )
    return inner, column_total(dy * xhat), column_total(dy)


def positions_of(first, count, width):
    half = width // 2
    step = math.log(10000.0) / (half - 1)
    rate = jnp.exp(-step * jnp.arange(half, dtype=F32))[None, :]
    fine = math.gcd(count, 16)
    coarse = count // fine
    a = (first + fine * jnp.arange(coarse, dtype=jnp.int32)).astype(F32)[:, None] * rate
    b = jnp.arange(fine, dtype=jnp.int32).astype(F32)[:, None] * rate
    sa, ca = jnp.sin(a)[:, None, :], jnp.cos(a)[:, None, :]
    sb, cb = jnp.sin(b)[None, :, :], jnp.cos(b)[None, :, :]
    both = jnp.concatenate([sa * cb + ca * sb, ca * cb - sa * sb], axis=2)
    return both.reshape(count, width)


def half_mask(shape, h, hd):
    lane = lax.broadcasted_iota(jnp.int32, shape, 1)
    return (lane >= h*hd) & (lane < (h+1)*hd)

def fwd_kernel(scale, hd, q_ref, k_ref, v_ref, p_ref, o_ref, s_ref):
    per = 128//hd
    k = k_ref[...]
    vt = v_ref[...].T
    outs=[]
    for h in range(per):
        q = q_ref[...]
        q = jnp.where(half_mask(q.shape,h,hd), q, jnp.zeros_like(q))
        s_ref[h] = lax.dot_general(k, q, (((1,),(1,)),((),())), preferred_element_type=F32)
    for h in range(per):
        s = s_ref[h]
        m = jnp.max(s, axis=0, keepdims=True)
        e = jnp.exp((s - m)*scale)
        l = jnp.sum(e, axis=0, keepdims=True)
        p = (e * (1.0/l)).astype(BF16)
        p_ref[h] = p
        outs.append(jnp.dot(vt[h*hd:(h+1)*hd], p, preferred_element_type=F32))
    o_ref[...] = jnp.concatenate(outs, axis=0).T

def attn_fwd(q, k, v, scale, heads, QB):
    R, D = q.shape; N = k.shape[0]; hd = D//heads; per=128//hd; pairs=D//128
    return pl.pallas_call(
        functools.partial(fwd_kernel, scale, hd),
        grid=(pairs, R//QB),
        in_specs=[pl.BlockSpec((QB,128),lambda p,i:(i,p)),
                  pl.BlockSpec((N,128),lambda p,i:(0,p)),
                  pl.BlockSpec((N,128),lambda p,i:(0,p))],
        out_specs=[pl.BlockSpec((per,N,QB),lambda p,i:(p,0,i)),
                   pl.BlockSpec((QB,128),lambda p,i:(i,p))],
        out_shape=[jax.ShapeDtypeStruct((heads,N,R),BF16), jax.ShapeDtypeStruct((R,D),F32)],
        scratch_shapes=[pltpu.VMEM((per,N,QB),F32)],
        compiler_params=pltpu.CompilerParams(vmem_limit_bytes=60<<20),
    )(q,k,v)

def bwd_kernel(scale, hd, q_ref, do_ref, o_ref, k_ref, v_ref, p_ref, dq_ref, dk_ref, dv_ref, dp_ref, kt_ref):
    per = 128//hd
    i = pl.program_id(1)
    @pl.when(i==0)
    def _():
        kt_ref[...] = k_ref[...].T
        dk_ref[...] = jnp.zeros_like(dk_ref)
        dv_ref[...] = jnp.zeros_like(dv_ref)
    do = do_ref[...]
    q = q_ref[...]
    v = v_ref[...]
    prod = (do.astype(F32)*o_ref[...]).T
    for h in range(per):
        doh = jnp.where(half_mask(do.shape,h,hd), do, jnp.zeros_like(do))
        dp_ref[h] = lax.dot_general(v, doh, (((1,),(1,)),((),())), preferred_element_type=F32)
    dqs=[]
    for h in range(per):
        doh = jnp.where(half_mask(do.shape,h,hd), do, jnp.zeros_like(do))
        qh = jnp.where(half_mask(q.shape,h,hd), q, jnp.zeros_like(q))
        delta = jnp.sum(prod[h*hd:(h+1)*hd], axis=0, keepdims=True)
        p = p_ref[h]
        ds = (p.astype(F32)*(dp_ref[h]-delta)).astype(BF16)
        dv_ref[...] += jnp.dot(p, doh, preferred_element_type=F32)
        dk_ref[...] += jnp.dot(ds, qh, preferred_element_type=F32)
        dqs.append(jnp.dot(kt_ref[h*hd:(h+1)*hd], ds, preferred_element_type=F32))
    dq_ref[...] = (jnp.concatenate(dqs,axis=0)*scale).T.astype(BF16)
    @pl.when(i==pl.num_programs(1)-1)
    def _():
        dk_ref[...] = dk_ref[...]*scale

def attn_bwd(q, do, o, k, v, p, scale, heads, QB):
    R, D = q.shape; N = k.shape[0]; hd = D//heads; per=128//hd; pairs=D//128
    row = pl.BlockSpec((QB,128),lambda p,i:(i,p))
    key = pl.BlockSpec((N,128),lambda p,i:(0,p))
    return pl.pallas_call(
        functools.partial(bwd_kernel, scale, hd),
        grid=(pairs, R//QB),
        in_specs=[row,row,row,key,key,pl.BlockSpec((per,N,QB),lambda p,i:(p,0,i))],
        out_specs=[row,key,key],
        out_shape=[jax.ShapeDtypeStruct((R,D),BF16), jax.ShapeDtypeStruct((N,D),F32), jax.ShapeDtypeStruct((N,D),F32)],
        scratch_shapes=[pltpu.VMEM((per,N,QB),F32), pltpu.VMEM((128,N),BF16)],
        compiler_params=pltpu.CompilerParams(vmem_limit_bytes=60<<20),
    )(q,do,o,k,v,p)


MESH = pl.DeviceIdType.MESH
TILE = 512
LAG = 3


def sum_kernel(sizes, tiles, count, *refs):
    p_refs, g_refs = refs[:count], refs[count : 2 * count]
    w_ref, s_ref, r0, r1, r2, r3, send_sem, recv_sem, own_sem, out_sem = refs[2 * count :]
    recv = (r0, r1, r2, r3)
    chunks = len(tiles)
    Y = sizes[2]
    dp = lax.axis_index("dp")
    fr = lax.axis_index("frame")
    z = dp // Y
    y = lax.rem(dp, Y)
    x = fr // 2
    core = lax.rem(fr, 2)
    first = core == 0
    me = (core, jnp.where(first, x, y), jnp.where(first, y, x), z)

    def device(kind, p):
        if kind == 0:
            return (dp, x * 2 + p)
        if kind == 3:
            return (p * Y + y, fr)
        along_x = first if kind == 1 else jnp.logical_not(first)
        return (z * Y + jnp.where(along_x, y, p), jnp.where(along_x, p, x) * 2 + core)

    def peer(k, o):
        return lax.rem(me[k] + o, sizes[k])

    pairs = [(k, o) for k in range(4) for o in range(1, sizes[k])]
    barrier = pltpu.get_barrier_semaphore()
    for k, o in pairs:
        pl.semaphore_signal(barrier, inc=1, device_id=device(k, peer(k, o)), device_id_type=MESH)
    pl.semaphore_wait(barrier, len(pairs))

    cut = [TILE]
    for k in range(4):
        cut.append(cut[-1] // sizes[k])
    split = cut[4] % 16 == 0
    if not split:
        cut[4] = cut[3]

    def start_of(level):
        at = 0
        for k in range(level):
            if k < 3 or split:
                at = at + me[k] * cut[k + 1]
        return pl.multiple_of(at, 16) if level else 0

    def scatter_copy(c, k, o):
        p = peer(k, o)
        at = start_of(k)
        if k < 3 or split:
            at = pl.multiple_of(at + p * cut[k + 1], 16)
        if k == 0:
            which, row, col = tiles[c]
            src = p_refs[which].at[pl.ds(row + at, cut[1]), pl.ds(col, TILE)]
        else:
            src = w_ref.at[c, pl.ds(at, cut[k + 1])]
        return pltpu.make_async_remote_copy(
            src_ref=src,
            dst_ref=recv[k].at[c, o - 1],
            send_sem=send_sem.at[c, k, o - 1],
            recv_sem=recv_sem.at[c, k, o - 1],
            device_id=device(k, p),
            device_id_type=MESH,
        )

    def gather_copy(c, k, o):
        here = s_ref.at[c, pl.ds(start_of(k + 1), cut[k + 1])]
        return pltpu.make_async_remote_copy(
            src_ref=here,
            dst_ref=here,
            send_sem=send_sem.at[c, 4 + k, o - 1],
            recv_sem=recv_sem.at[c, 4 + k, o - 1],
            device_id=device(k, peer(k, o)),
            device_id_type=MESH,
        )

    def own_copy(c):
        which, row, col = tiles[c]
        at = start_of(1)
        src = p_refs[which].at[pl.ds(row + at, cut[1]), pl.ds(col, TILE)]
        return pltpu.make_async_copy(src, w_ref.at[c, pl.ds(at, cut[1])], own_sem.at[c])

    def out_copy(c):
        which, row, col = tiles[c]
        dst = g_refs[which].at[pl.ds(row, TILE), pl.ds(col, TILE)]
        return pltpu.make_async_copy(s_ref.at[c], dst, out_sem.at[c])

    def add(c, k):
        at = start_of(k + 1)
        dst = w_ref if k < 3 else s_ref
        step = math.gcd(cut[k + 1], 64)

        def body(i, _):
            r = pl.multiple_of(at + i * step, 16)
            total = w_ref[c, pl.ds(r, step)].astype(F32)
            for o in range(1, sizes[k]):
                total = total + recv[k][
                    c, o - 1, pl.ds(pl.multiple_of(i * step, 16), step)
                ].astype(F32)
            dst[c, pl.ds(r, step)] = total.astype(BF16)
            return 0

        lax.fori_loop(0, cut[k + 1] // step, body, 0)

    for c in range(chunks):
        for o in range(1, sizes[0]):
            scatter_copy(c, 0, o).start()
        own_copy(c).start()

    stages = [("s", k) for k in range(4)] + [("g", k) for k in (3, 2, 1, 0) if k < 3 or split]
    copies = {"s": scatter_copy, "g": gather_copy}

    def finish(c, n):
        kind, k = stages[n]
        for o in range(1, sizes[k]):
            if n == 0:
                landed = recv[0].at[c, o - 1]
                pltpu.make_async_copy(landed, landed, recv_sem.at[c, 0, o - 1]).wait()
            else:
                copies[kind](c, k, o).wait_recv()
        if n == 0:
            half = w_ref.at[c, pl.ds(0, cut[1])]
            pltpu.make_async_copy(half, half, own_sem.at[c]).wait()
        if kind == "s":
            add(c, k)
        if n + 1 < len(stages):
            kind, k = stages[n + 1]
            for o in range(1, sizes[k]):
                copies[kind](c, k, o).start()

    def turn(t, _):
        for n in range(len(stages) - 1, -1, -1):
            c = t - LAG * n

            @pl.when((c >= 0) & (c < chunks))
            def _():
                finish(c, n)

        for c in range(chunks):

            @pl.when(t == c + LAG * (len(stages) - 1))
            def _():
                out_copy(c).start()

        return 0

    lax.fori_loop(0, chunks + LAG * (len(stages) - 1), turn, 0)
    for c in range(chunks):
        for o in range(1, sizes[0]):
            scatter_copy(c, 0, o).wait_send()

    def drain(c, _):
        for kind, k in stages[1:]:
            for o in range(1, sizes[k]):
                copies[kind](c, k, o).wait_send()
        return 0

    lax.fori_loop(0, chunks, drain, 0)
    for c in range(chunks):
        out_copy(c).wait()


def sum_everywhere(arrays, sizes, cid):
    tiles = []
    for n, a in enumerate(arrays):
        for row in range(0, a.shape[0], TILE):
            for col in range(0, a.shape[1], TILE):
                tiles.append((n, row, col))
    chunks = len(tiles)
    cut = [TILE]
    for n in sizes:
        cut.append(cut[-1] // n)
    if cut[4] % 16:
        cut[4] = cut[3]
    most = max(sizes) - 1
    spec = pl.BlockSpec(memory_space=pl.ANY)
    return pl.pallas_call(
        functools.partial(sum_kernel, sizes, tiles, len(arrays)),
        in_specs=[spec] * len(arrays),
        out_specs=[spec] * len(arrays),
        out_shape=[jax.ShapeDtypeStruct(a.shape, BF16) for a in arrays],
        scratch_shapes=[pltpu.VMEM((chunks, TILE, TILE), BF16)] * 2
        + [pltpu.VMEM((chunks, sizes[k] - 1, cut[k + 1], TILE), BF16) for k in range(4)]
        + [
            pltpu.SemaphoreType.DMA((chunks, 8, most)),
            pltpu.SemaphoreType.DMA((chunks, 8, most)),
            pltpu.SemaphoreType.DMA((chunks,)),
            pltpu.SemaphoreType.DMA((chunks,)),
        ],
        compiler_params=pltpu.CompilerParams(
            collective_id=cid, has_side_effects=True, vmem_limit_bytes=60 << 20
        ),
    )(*arrays)


def on_device(
    mel_frames,
    window_count,
    stem_weight,
    stem_bias,
    reduce_weight,
    reduce_bias,
    first_gain,
    first_shift,
    query_weight,
    query_bias,
    key_weight,
    value_weight,
    value_bias,
    output_weight,
    output_bias,
    second_gain,
    second_shift,
    hidden_weight,
    hidden_bias,
    return_weight,
    return_bias,
    cotangent,
):
    S, piece_frames, mels = mel_frames.shape
    piece = cotangent.shape[1]
    D = stem_weight.shape[2]
    hd = D // HEADS
    scale = hd ** (-0.5)
    F = lax.axis_size("frame")
    G = F // S
    T = S * piece
    R = -(-(T + 2) // 128) * 128
    f = lax.axis_index("frame")
    s = f // G
    r = f % G
    alive = s < window_count[0]

    def gather_window(x):
        parts = []
        out = jnp.zeros((S * x.shape[1], x.shape[2]), x.dtype)
        for t in range(S):
            part = lax.dynamic_index_in_dim(x, (f + t) % S, 0, keepdims=False)
            perm = [(p, ((p % S + t) % S) * G + p // S) for p in range(F)]
            got = lax.ppermute(part, "frame", perm)
            j = (s - t) % S
            out = lax.dynamic_update_slice(out, got, (j * x.shape[1], 0))
        return out

    def scatter_window(x):
        n = x.shape[0] // S
        out = jnp.zeros((S, n, x.shape[1]), x.dtype)
        for t in range(S):
            j = (s - t) % S
            part = lax.dynamic_slice(x, (j * n, 0), (n, x.shape[1]))
            perm = [(((p % S + t) % S) * G + p // S, p) for p in range(F)]
            got = lax.ppermute(part, "frame", perm)
            out = lax.dynamic_update_slice(out, got[None], ((f + t) % S, 0, 0))
        return out

    down = [(i, i + 1) for i in range(F) if (i + 1) % G != 0]
    up = [(i + 1, i) for i in range(F) if (i + 1) % G != 0]

    def with_halo(x):
        before = lax.ppermute(x[T - 1 : T], "frame", down)
        after = lax.ppermute(x[0:1], "frame", up)
        gap = jnp.zeros((R - T - 2, x.shape[1]), x.dtype)
        return jnp.concatenate([x, after, gap, before], axis=0)

    mel = gather_window(mel_frames.reshape(S, piece, 2 * mels))
    cot = gather_window(cotangent)
    cot = jnp.where(alive, cot, jnp.zeros_like(cot))
    mel = with_halo(mel)
    odd_before = jnp.roll(mel[:, mels:], 1, axis=0)
    even_after = jnp.roll(mel[:, :mels], -1, axis=0)
    columns = jnp.concatenate([odd_before, mel, even_after], axis=1)
    stem_matrix = stem_weight.reshape(3 * mels, D)
    gap = jnp.zeros((mels, D), BF16)
    stem_pair = jnp.concatenate(
        [
            jnp.concatenate([stem_matrix, gap], axis=0),
            jnp.concatenate([gap, stem_matrix], axis=0),
        ],
        axis=1,
    )
    stem_bias2 = jnp.concatenate([stem_bias, stem_bias])
    stem_linear = dot(columns, stem_pair) + stem_bias2
    row = lax.broadcasted_iota(jnp.int32, (R, 1), 0)
    valid = (row < T) | ((row == T) & (r < G - 1)) | ((row == R - 1) & (r > 0))
    stem_active = jnp.where(valid, gelu(stem_linear), 0.0).astype(BF16)

    odd_active_before = jnp.roll(stem_active[:, D:], 1, axis=0)[:T]
    conv_columns = jnp.concatenate([odd_active_before, stem_active[:T]], axis=1)
    reduce_matrix = reduce_weight.reshape(3 * D, D)
    conv_linear = dot(conv_columns, reduce_matrix) + reduce_bias
    stream = gelu(conv_linear) + positions_of(r * T, T, D)
    xhat1, r1 = norm_parts(stream)
    first_normed = (xhat1 * first_gain + first_shift).astype(BF16)
    query = (dot(first_normed, query_weight) + query_bias).astype(BF16)
    key = dot(first_normed, key_weight).astype(BF16)
    value = (dot(first_normed, value_weight) + value_bias).astype(BF16)
    keyval = jnp.concatenate([key, value], axis=1)
    others = []
    for t in range(1, G):
        perm = [(i, (i // G) * G + (i % G + t) % G) for i in range(F)]
        others.append(lax.ppermute(keyval, "frame", perm))
    whole = jnp.concatenate([keyval] + others, axis=0)
    tokens = whole.shape[0]
    key_all, value_all = whole[:, :D], whole[:, D:]
    query_ext = jnp.pad(query, ((0, R - T), (0, 0)))
    block = 256 if R % 256 == 0 else 128
    probs, attended_wide = attn_fwd(query_ext, key_all, value_all, scale, HEADS, block)
    attended = attended_wide[:T].astype(BF16)
    mixed = stream + dot(attended, output_weight) + output_bias
    xhat2, r2 = norm_parts(mixed)
    second_normed = (xhat2 * second_gain + second_shift).astype(BF16)
    hidden_linear = dot(second_normed, hidden_weight) + hidden_bias
    hidden_cdf, hidden_pdf = phi_parts(hidden_linear)
    hidden_active = (hidden_linear * hidden_cdf).astype(BF16)
    layer = mixed + dot(hidden_active, return_weight) + return_bias
    layer = jnp.where(alive, layer, 0.0).astype(BF16)
    layer_output = scatter_window(layer)

    return_bias_grad = column_total(cot)
    return_weight_grad = outer(hidden_active, cot)
    slope = hidden_cdf + hidden_linear * hidden_pdf
    hidden_grad = (slope * dot_t(cot, return_weight)).astype(BF16)
    hidden_bias_grad = column_total(hidden_grad)
    hidden_weight_grad = outer(second_normed, hidden_grad)
    inner, second_gain_grad, second_shift_grad = norm_pull(
        xhat2, r2, second_gain, dot_t(hidden_grad, hidden_weight)
    )
    mixed_grad = cot.astype(F32) + inner
    branch_grad = mixed_grad.astype(BF16)
    output_bias_grad = column_total(branch_grad)
    output_weight_grad = outer(attended, branch_grad)

    attended_grad = jnp.pad(dot_t(branch_grad, output_weight).astype(BF16), ((0, R - T), (0, 0)))
    query_grad, key_term, value_term = attn_bwd(
        query_ext, attended_grad, attended_wide, key_all, value_all, probs, scale, HEADS, block
    )
    query_grad = query_grad[:T]
    terms = jnp.concatenate([key_term, value_term], axis=1)
    total = terms[:T]
    for t in range(1, G):
        perm = [((i // G) * G + (i % G + t) % G, i) for i in range(F)]
        back = lax.ppermute(terms[t * T : (t + 1) * T], "frame", perm)
        total = total + back
    key_grad = total[:, :D].astype(BF16)
    value_grad = total[:, D:].astype(BF16)
    query_weight_grad = outer(first_normed, query_grad)
    key_weight_grad = outer(first_normed, key_grad)
    value_weight_grad = outer(first_normed, value_grad)
    query_bias_grad = column_total(query_grad)
    value_bias_grad = column_total(value_grad)
    normed_grad = (
        dot_t(query_grad, query_weight)
        + dot_t(key_grad, key_weight)
        + dot_t(value_grad, value_weight)
    )
    inner, first_gain_grad, first_shift_grad = norm_pull(xhat1, r1, first_gain, normed_grad)
    stream_grad = mixed_grad + inner
    conv_grad = (gelu_slope(conv_linear) * stream_grad).astype(BF16)
    reduce_bias_grad = column_total(conv_grad)
    reduce_matrix_grad = outer(conv_columns, conv_grad)
    conv_ext = with_halo(conv_grad)
    conv_after = jnp.roll(conv_ext, -1, axis=0)
    pair_grad = dot_t(conv_ext, reduce_matrix[D:])
    third_grad = dot_t(conv_after, reduce_matrix[:D])
    active_grad = pair_grad + jnp.concatenate([jnp.zeros_like(third_grad), third_grad], axis=1)
    stem_grad = jnp.where(valid, gelu_slope(stem_linear) * active_grad, 0.0).astype(BF16)
    own = stem_grad[:T]
    totals = column_total(own)
    stem_bias_grad = totals[:D] + totals[D:]
    pair_matrix_grad = outer(columns[:T], own)
    stem_matrix_grad = pair_matrix_grad[: 3 * mels, :D] + pair_matrix_grad[mels:, D:]
    mel_columns = dot_t(stem_grad, stem_pair)
    mel_pair = (
        mel_columns[:, mels : 3 * mels]
        + jnp.concatenate(
            [
                jnp.roll(mel_columns[:, 3 * mels :], 1, axis=0),
                jnp.roll(mel_columns[:, :mels], -1, axis=0),
            ],
            axis=1,
        )
    )[:T]
    mel_gradient = scatter_window(mel_pair).reshape(S, piece_frames, mels)

    small = [
        stem_bias_grad,
        reduce_bias_grad,
        first_gain_grad,
        first_shift_grad,
        query_bias_grad,
        value_bias_grad,
        output_bias_grad,
        second_gain_grad,
        second_shift_grad,
        hidden_bias_grad,
        return_bias_grad,
    ]
    sizes = (2, F // 2, F // 2, lax.axis_size("dp") // (F // 2))
    short = jnp.concatenate([stem_matrix_grad, jnp.concatenate(small).reshape(-1, D)], axis=0)
    rows = short.shape[0]
    short = jnp.pad(short, ((0, -rows % TILE), (0, 0)))
    terms = [
        return_weight_grad,
        hidden_weight_grad,
        output_weight_grad,
        reduce_matrix_grad,
        query_weight_grad,
        key_weight_grad,
        value_weight_grad,
        short,
    ]
    terms = sum_everywhere([v.astype(BF16) for v in terms], sizes, 0)
    return_w, hidden_w, output_w, reduce_w, query_w, key_w, value_w, short = [
        v.astype(F32) for v in terms
    ]
    stem_w = short[: 3 * mels]
    flat = short[3 * mels : rows].reshape(-1)
    lengths = [v.shape[0] for v in small]
    small = []
    at = 0
    for n in lengths:
        small.append(flat[at : at + n])
        at += n
    return (
        layer_output,
        mel_gradient,
        stem_w.reshape(3, mels, D),
        small[0],
        reduce_w.reshape(3, D, D),
        small[1],
        small[2],
        small[3],
        query_w,
        small[4],
        key_w,
        value_w,
        small[5],
        output_w,
        small[6],
        small[7],
        small[8],
        hidden_w,
        small[9],
        return_w,
        small[10],
    )


def solution(mesh):
    cut = P("dp", "frame", None)
    return jax.shard_map(
        on_device,
        mesh=mesh,
        in_specs=(cut, P("dp")) + (P(),) * 19 + (cut,),
        out_specs=(cut, cut) + (P(),) * 19,
        check_vma=False,
    )
```

```python
import functools
import math

import jax
import jax.numpy as jnp
from jax import lax
from jax.experimental import pallas as pl
from jax.experimental.pallas import tpu as pltpu
from jax.sharding import PartitionSpec as P

HEADS = 8
EPS = 1e-05
F32 = jnp.float32
BF16 = jnp.bfloat16
PHI_SLOPE = 0.28
PHI_POLY = (
    0.1167294156016242,
    0.06622785593379492,
    0.27197610469464767,
    -0.24067367858721922,
    0.3920693507793772,
    -0.10632905941542621,
)


def phi_parts(v):
    size = jnp.abs(v)
    t = 1.0 / (1.0 + PHI_SLOPE * size)
    bell = jnp.exp(-0.5 * v * v)
    poly = PHI_POLY[5]
    for c in PHI_POLY[4::-1]:
        poly = poly * t + c
    tail = poly * t * bell
    cdf = jnp.where(v >= 0, 1.0 - tail, tail)
    return cdf, bell * (1.0 / math.sqrt(2.0 * math.pi))


def gelu(v):
    cdf, _ = phi_parts(v)
    return v * cdf


def gelu_slope(v):
    cdf, pdf = phi_parts(v)
    return cdf + v * pdf


def dot(left, right):
    return jnp.dot(left, right, preferred_element_type=F32)


def dot_t(left, right):
    return lax.dot_general(left, right, (((1,), (1,)), ((), ())), preferred_element_type=F32)


def outer(left, right):
    return lax.dot_general(left, right, (((0,), (0,)), ((), ())), preferred_element_type=F32)


def column_total(x):
    return jnp.sum(x.astype(F32), axis=0)


def norm_parts(x):
    centred = x - jnp.mean(x, axis=-1, keepdims=True)
    r = lax.rsqrt(jnp.mean(centred * centred, axis=-1, keepdims=True) + EPS)
    return centred * r, r


def norm_pull(xhat, r, gain, dy):
    dh = dy * gain
    inner = r * (
        dh
        - jnp.mean(dh, axis=-1, keepdims=True)
        - xhat * jnp.mean(dh * xhat, axis=-1, keepdims=True)
    )
    return inner, column_total(dy * xhat), column_total(dy)


def positions_of(first, count, width):
    half = width // 2
    step = math.log(10000.0) / (half - 1)
    rate = jnp.exp(-step * jnp.arange(half, dtype=F32))[None, :]
    fine = math.gcd(count, 16)
    coarse = count // fine
    a = (first + fine * jnp.arange(coarse, dtype=jnp.int32)).astype(F32)[:, None] * rate
    b = jnp.arange(fine, dtype=jnp.int32).astype(F32)[:, None] * rate
    sa, ca = jnp.sin(a)[:, None, :], jnp.cos(a)[:, None, :]
    sb, cb = jnp.sin(b)[None, :, :], jnp.cos(b)[None, :, :]
    both = jnp.concatenate([sa * cb + ca * sb, ca * cb - sa * sb], axis=2)
    return both.reshape(count, width)


def half_mask(shape, h, hd):
    lane = lax.broadcasted_iota(jnp.int32, shape, 1)
    return (lane >= h*hd) & (lane < (h+1)*hd)

MESH = pl.DeviceIdType.MESH


def group_peer(G, o):
    fr = lax.axis_index("frame")
    return (lax.axis_index("dp"), fr // G * G + lax.rem(lax.rem(fr, G) + o, G))


def greet(F):
    barrier = pltpu.get_barrier_semaphore()
    for o in range(1, F):
        pl.semaphore_signal(barrier, inc=1, device_id=group_peer(F, o), device_id_type=MESH)


def meet(F):
    greet(F)
    pl.semaphore_wait(pltpu.get_barrier_semaphore(), F - 1)


class Move:
    def __init__(self, gather, F, src, dst, sems):
        self.src, self.dst = src, dst
        self.send, self.recv, self.own = sems
        self.S = src.shape[0]
        S, G = self.S, F // src.shape[0]
        self.dp, self.fr = lax.axis_index("dp"), lax.axis_index("frame")
        over = [a * G + self.fr // S for a in range(S)]
        back = [lax.rem(self.fr, G) * S + a for a in range(S)]
        self.to, self.sender = (over, back) if gather else (back, over)
        self.place = lax.rem(self.fr, S) if gather else self.fr // G

    def far(self, a):
        return pltpu.make_async_remote_copy(
            src_ref=self.src.at[a],
            dst_ref=self.dst.at[self.place],
            send_sem=self.send.at[a],
            recv_sem=self.recv.at[self.place],
            device_id=(self.dp, self.to[a]),
            device_id_type=MESH,
        )

    def near(self, a):
        return pltpu.make_async_copy(self.src.at[a], self.dst.at[self.place], self.own.at[a])

    def start(self):
        for a in range(self.S):

            @pl.when(self.to[a] != self.fr)
            def _():
                self.far(a).start()

            @pl.when(self.to[a] == self.fr)
            def _():
                self.near(a).start()

    def wait(self):
        for a in range(self.S):

            @pl.when(self.to[a] != self.fr)
            def _():
                self.far(a).wait_send()

            @pl.when(self.to[a] == self.fr)
            def _():
                self.near(a).wait()

            @pl.when(self.sender[a] != self.fr)
            def _():
                landed = self.dst.at[a]
                pltpu.make_async_copy(landed, landed, self.recv.at[a]).wait()


def move_sems(S):
    return [pltpu.SemaphoreType.DMA((S,))] * 3


def lanes_of(pair):
    return pl.ds(pl.multiple_of(pair * 128, 128), 128)


def fwd_kernel(
    scale,
    hd,
    F,
    G,
    T,
    pairs,
    q_ref,
    k_own,
    v_own,
    c_ref,
    p_ref,
    o_ref,
    k_all,
    v_all,
    d_ref,
    s_ref,
    k_buf,
    v_buf,
    send_sem,
    recv_sem,
    own_sem,
    out_sem,
    *sems,
):
    per = 128 // hd
    pair, i = pl.program_id(0), pl.program_id(1)
    rows = k_own.shape[0]
    both = ((k_own, k_buf), (v_own, v_buf))
    kept = ((k_buf, k_all), (v_buf, v_all))

    def own_copy(n, p):
        src, dst = both[n]
        return pltpu.make_async_copy(
            src.at[:, lanes_of(p)], dst.at[pl.ds(0, rows), lanes_of(p)], own_sem.at[n, p]
        )

    def keep(n, p):
        src, dst = kept[n]
        return pltpu.make_async_copy(
            src.at[:, lanes_of(p)], dst.at[:, lanes_of(p)], out_sem.at[n, p]
        )

    def copy_to(n, p, o):
        src, dst = both[n]
        return pltpu.make_async_remote_copy(
            src_ref=src.at[:, lanes_of(p)],
            dst_ref=dst.at[pl.ds((G - o) * rows, rows), lanes_of(p)],
            send_sem=send_sem.at[n, p, o - 1],
            recv_sem=recv_sem.at[n, p, o - 1],
            device_id=group_peer(G, o),
            device_id_type=MESH,
        )

    @pl.when((pair == 0) & (i == 0))
    def _():
        for p in range(pairs):
            for n in range(2):
                own_copy(n, p).start()
        meet(F)
        for p in range(pairs):
            for n in range(2):
                for o in range(1, G):
                    copy_to(n, p, o).start()
        Move(True, F, c_ref, d_ref, sems).start()

    @pl.when(i == 0)
    def _():
        for n in range(2):
            own_copy(n, pair).wait()
            for o in range(1, G):
                copy_to(n, pair, o).wait_recv()
            keep(n, pair).start()

    k = k_buf[:, lanes_of(pair)]
    vt = v_buf[:, lanes_of(pair)].T
    outs = []
    for h in range(per):
        q = q_ref[...]
        q = jnp.where(half_mask(q.shape, h, hd), q, jnp.zeros_like(q))
        s_ref[h] = lax.dot_general(k, q, (((1,), (1,)), ((), ())), preferred_element_type=F32)
    for h in range(per):
        s = s_ref[h]
        if rows != T:
            at = lax.rem(lax.broadcasted_iota(jnp.int32, s.shape, 0), rows)
            s = jnp.where(at < T, s, -1e30)
        m = jnp.max(s, axis=0, keepdims=True)
        e = jnp.exp((s - m) * scale)
        l = jnp.sum(e, axis=0, keepdims=True)
        p = (e * (1.0 / l)).astype(BF16)
        p_ref[h] = p
        outs.append(jnp.dot(vt[h * hd : (h + 1) * hd], p, preferred_element_type=F32))
    o_ref[...] = jnp.concatenate(outs, axis=0).T

    @pl.when((pair == pairs - 1) & (i == pl.num_programs(1) - 1))
    def _():
        for p in range(pairs):
            for n in range(2):
                keep(n, p).wait()
                for o in range(1, G):
                    copy_to(n, p, o).wait_send()
        Move(True, F, c_ref, d_ref, sems).wait()


def attn_fwd(q, k, v, slots, scale, heads, QB, F, T):
    G = F // slots.shape[0]
    R, D = q.shape
    N = k.shape[0] * G
    hd = D // heads
    per = 128 // hd
    pairs = D // 128
    far = pl.BlockSpec(memory_space=pl.ANY)
    sems = pltpu.SemaphoreType.DMA((2, pairs, G - 1))
    return pl.pallas_call(
        functools.partial(fwd_kernel, scale, hd, F, G, T, pairs),
        grid=(pairs, R // QB),
        in_specs=[pl.BlockSpec((QB, 128), lambda p, i: (i, p)), far, far, far],
        out_specs=[
            pl.BlockSpec((per, N, QB), lambda p, i: (p, 0, i)),
            pl.BlockSpec((QB, 128), lambda p, i: (i, p)),
            far,
            far,
            far,
        ],
        out_shape=[
            jax.ShapeDtypeStruct((heads, N, R), BF16),
            jax.ShapeDtypeStruct((R, D), F32),
            jax.ShapeDtypeStruct((N, D), BF16),
            jax.ShapeDtypeStruct((N, D), BF16),
            jax.ShapeDtypeStruct(slots.shape, slots.dtype),
        ],
        scratch_shapes=[
            pltpu.VMEM((per, N, QB), F32),
            pltpu.VMEM((N, D), BF16),
            pltpu.VMEM((N, D), BF16),
            sems,
            sems,
            pltpu.SemaphoreType.DMA((2, pairs)),
            pltpu.SemaphoreType.DMA((2, pairs)),
        ]
        + move_sems(slots.shape[0]),
        compiler_params=pltpu.CompilerParams(
            collective_id=1, has_side_effects=True, vmem_limit_bytes=60 << 20
        ),
    )(q, k, v, slots)


def bwd_kernel(
    scale,
    hd,
    F,
    G,
    pairs,
    q_ref,
    do_ref,
    o_ref,
    k_ref,
    v_ref,
    p_ref,
    y_ref,
    dq_ref,
    dk_ref,
    dv_ref,
    z_ref,
    dp_ref,
    kt_ref,
    acc_ref,
    got_ref,
    send_sem,
    recv_sem,
    *sems,
):
    per = 128 // hd
    pair, i = pl.program_id(0), pl.program_id(1)
    slot = lax.rem(pair, 2)
    rows = dk_ref.shape[0]

    def copy_to(n, p, o):
        return pltpu.make_async_remote_copy(
            src_ref=acc_ref.at[lax.rem(p, 2), n, pl.ds(o * rows, rows)],
            dst_ref=got_ref.at[p, n, o - 1],
            send_sem=send_sem.at[n, p, o - 1],
            recv_sem=recv_sem.at[n, p, o - 1],
            device_id=group_peer(G, o),
            device_id_type=MESH,
        )

    every = [(n, o) for n in range(2) for o in range(1, G)]

    @pl.when((pair == 0) & (i == 0))
    def _():
        meet(F)
        Move(False, F, y_ref, z_ref, sems).start()

    @pl.when((pair >= 2) & (i == 0))
    def _():
        for n, o in every:
            copy_to(n, pair - 2, o).wait_send()

    @pl.when(i == 0)
    def _():
        kt_ref[...] = k_ref[...].T
        acc_ref[slot] = jnp.zeros(acc_ref.shape[1:], F32)

    do = do_ref[...]
    q = q_ref[...]
    v = v_ref[...]
    prod = (do.astype(F32) * o_ref[...]).T
    for h in range(per):
        doh = jnp.where(half_mask(do.shape, h, hd), do, jnp.zeros_like(do))
        dp_ref[h] = lax.dot_general(v, doh, (((1,), (1,)), ((), ())), preferred_element_type=F32)
    dqs = []
    for h in range(per):
        doh = jnp.where(half_mask(do.shape, h, hd), do, jnp.zeros_like(do))
        qh = jnp.where(half_mask(q.shape, h, hd), q, jnp.zeros_like(q))
        delta = jnp.sum(prod[h * hd : (h + 1) * hd], axis=0, keepdims=True)
        p = p_ref[h]
        ds = (p.astype(F32) * (dp_ref[h] - delta)).astype(BF16)
        acc_ref[slot, 1] += jnp.dot(p, doh, preferred_element_type=F32)
        acc_ref[slot, 0] += jnp.dot(ds, qh, preferred_element_type=F32)
        dqs.append(jnp.dot(kt_ref[h * hd : (h + 1) * hd], ds, preferred_element_type=F32))
    dq_ref[...] = (jnp.concatenate(dqs, axis=0) * scale).T.astype(BF16)

    def finish(p):
        for n, o in every:
            copy_to(n, p, o).wait_recv()
        for n, out, factor in ((0, dk_ref, scale), (1, dv_ref, 1.0)):
            total = acc_ref[lax.rem(p, 2), n, pl.ds(0, rows)]
            for o in range(1, G):
                total = total + got_ref[p, n, o - 1]
            out[:, lanes_of(p)] = (total * factor).astype(BF16)

    ends = i == pl.num_programs(1) - 1

    @pl.when(ends & (pair >= 1))
    def _():
        finish(pair - 1)

    @pl.when(ends)
    def _():
        for n, o in every:
            copy_to(n, pair, o).start()

    @pl.when(ends & (pair == pairs - 1))
    def _():
        finish(pair)
        for p in range(max(pairs - 2, 0), pairs):
            for n, o in every:
                copy_to(n, p, o).wait_send()
        Move(False, F, y_ref, z_ref, sems).wait()


def attn_bwd(q, do, o, k, v, p, pieces, scale, heads, QB, F):
    G = F // pieces.shape[0]
    far = pl.BlockSpec(memory_space=pl.ANY)
    R, D = q.shape
    N = k.shape[0]
    hd = D // heads
    per = 128 // hd
    pairs = D // 128
    row = pl.BlockSpec((QB, 128), lambda p, i: (i, p))
    key = pl.BlockSpec((N, 128), lambda p, i: (0, p))
    near = pl.BlockSpec(memory_space=pltpu.VMEM)
    sems = pltpu.SemaphoreType.DMA((2, pairs, G - 1))
    own = jax.ShapeDtypeStruct((N // G, D), BF16)
    return pl.pallas_call(
        functools.partial(bwd_kernel, scale, hd, F, G, pairs),
        grid=(pairs, R // QB),
        in_specs=[row, row, row, key, key, pl.BlockSpec((per, N, QB), lambda p, i: (p, 0, i)), far],
        out_specs=[row, near, near, far],
        out_shape=[
            jax.ShapeDtypeStruct((R, D), BF16),
            own,
            own,
            jax.ShapeDtypeStruct(pieces.shape, pieces.dtype),
        ],
        scratch_shapes=[
            pltpu.VMEM((per, N, QB), F32),
            pltpu.VMEM((128, N), BF16),
            pltpu.VMEM((2, 2, N, 128), F32),
            pltpu.VMEM((pairs, 2, G - 1, N // G, 128), F32),
            sems,
            sems,
        ]
        + move_sems(pieces.shape[0]),
        compiler_params=pltpu.CompilerParams(
            collective_id=2, has_side_effects=True, vmem_limit_bytes=60 << 20
        ),
    )(q, do, o, k, v, p, pieces)


TILE = 512
LAG = 3
AHEAD = 3


def pick(c, values):
    out = values[0]
    for n in range(1, len(values)):
        if values[n] != values[n - 1]:
            out = jnp.where(c >= n, values[n], out)
    return out


def sum_kernel(sizes, F, used, plan, *refs):
    places, left_at, right_at, lefts, rights, n_in, n_out = plan
    in_refs, short_ref, piece_ref = refs[: n_in - 2], refs[n_in - 2], refs[n_in - 1]
    g_refs, slot_ref = refs[n_in : n_in + n_out - 1], refs[n_in + n_out - 1]
    refs = refs[n_in + n_out :]
    l_ref, m_ref, t_ref, w_ref, s_ref, r0, r1, r2, r3 = refs[:9]
    send_sem, recv_sem, load_sem, out_sem, *sems = refs[9:]
    t_ref[...] = jnp.zeros_like(t_ref)
    recv = (r0, r1, r2, r3)
    chunks = len(places)
    T = l_ref.shape[1]
    Y = sizes[2]
    dp = lax.axis_index("dp")
    fr = lax.axis_index("frame")
    z = dp // Y
    y = lax.rem(dp, Y)
    x = fr // 2
    core = lax.rem(fr, 2)
    first = core == 0
    me = (core, jnp.where(first, x, y), jnp.where(first, y, x), z)

    loads = []
    for buf, sources, base in ((l_ref, lefts, 0), (m_ref, rights, len(lefts))):
        for n, (which, col) in enumerate(sources):
            src = in_refs[which].at[pl.ds(0, T), pl.ds(col, TILE)]
            loads.append(pltpu.make_async_copy(src, buf.at[n], load_sem.at[base + n]))
    loads.append(
        pltpu.make_async_copy(short_ref, w_ref.at[chunks - 1], load_sem.at[len(lefts) + len(rights)])
    )
    due = [0] * len(loads)
    for n in range(len(lefts)):
        due[n] = left_at.index(n)
    for n in range(len(rights)):
        due[len(lefts) + n] = right_at.index(n)
    due[-1] = chunks - 1
    for n in sorted(range(len(loads)), key=lambda n: (due[n], n)):
        loads[n].start()

    def device(kind, p):
        if kind == 0:
            return (dp, x * 2 + p)
        if kind == 3:
            return (p * Y + y, fr)
        along_x = first if kind == 1 else jnp.logical_not(first)
        return (z * Y + jnp.where(along_x, y, p), jnp.where(along_x, p, x) * 2 + core)

    def peer(k, o):
        return lax.rem(me[k] + o, sizes[k])

    pairs = [(k, o) for k in range(4) for o in range(1, sizes[k])]
    barrier = pltpu.get_barrier_semaphore()
    for k, o in pairs:
        pl.semaphore_signal(barrier, inc=1, device_id=device(k, peer(k, o)), device_id_type=MESH)
    greet(F)
    pl.semaphore_wait(barrier, len(pairs) + F - 1)
    move = Move(False, F, piece_ref, slot_ref, sems)
    move.start()

    cut = [TILE]
    for k in range(4):
        cut.append(cut[-1] // sizes[k])
    split = cut[4] % 16 == 0
    if not split:
        cut[4] = cut[3]

    def start_of(level):
        at = 0
        for k in range(level):
            if k < 3 or split:
                at = at + me[k] * cut[k + 1]
        return pl.multiple_of(at, 16) if level else 0

    def scatter_copy(c, k, o):
        p = peer(k, o)
        at = start_of(k)
        if k < 3 or split:
            at = pl.multiple_of(at + p * cut[k + 1], 16)
        return pltpu.make_async_remote_copy(
            src_ref=w_ref.at[c, pl.ds(at, cut[k + 1])],
            dst_ref=recv[k].at[c, o - 1],
            send_sem=send_sem.at[c, k, o - 1],
            recv_sem=recv_sem.at[c, k, o - 1],
            device_id=device(k, p),
            device_id_type=MESH,
        )

    def gather_copy(c, k, o):
        here = s_ref.at[c, pl.ds(start_of(k + 1), cut[k + 1])]
        return pltpu.make_async_remote_copy(
            src_ref=here,
            dst_ref=here,
            send_sem=send_sem.at[c, 4 + k, o - 1],
            recv_sem=recv_sem.at[c, 4 + k, o - 1],
            device_id=device(k, peer(k, o)),
            device_id_type=MESH,
        )

    def out_copy(c):
        which, row, col = places[c]
        dst = g_refs[which].at[pl.ds(row, TILE), pl.ds(col, TILE)]
        return pltpu.make_async_copy(s_ref.at[c], dst, out_sem.at[c])

    def add(c, k):
        at = start_of(k + 1)
        dst = w_ref if k < 3 else s_ref
        step = math.gcd(cut[k + 1], 64)

        def body(i, _):
            r = pl.multiple_of(at + i * step, 16)
            total = w_ref[c, pl.ds(r, step)].astype(F32)
            for o in range(1, sizes[k]):
                total = total + recv[k][
                    c, o - 1, pl.ds(pl.multiple_of(i * step, 16), step)
                ].astype(F32)
            dst[c, pl.ds(r, step)] = total.astype(BF16)
            return 0

        lax.fori_loop(0, cut[k + 1] // step, body, 0)

    stages = [("s", k) for k in range(4)] + [("g", k) for k in (3, 2, 1, 0) if k < 3 or split]
    copies = {"s": scatter_copy, "g": gather_copy}

    def finish(c, n):
        kind, k = stages[n]
        for o in range(1, sizes[k]):
            copies[kind](c, k, o).wait_recv()
        if kind == "s":
            add(c, k)
        if n + 1 < len(stages):
            kind, k = stages[n + 1]
            for o in range(1, sizes[k]):
                copies[kind](c, k, o).start()

    last = LAG * (len(stages) - 1) + AHEAD

    def turn(t, _):
        for n in range(len(loads)):

            @pl.when(t == due[n])
            def _():
                loads[n].wait()

        @pl.when(t < chunks - 1)
        def _():
            left = l_ref[pick(t, left_at)]
            right = m_ref[pick(t, right_at)]
            w_ref[t] = outer(left, right).astype(BF16)
            ones = jnp.ones((16, T), BF16)
            t_ref[pl.ds(pick(t, right_at), 1)] = dot(ones, right)[:1]

        @pl.when(t == chunks - 1)
        def _():
            w_ref[chunks - 1, pl.ds(used, t_ref.shape[0])] = t_ref[...].astype(BF16)

        @pl.when((t >= 1) & (t <= chunks))
        def _():
            for o in range(1, sizes[0]):
                scatter_copy(t - 1, 0, o).start()

        for n in range(len(stages) - 1, -1, -1):
            c = t - AHEAD - LAG * n

            @pl.when((c >= 0) & (c < chunks))
            def _():
                finish(c, n)

        for c in range(chunks):

            @pl.when(t == c + last)
            def _():
                out_copy(c).start()

        return 0

    lax.fori_loop(0, chunks + last, turn, 0)

    def drain(c, _):
        for kind, k in stages:
            for o in range(1, sizes[k]):
                copies[kind](c, k, o).wait_send()
        return 0

    lax.fori_loop(0, chunks, drain, 0)
    move.wait()
    for c in range(chunks):
        out_copy(c).wait()


def sum_everywhere(products, short, used, pieces, F, sizes, cid):
    arrays, lefts, rights = [], [], []
    places, left_at, right_at, shapes = [], [], [], []

    def slots_of(pieces, slots):
        found = []
        for array, width in pieces:
            which = next((n for n, a in enumerate(arrays) if a is array), None)
            if which is None:
                which = len(arrays)
                arrays.append(array)
            for col in range(0, width, TILE):
                if (which, col) not in slots:
                    slots.append((which, col))
                found.append(slots.index((which, col)))
        return found

    for n, (left, right) in enumerate(products):
        a, b = slots_of(left, lefts), slots_of(right, rights)
        shapes.append((len(a) * TILE, len(b) * TILE))
        for i, u in enumerate(a):
            for j, v in enumerate(b):
                places.append((n, i * TILE, j * TILE))
                left_at.append(u)
                right_at.append(v)
    places.append((len(products), 0, 0))
    shapes.append(short.shape)
    T = min(a.shape[0] for a in arrays)
    chunks = len(places)
    cut = [TILE]
    for n in sizes:
        cut.append(cut[-1] // n)
    if cut[4] % 16:
        cut[4] = cut[3]
    most = max(sizes) - 1
    spec = pl.BlockSpec(memory_space=pl.ANY)
    sums = len(rights) + -len(rights) % 16
    plan = (places, left_at, right_at, lefts, rights, len(arrays) + 2, len(shapes) + 1)
    return pl.pallas_call(
        functools.partial(sum_kernel, sizes, F, used, plan),
        in_specs=[spec] * (len(arrays) + 2),
        out_specs=[spec] * (len(shapes) + 1),
        out_shape=[jax.ShapeDtypeStruct(v, BF16) for v in shapes]
        + [jax.ShapeDtypeStruct(pieces.shape, pieces.dtype)],
        scratch_shapes=[
            pltpu.VMEM((len(lefts), T, TILE), BF16),
            pltpu.VMEM((len(rights), T, TILE), BF16),
            pltpu.VMEM((sums, TILE), F32),
        ]
        + [pltpu.VMEM((chunks, TILE, TILE), BF16)] * 2
        + [pltpu.VMEM((chunks, sizes[k] - 1, cut[k + 1], TILE), BF16) for k in range(4)]
        + [
            pltpu.SemaphoreType.DMA((chunks, 8, most)),
            pltpu.SemaphoreType.DMA((chunks, 8, most)),
            pltpu.SemaphoreType.DMA((len(lefts) + len(rights) + 1,)),
            pltpu.SemaphoreType.DMA((chunks,)),
        ]
        + move_sems(pieces.shape[0]),
        compiler_params=pltpu.CompilerParams(
            collective_id=cid, has_side_effects=True, vmem_limit_bytes=60 << 20
        ),
    )(*arrays, short, pieces)


def on_device(
    mel_frames,
    window_count,
    stem_weight,
    stem_bias,
    reduce_weight,
    reduce_bias,
    first_gain,
    first_shift,
    query_weight,
    query_bias,
    key_weight,
    value_weight,
    value_bias,
    output_weight,
    output_bias,
    second_gain,
    second_shift,
    hidden_weight,
    hidden_bias,
    return_weight,
    return_bias,
    cotangent,
):
    S, piece_frames, mels = mel_frames.shape
    piece = cotangent.shape[1]
    D = stem_weight.shape[2]
    hd = D // HEADS
    scale = hd ** (-0.5)
    F = lax.axis_size("frame")
    G = F // S
    T = S * piece
    R = -(-(T + 2) // 128) * 128
    f = lax.axis_index("frame")
    s = f // G
    r = f % G
    alive = s < window_count[0]

    def gather_window(x):
        parts = []
        out = jnp.zeros((S * x.shape[1], x.shape[2]), x.dtype)
        for t in range(S):
            part = lax.dynamic_index_in_dim(x, (f + t) % S, 0, keepdims=False)
            perm = [(p, ((p % S + t) % S) * G + p // S) for p in range(F)]
            got = lax.ppermute(part, "frame", perm)
            j = (s - t) % S
            out = lax.dynamic_update_slice(out, got, (j * x.shape[1], 0))
        return out

    down = [(i, i + 1) for i in range(F) if (i + 1) % G != 0]
    up = [(i + 1, i) for i in range(F) if (i + 1) % G != 0]

    def with_halo(x):
        before = lax.ppermute(x[T - 1 : T], "frame", down)
        after = lax.ppermute(x[0:1], "frame", up)
        gap = jnp.zeros((R - T - 2, x.shape[1]), x.dtype)
        return jnp.concatenate([x, after, gap, before], axis=0)

    mel = gather_window(mel_frames.reshape(S, piece, 2 * mels))
    mel = with_halo(mel)
    odd_before = jnp.roll(mel[:, mels:], 1, axis=0)
    even_after = jnp.roll(mel[:, :mels], -1, axis=0)
    columns = jnp.concatenate([odd_before, mel, even_after], axis=1)
    stem_matrix = stem_weight.reshape(3 * mels, D)
    gap = jnp.zeros((mels, D), BF16)
    stem_pair = jnp.concatenate(
        [
            jnp.concatenate([stem_matrix, gap], axis=0),
            jnp.concatenate([gap, stem_matrix], axis=0),
        ],
        axis=1,
    )
    stem_bias2 = jnp.concatenate([stem_bias, stem_bias])
    stem_linear = dot(columns, stem_pair) + stem_bias2
    row = lax.broadcasted_iota(jnp.int32, (R, 1), 0)
    valid = (row < T) | ((row == T) & (r < G - 1)) | ((row == R - 1) & (r > 0))
    stem_active = jnp.where(valid, gelu(stem_linear), 0.0).astype(BF16)

    odd_active_before = jnp.roll(stem_active[:, D:], 1, axis=0)[:T]
    conv_columns = jnp.concatenate([odd_active_before, stem_active[:T]], axis=1)
    reduce_matrix = reduce_weight.reshape(3 * D, D)
    conv_linear = dot(conv_columns, reduce_matrix) + reduce_bias
    stream = gelu(conv_linear) + positions_of(r * T, T, D)
    xhat1, r1 = norm_parts(stream)
    first_normed = (xhat1 * first_gain + first_shift).astype(BF16)
    query = (dot(first_normed, query_weight) + query_bias).astype(BF16)
    key = dot(first_normed, key_weight).astype(BF16)
    value = (dot(first_normed, value_weight) + value_bias).astype(BF16)
    key = jnp.pad(key, ((0, -T % 16), (0, 0)))
    value = jnp.pad(value, ((0, -T % 16), (0, 0)))
    query_ext = jnp.pad(query, ((0, R - T), (0, 0)))
    block = 256 if R % 256 == 0 else 128
    probs, attended_wide, key_all, value_all, cot = attn_fwd(
        query_ext, key, value, cotangent, scale, HEADS, block, F, T
    )
    cot = cot.reshape(T, D)
    cot = jnp.where(alive, cot, jnp.zeros_like(cot))
    attended = attended_wide[:T].astype(BF16)
    mixed = stream + dot(attended, output_weight) + output_bias
    xhat2, r2 = norm_parts(mixed)
    second_normed = (xhat2 * second_gain + second_shift).astype(BF16)
    hidden_linear = dot(second_normed, hidden_weight) + hidden_bias
    hidden_cdf, hidden_pdf = phi_parts(hidden_linear)
    hidden_active = (hidden_linear * hidden_cdf).astype(BF16)
    layer = mixed + dot(hidden_active, return_weight) + return_bias
    layer = jnp.where(alive, layer, 0.0).astype(BF16)

    slope = hidden_cdf + hidden_linear * hidden_pdf
    hidden_grad = (slope * dot_t(cot, return_weight)).astype(BF16)
    inner, second_gain_grad, second_shift_grad = norm_pull(
        xhat2, r2, second_gain, dot_t(hidden_grad, hidden_weight)
    )
    mixed_grad = cot.astype(F32) + inner
    branch_grad = mixed_grad.astype(BF16)

    attended_grad = jnp.pad(dot_t(branch_grad, output_weight).astype(BF16), ((0, R - T), (0, 0)))
    query_wide, key_grad, value_grad, layer_output = attn_bwd(
        query_ext,
        attended_grad,
        attended_wide,
        key_all,
        value_all,
        probs,
        layer.reshape(S, piece, D),
        scale,
        HEADS,
        block,
        F,
    )
    query_grad, key_grad, value_grad = query_wide[:T], key_grad[:T], value_grad[:T]
    normed_grad = (
        dot_t(query_grad, query_weight)
        + dot_t(key_grad, key_weight)
        + dot_t(value_grad, value_weight)
    )
    inner, first_gain_grad, first_shift_grad = norm_pull(xhat1, r1, first_gain, normed_grad)
    stream_grad = mixed_grad + inner
    conv_grad = (gelu_slope(conv_linear) * stream_grad).astype(BF16)
    conv_ext = with_halo(conv_grad)
    conv_after = jnp.roll(conv_ext, -1, axis=0)
    pair_grad = dot_t(conv_ext, reduce_matrix[D:])
    third_grad = dot_t(conv_after, reduce_matrix[:D])
    active_grad = pair_grad + jnp.concatenate([jnp.zeros_like(third_grad), third_grad], axis=1)
    stem_grad = jnp.where(valid, gelu_slope(stem_linear) * active_grad, 0.0).astype(BF16)
    own = stem_grad[:T]
    totals = column_total(own)
    stem_bias_grad = totals[:D] + totals[D:]
    pair_matrix_grad = outer(columns[:T], own)
    stem_matrix_grad = pair_matrix_grad[: 3 * mels, :D] + pair_matrix_grad[mels:, D:]
    mel_columns = dot_t(stem_grad, stem_pair)
    mel_pair = (
        mel_columns[:, mels : 3 * mels]
        + jnp.concatenate(
            [
                jnp.roll(mel_columns[:, 3 * mels :], 1, axis=0),
                jnp.roll(mel_columns[:, :mels], -1, axis=0),
            ],
            axis=1,
        )
    )[:T]
    sizes = (2, F // 2, F // 2, lax.axis_size("dp") // (F // 2))
    small = [stem_bias_grad, first_gain_grad, first_shift_grad, second_gain_grad, second_shift_grad]
    at = 3 * mels
    used = at + len(small) + -(at + len(small)) % 16
    short = jnp.pad(stem_matrix_grad, ((0, TILE - at), (0, 0)))
    place = lax.broadcasted_iota(jnp.int32, (TILE, 1), 0)
    for n, v in enumerate(small):
        short = jnp.where(place == at + n, v[None, :], short)
    FF = hidden_weight.shape[1]
    one = [(first_normed, D)]
    *terms, mel_slots = sum_everywhere(
        [
            ([(hidden_active, FF)], [(cot, D)]),
            ([(second_normed, D)], [(hidden_grad, FF)]),
            ([(attended, D)], [(branch_grad, D)]),
            ([(odd_active_before, D), (stem_active, 2 * D)], [(conv_grad, D)]),
            (one, [(query_wide, D)]),
            (one, [(key_grad, D)]),
            (one, [(value_grad, D)]),
        ],
        short.astype(BF16),
        used,
        mel_pair.reshape(S, piece, 2 * mels),
        F,
        sizes,
        0,
    )
    mel_gradient = mel_slots.reshape(S, piece_frames, mels)
    return_w, hidden_w, output_w, reduce_w, query_w, key_w, value_w, short = [
        v.astype(F32) for v in terms
    ]
    stem_w = short[: 3 * mels]
    small = [short[at + n] for n in range(len(small))]
    sums = short[used:]
    wide = FF // D
    return (
        layer_output,
        mel_gradient,
        stem_w.reshape(3, mels, D),
        small[0],
        reduce_w.reshape(3, D, D),
        sums[wide + 2],
        small[1],
        small[2],
        query_w,
        sums[wide + 3],
        key_w,
        value_w,
        sums[wide + 5],
        output_w,
        sums[wide + 1],
        small[3],
        small[4],
        hidden_w,
        sums[1 : wide + 1].reshape(FF),
        return_w,
        sums[0],
    )


def solution(mesh):
    cut = P("dp", "frame", None)
    return jax.shard_map(
        on_device,
        mesh=mesh,
        in_specs=(cut, P("dp")) + (P(),) * 19 + (cut,),
        out_specs=(cut, cut) + (P(),) * 19,
        check_vma=False,
    )
```

```python
import functools
import math

import jax
import jax.numpy as jnp
from jax import lax
from jax.experimental import pallas as pl
from jax.experimental.pallas import tpu as pltpu
from jax.sharding import PartitionSpec as P

HEADS = 8
EPS = 1e-05
F32 = jnp.float32
BF16 = jnp.bfloat16
PHI_SLOPE = 0.28
PHI_POLY = (
    0.1167294156016242,
    0.06622785593379492,
    0.27197610469464767,
    -0.24067367858721922,
    0.3920693507793772,
    -0.10632905941542621,
)


def phi_parts(v):
    size = jnp.abs(v)
    t = 1.0 / (1.0 + PHI_SLOPE * size)
    bell = jnp.exp(-0.5 * v * v)
    poly = PHI_POLY[5]
    for c in PHI_POLY[4::-1]:
        poly = poly * t + c
    tail = poly * t * bell
    cdf = jnp.where(v >= 0, 1.0 - tail, tail)
    return cdf, bell * (1.0 / math.sqrt(2.0 * math.pi))


def gelu(v):
    cdf, _ = phi_parts(v)
    return v * cdf


def gelu_slope(v):
    cdf, pdf = phi_parts(v)
    return cdf + v * pdf


def dot(left, right):
    return jnp.dot(left, right, preferred_element_type=F32)


def dot_t(left, right):
    return lax.dot_general(left, right, (((1,), (1,)), ((), ())), preferred_element_type=F32)


def outer(left, right):
    return lax.dot_general(left, right, (((0,), (0,)), ((), ())), preferred_element_type=F32)


def column_total(x):
    return jnp.sum(x.astype(F32), axis=0)


def norm_parts(x):
    centred = x - jnp.mean(x, axis=-1, keepdims=True)
    r = lax.rsqrt(jnp.mean(centred * centred, axis=-1, keepdims=True) + EPS)
    return centred * r, r


def norm_pull(xhat, r, gain, dy):
    dh = dy * gain
    inner = r * (
        dh
        - jnp.mean(dh, axis=-1, keepdims=True)
        - xhat * jnp.mean(dh * xhat, axis=-1, keepdims=True)
    )
    return inner, column_total(dy * xhat), column_total(dy)


def positions_of(first, count, width):
    half = width // 2
    step = math.log(10000.0) / (half - 1)
    rate = jnp.exp(-step * jnp.arange(half, dtype=F32))[None, :]
    fine = math.gcd(count, 16)
    coarse = count // fine
    a = (first + fine * jnp.arange(coarse, dtype=jnp.int32)).astype(F32)[:, None] * rate
    b = jnp.arange(fine, dtype=jnp.int32).astype(F32)[:, None] * rate
    sa, ca = jnp.sin(a)[:, None, :], jnp.cos(a)[:, None, :]
    sb, cb = jnp.sin(b)[None, :, :], jnp.cos(b)[None, :, :]
    both = jnp.concatenate([sa * cb + ca * sb, ca * cb - sa * sb], axis=2)
    return both.reshape(count, width)


def half_mask(shape, h, hd):
    lane = lax.broadcasted_iota(jnp.int32, shape, 1)
    return (lane >= h*hd) & (lane < (h+1)*hd)

MESH = pl.DeviceIdType.MESH


def group_peer(G, o):
    fr = lax.axis_index("frame")
    return (lax.axis_index("dp"), fr // G * G + lax.rem(lax.rem(fr, G) + o, G))


def greet(F):
    barrier = pltpu.get_barrier_semaphore()
    for o in range(1, F):
        pl.semaphore_signal(barrier, inc=1, device_id=group_peer(F, o), device_id_type=MESH)


def meet(F):
    greet(F)
    pl.semaphore_wait(pltpu.get_barrier_semaphore(), F - 1)


class Move:
    def __init__(self, gather, F, src, dst, sems):
        self.src, self.dst = src, dst
        self.send, self.recv, self.own = sems
        self.S = src.shape[0]
        S, G = self.S, F // src.shape[0]
        self.dp, self.fr = lax.axis_index("dp"), lax.axis_index("frame")
        over = [a * G + self.fr // S for a in range(S)]
        back = [lax.rem(self.fr, G) * S + a for a in range(S)]
        self.to, self.sender = (over, back) if gather else (back, over)
        self.place = lax.rem(self.fr, S) if gather else self.fr // G

    def far(self, a):
        return pltpu.make_async_remote_copy(
            src_ref=self.src.at[a],
            dst_ref=self.dst.at[self.place],
            send_sem=self.send.at[a],
            recv_sem=self.recv.at[self.place],
            device_id=(self.dp, self.to[a]),
            device_id_type=MESH,
        )

    def near(self, a):
        return pltpu.make_async_copy(self.src.at[a], self.dst.at[self.place], self.own.at[a])

    def start(self):
        for a in range(self.S):

            @pl.when(self.to[a] != self.fr)
            def _():
                self.far(a).start()

            @pl.when(self.to[a] == self.fr)
            def _():
                self.near(a).start()

    def wait(self):
        for a in range(self.S):

            @pl.when(self.to[a] != self.fr)
            def _():
                self.far(a).wait_send()

            @pl.when(self.to[a] == self.fr)
            def _():
                self.near(a).wait()

            @pl.when(self.sender[a] != self.fr)
            def _():
                landed = self.dst.at[a]
                pltpu.make_async_copy(landed, landed, self.recv.at[a]).wait()


def move_sems(S):
    return [pltpu.SemaphoreType.DMA((S,))] * 3


def lanes_of(pair):
    return pl.ds(pl.multiple_of(pair * 128, 128), 128)


def fwd_kernel(
    scale,
    hd,
    F,
    G,
    T,
    pairs,
    q_ref,
    k_own,
    v_own,
    c_ref,
    p_ref,
    o_ref,
    k_all,
    v_all,
    d_ref,
    s_ref,
    k_buf,
    v_buf,
    send_sem,
    recv_sem,
    own_sem,
    out_sem,
    *sems,
):
    per = 128 // hd
    pair, i = pl.program_id(0), pl.program_id(1)
    rows = k_own.shape[0]
    both = ((k_own, k_buf), (v_own, v_buf))
    kept = ((k_buf, k_all), (v_buf, v_all))

    def own_copy(n, p):
        src, dst = both[n]
        return pltpu.make_async_copy(
            src.at[:, lanes_of(p)], dst.at[pl.ds(0, rows), lanes_of(p)], own_sem.at[n, p]
        )

    def keep(n, p):
        src, dst = kept[n]
        return pltpu.make_async_copy(
            src.at[:, lanes_of(p)], dst.at[:, lanes_of(p)], out_sem.at[n, p]
        )

    def copy_to(n, p, o):
        src, dst = both[n]
        return pltpu.make_async_remote_copy(
            src_ref=src.at[:, lanes_of(p)],
            dst_ref=dst.at[pl.ds((G - o) * rows, rows), lanes_of(p)],
            send_sem=send_sem.at[n, p, o - 1],
            recv_sem=recv_sem.at[n, p, o - 1],
            device_id=group_peer(G, o),
            device_id_type=MESH,
        )

    @pl.when((pair == 0) & (i == 0))
    def _():
        for p in range(pairs):
            for n in range(2):
                own_copy(n, p).start()
        meet(F)
        for p in range(pairs):
            for n in range(2):
                for o in range(1, G):
                    copy_to(n, p, o).start()
        Move(True, F, c_ref, d_ref, sems).start()

    @pl.when(i == 0)
    def _():
        for n in range(2):
            own_copy(n, pair).wait()
            for o in range(1, G):
                copy_to(n, pair, o).wait_recv()
            keep(n, pair).start()

    k = k_buf[:, lanes_of(pair)]
    vt = v_buf[:, lanes_of(pair)].T
    outs = []
    for h in range(per):
        q = q_ref[...]
        q = jnp.where(half_mask(q.shape, h, hd), q, jnp.zeros_like(q))
        s_ref[h] = lax.dot_general(k, q, (((1,), (1,)), ((), ())), preferred_element_type=F32)
    for h in range(per):
        s = s_ref[h]
        if rows != T:
            at = lax.rem(lax.broadcasted_iota(jnp.int32, s.shape, 0), rows)
            s = jnp.where(at < T, s, -1e30)
        m = jnp.max(s, axis=0, keepdims=True)
        e = jnp.exp((s - m) * scale)
        l = jnp.sum(e, axis=0, keepdims=True)
        p = (e * (1.0 / l)).astype(BF16)
        p_ref[h] = p
        outs.append(jnp.dot(vt[h * hd : (h + 1) * hd], p, preferred_element_type=F32))
    o_ref[...] = jnp.concatenate(outs, axis=0).T

    @pl.when((pair == pairs - 1) & (i == pl.num_programs(1) - 1))
    def _():
        for p in range(pairs):
            for n in range(2):
                keep(n, p).wait()
                for o in range(1, G):
                    copy_to(n, p, o).wait_send()
        Move(True, F, c_ref, d_ref, sems).wait()


def attn_fwd(q, k, v, slots, scale, heads, QB, F, T):
    G = F // slots.shape[0]
    R, D = q.shape
    N = k.shape[0] * G
    hd = D // heads
    per = 128 // hd
    pairs = D // 128
    far = pl.BlockSpec(memory_space=pl.ANY)
    sems = pltpu.SemaphoreType.DMA((2, pairs, G - 1))
    return pl.pallas_call(
        functools.partial(fwd_kernel, scale, hd, F, G, T, pairs),
        grid=(pairs, R // QB),
        in_specs=[pl.BlockSpec((QB, 128), lambda p, i: (i, p)), far, far, far],
        out_specs=[
            pl.BlockSpec((per, N, QB), lambda p, i: (p, 0, i)),
            pl.BlockSpec((QB, 128), lambda p, i: (i, p)),
            far,
            far,
            far,
        ],
        out_shape=[
            jax.ShapeDtypeStruct((heads, N, R), BF16),
            jax.ShapeDtypeStruct((R, D), F32),
            jax.ShapeDtypeStruct((N, D), BF16),
            jax.ShapeDtypeStruct((N, D), BF16),
            jax.ShapeDtypeStruct(slots.shape, slots.dtype),
        ],
        scratch_shapes=[
            pltpu.VMEM((per, N, QB), F32),
            pltpu.VMEM((N, D), BF16),
            pltpu.VMEM((N, D), BF16),
            sems,
            sems,
            pltpu.SemaphoreType.DMA((2, pairs)),
            pltpu.SemaphoreType.DMA((2, pairs)),
        ]
        + move_sems(slots.shape[0]),
        compiler_params=pltpu.CompilerParams(
            collective_id=1, has_side_effects=True, vmem_limit_bytes=60 << 20
        ),
    )(q, k, v, slots)


def bwd_kernel(
    scale,
    hd,
    F,
    G,
    pairs,
    q_ref,
    do_ref,
    o_ref,
    k_ref,
    v_ref,
    p_ref,
    y_ref,
    dq_ref,
    dk_ref,
    dv_ref,
    z_ref,
    dp_ref,
    kt_ref,
    acc_ref,
    got_ref,
    send_sem,
    recv_sem,
    *sems,
):
    per = 128 // hd
    pair, i = pl.program_id(0), pl.program_id(1)
    slot = lax.rem(pair, 2)
    rows = dk_ref.shape[0]

    def copy_to(n, p, o):
        return pltpu.make_async_remote_copy(
            src_ref=acc_ref.at[lax.rem(p, 2), n, pl.ds(o * rows, rows)],
            dst_ref=got_ref.at[p, n, o - 1],
            send_sem=send_sem.at[n, p, o - 1],
            recv_sem=recv_sem.at[n, p, o - 1],
            device_id=group_peer(G, o),
            device_id_type=MESH,
        )

    every = [(n, o) for n in range(2) for o in range(1, G)]

    @pl.when((pair == 0) & (i == 0))
    def _():
        meet(F)
        Move(False, F, y_ref, z_ref, sems).start()

    @pl.when((pair >= 2) & (i == 0))
    def _():
        for n, o in every:
            copy_to(n, pair - 2, o).wait_send()

    @pl.when(i == 0)
    def _():
        kt_ref[...] = k_ref[...].T
        acc_ref[slot] = jnp.zeros(acc_ref.shape[1:], F32)

    do = do_ref[...]
    q = q_ref[...]
    v = v_ref[...]
    prod = (do.astype(F32) * o_ref[...]).T
    for h in range(per):
        doh = jnp.where(half_mask(do.shape, h, hd), do, jnp.zeros_like(do))
        dp_ref[h] = lax.dot_general(v, doh, (((1,), (1,)), ((), ())), preferred_element_type=F32)
    dqs = []
    for h in range(per):
        doh = jnp.where(half_mask(do.shape, h, hd), do, jnp.zeros_like(do))
        qh = jnp.where(half_mask(q.shape, h, hd), q, jnp.zeros_like(q))
        delta = jnp.sum(prod[h * hd : (h + 1) * hd], axis=0, keepdims=True)
        p = p_ref[h]
        ds = (p.astype(F32) * (dp_ref[h] - delta)).astype(BF16)
        acc_ref[slot, 1] += jnp.dot(p, doh, preferred_element_type=F32)
        acc_ref[slot, 0] += jnp.dot(ds, qh, preferred_element_type=F32)
        dqs.append(jnp.dot(kt_ref[h * hd : (h + 1) * hd], ds, preferred_element_type=F32))
    dq_ref[...] = (jnp.concatenate(dqs, axis=0) * scale).T.astype(BF16)

    def finish(p):
        for n, o in every:
            copy_to(n, p, o).wait_recv()
        for n, out, factor in ((0, dk_ref, scale), (1, dv_ref, 1.0)):
            total = acc_ref[lax.rem(p, 2), n, pl.ds(0, rows)]
            for o in range(1, G):
                total = total + got_ref[p, n, o - 1]
            out[:, lanes_of(p)] = (total * factor).astype(BF16)

    ends = i == pl.num_programs(1) - 1

    @pl.when(ends & (pair >= 1))
    def _():
        finish(pair - 1)

    @pl.when(ends)
    def _():
        for n, o in every:
            copy_to(n, pair, o).start()

    @pl.when(ends & (pair == pairs - 1))
    def _():
        finish(pair)
        for p in range(max(pairs - 2, 0), pairs):
            for n, o in every:
                copy_to(n, p, o).wait_send()
        Move(False, F, y_ref, z_ref, sems).wait()


def attn_bwd(q, do, o, k, v, p, pieces, scale, heads, QB, F):
    G = F // pieces.shape[0]
    far = pl.BlockSpec(memory_space=pl.ANY)
    R, D = q.shape
    N = k.shape[0]
    hd = D // heads
    per = 128 // hd
    pairs = D // 128
    row = pl.BlockSpec((QB, 128), lambda p, i: (i, p))
    key = pl.BlockSpec((N, 128), lambda p, i: (0, p))
    near = pl.BlockSpec(memory_space=pltpu.VMEM)
    sems = pltpu.SemaphoreType.DMA((2, pairs, G - 1))
    own = jax.ShapeDtypeStruct((N // G, D), BF16)
    return pl.pallas_call(
        functools.partial(bwd_kernel, scale, hd, F, G, pairs),
        grid=(pairs, R // QB),
        in_specs=[row, row, row, key, key, pl.BlockSpec((per, N, QB), lambda p, i: (p, 0, i)), far],
        out_specs=[row, near, near, far],
        out_shape=[
            jax.ShapeDtypeStruct((R, D), BF16),
            own,
            own,
            jax.ShapeDtypeStruct(pieces.shape, pieces.dtype),
        ],
        scratch_shapes=[
            pltpu.VMEM((per, N, QB), F32),
            pltpu.VMEM((128, N), BF16),
            pltpu.VMEM((2, 2, N, 128), F32),
            pltpu.VMEM((pairs, 2, G - 1, N // G, 128), F32),
            sems,
            sems,
        ]
        + move_sems(pieces.shape[0]),
        compiler_params=pltpu.CompilerParams(
            collective_id=2, has_side_effects=True, vmem_limit_bytes=60 << 20
        ),
    )(q, do, o, k, v, p, pieces)


TILE = 512
LAG = 3
AHEAD = 3


def pick(c, values):
    out = values[0]
    for n in range(1, len(values)):
        if values[n] != values[n - 1]:
            out = jnp.where(c >= n, values[n], out)
    return out


class Rest:
    FIRST = 2

    def __init__(self, G, T, taps, m_ref, t_ref, w_ref, data, scratch, sems):
        self.m, self.t, self.w = m_ref, t_ref, w_ref
        self.data = data
        self.ext, self.edge, self.halo, self.sg, self.y0, self.y1, self.y2 = scratch
        self.send, self.recv = sems
        self.G, self.T, self.taps = G, T, taps
        self.R = self.sg.shape[0]
        self.row = lax.rem(lax.axis_index("frame"), G)
        self.size = 256 if self.R % 256 == 0 else 128
        self.token_blocks = [(a, min(a + 256, T)) for a in range(0, T, 256)]
        self.edges_at = self.FIRST + len(self.token_blocks)
        self.halo_at = self.edges_at + 2
        self.stem_at = self.halo_at + 1
        self.mel_at = self.stem_at + self.R // self.size
        self.weights_at = self.mel_at + 1
        self.halo[...] = jnp.zeros_like(self.halo)

    def due(self, name):
        if name in ("reduce", "stem_linear", "stem_taps"):
            return self.stem_at
        if name in ("columns", "second"):
            return self.weights_at
        return self.FIRST

    def tokens(self, n):
        a, b = self.token_blocks[n]
        q, k, v, conv, base = self.taps
        data, rows = self.data, pl.ds(a, b - a)
        dy = (
            dot_t(self.m[q, rows], data["query"][...])
            + dot_t(self.m[k, rows], data["key"][...])
            + dot_t(self.m[v, rows], data["value"][...])
        )
        xhat = data["xhat"][rows]
        r = data["r"][rows][:, :1]
        dh = dy * data["gain"][...][:1]
        inner = r * (
            dh
            - jnp.mean(dh, axis=-1, keepdims=True)
            - xhat * jnp.mean(dh * xhat, axis=-1, keepdims=True)
        )
        self.t[base + 1 : base + 2] += jnp.sum(dy * xhat, axis=0, keepdims=True)
        self.t[base + 2 : base + 3] += jnp.sum(dy, axis=0, keepdims=True)
        grad = gelu_slope(data["conv_linear"][rows]) * (data["mixed"][rows] + inner)
        grad = grad.astype(BF16)
        self.m[conv, rows] = grad
        self.ext[rows] = grad
        if n == 0:
            self.edge[1] = grad[:16]
            self.ext[pl.ds(self.R, 16)] = grad[:16]
        if b == self.T:
            self.edge[0] = grad[b - a - 16 :]

    def edge_copy(self, n):
        return pltpu.make_async_remote_copy(
            src_ref=self.edge.at[n],
            dst_ref=self.halo.at[n],
            send_sem=self.send.at[n],
            recv_sem=self.recv.at[n],
            device_id=group_peer(self.G, 1 if n == 0 else self.G - 1),
            device_id_type=MESH,
        )

    def has(self, n):
        return self.row < self.G - 1 if n == 0 else self.row > 0

    def send_edges(self):
        for n in range(2):

            @pl.when(self.has(n))
            def _():
                self.edge_copy(n).start()

    def fill_halo(self):
        for n in range(2):

            @pl.when(self.has(1 - n))
            def _():
                landed = self.halo.at[n]
                pltpu.make_async_copy(landed, landed, self.recv.at[n]).wait()

        at = self.T // 16 * 16
        rows = pl.ds(at, self.R - at)
        own = self.ext[rows].astype(F32)
        place = lax.broadcasted_iota(jnp.int32, own.shape, 0) + at
        before = self.halo[0].astype(F32)[15:16]
        after = self.halo[1].astype(F32)[:1]
        own = jnp.where(place < self.T, own, 0.0)
        own = jnp.where(place == self.T, after, own)
        own = jnp.where(place == self.R - 1, before, own)
        self.ext[rows] = own.astype(BF16)

    def stem(self, n):
        data, a = self.data, n * self.size
        D = self.ext.shape[1]
        rows = pl.ds(a, self.size)
        pair = dot_t(self.ext[rows], data["reduce"][pl.ds(D, 2 * D)])
        third = dot_t(self.ext[pl.ds(a, self.size + 16)], data["reduce"][pl.ds(0, D)])
        third = third[1 : self.size + 1]
        active = jnp.concatenate([pair[:, :D], pair[:, D:] + third], axis=1)
        place = lax.broadcasted_iota(jnp.int32, active.shape, 0) + a
        high = self.T + jnp.where(self.row < self.G - 1, 1, 0)
        low = self.R - jnp.where(self.row > 0, 1, 0)
        grad = gelu_slope(data["stem_linear"][rows]) * active
        grad = jnp.where((place < high) | (place >= low), grad, 0.0).astype(BF16)
        self.sg[rows] = grad
        self.y0[rows] = dot_t(grad, data["stem_taps"][0])
        y1 = dot_t(grad, data["stem_taps"][1])
        self.y1[pl.ds(a + 8, self.size)] = y1
        if a + self.size == self.R:
            self.y1[pl.ds(0, 8)] = y1[self.size - 8 :]
        self.y2[rows] = dot_t(grad, data["stem_taps"][2])

    def mel(self, out):
        T = self.T
        total = self.y0[pl.ds(0, T)] + self.y1[pl.ds(7, T)] + self.y2[pl.ds(1, T)]
        n = out.shape[1]
        for j in range(out.shape[0]):
            out[j] = total[j * n : (j + 1) * n]

    def weights(self):
        base = self.taps[-1]
        D = self.ext.shape[1]
        own = self.sg[pl.ds(0, self.T)]
        wide = outer(self.data["columns"][pl.ds(0, self.T)], own)
        mels = wide.shape[0] // 4
        sums = dot(jnp.ones((16, self.T), BF16), own)[:1]
        self.w[self.w.shape[0] - 1, pl.ds(0, 3 * mels)] = (
            wide[: 3 * mels, :D] + wide[mels:, D:]
        ).astype(BF16)
        self.t[base : base + 1] = sums[:, :D] + sums[:, D:]
        self.t[base + 3 : base + 5] = self.data["second"][...][:2]

    def step(self, t, out):
        todo = [(self.FIRST + n, functools.partial(self.tokens, n)) for n in range(len(self.token_blocks))]
        todo.append((self.edges_at, self.send_edges))
        todo.append((self.halo_at, self.fill_halo))
        todo += [
            (self.stem_at + n, functools.partial(self.stem, n)) for n in range(self.R // self.size)
        ]
        todo.append((self.mel_at, functools.partial(self.mel, out)))
        todo.append((self.weights_at, self.weights))
        for at, work in todo:
            pl.when(t == at)(work)

    def drain(self):
        for n in range(2):

            @pl.when(self.has(n))
            def _():
                self.edge_copy(n).wait_send()


REST = (
    "query",
    "key",
    "value",
    "xhat",
    "r",
    "gain",
    "mixed",
    "conv_linear",
    "reduce",
    "stem_linear",
    "stem_taps",
    "columns",
    "second",
)


def sum_kernel(sizes, F, used, plan, *refs):
    places, left_at, right_at, lefts, rights, n_in, n_out, taps, T = plan
    extra = len(REST)
    in_refs, rest_refs = refs[: n_in - extra], refs[n_in - extra : n_in]
    g_refs, slot_ref = refs[n_in : n_in + n_out - 1], refs[n_in + n_out - 1]
    refs = refs[n_in + n_out :]
    l_ref, m_ref, t_ref, w_ref, s_ref, r0, r1, r2, r3 = refs[:9]
    kept, work = refs[9 : 9 + extra], refs[9 + extra : 16 + extra]
    piece_ref, send_sem, recv_sem, load_sem, out_sem, edge_send, edge_recv, *sems = refs[16 + extra :]
    t_ref[...] = jnp.zeros_like(t_ref)
    w_ref[len(places) - 1] = jnp.zeros(w_ref.shape[1:], BF16)
    G = F // slot_ref.shape[0]
    rest = Rest(
        G, T, taps, m_ref, t_ref, w_ref, dict(zip(REST, kept)), work, (edge_send, edge_recv)
    )
    recv = (r0, r1, r2, r3)
    chunks = len(places)
    Y = sizes[2]
    dp = lax.axis_index("dp")
    fr = lax.axis_index("frame")
    z = dp // Y
    y = lax.rem(dp, Y)
    x = fr // 2
    core = lax.rem(fr, 2)
    first = core == 0
    me = (core, jnp.where(first, x, y), jnp.where(first, y, x), z)

    loads, due = [], []
    for buf, sources, at in ((l_ref, lefts, left_at), (m_ref, rights, right_at)):
        for n, (which, col) in enumerate(sources):
            if which is None:
                continue
            src = in_refs[which].at[pl.ds(0, T), pl.ds(col, TILE)]
            loads.append(pltpu.make_async_copy(src, buf.at[n], load_sem.at[len(loads)]))
            first_use = at.index(n)
            due.append(min(first_use, rest.FIRST) if at is right_at and n in taps[:3] else first_use)
    for name, src, dst in zip(REST, rest_refs, kept):
        loads.append(pltpu.make_async_copy(src, dst, load_sem.at[len(loads)]))
        due.append(rest.due(name))
    for n in sorted(range(len(loads)), key=lambda n: (due[n], n)):
        loads[n].start()

    def device(kind, p):
        if kind == 0:
            return (dp, x * 2 + p)
        if kind == 3:
            return (p * Y + y, fr)
        along_x = first if kind == 1 else jnp.logical_not(first)
        return (z * Y + jnp.where(along_x, y, p), jnp.where(along_x, p, x) * 2 + core)

    def peer(k, o):
        return lax.rem(me[k] + o, sizes[k])

    pairs = [(k, o) for k in range(4) for o in range(1, sizes[k])]
    barrier = pltpu.get_barrier_semaphore()
    for k, o in pairs:
        pl.semaphore_signal(barrier, inc=1, device_id=device(k, peer(k, o)), device_id_type=MESH)
    greet(F)
    pl.semaphore_wait(barrier, len(pairs) + F - 1)
    move = Move(False, F, piece_ref, slot_ref, sems)

    cut = [TILE]
    for k in range(4):
        cut.append(cut[-1] // sizes[k])
    split = cut[4] % 16 == 0
    if not split:
        cut[4] = cut[3]

    def start_of(level):
        at = 0
        for k in range(level):
            if k < 3 or split:
                at = at + me[k] * cut[k + 1]
        return pl.multiple_of(at, 16) if level else 0

    def scatter_copy(c, k, o):
        p = peer(k, o)
        at = start_of(k)
        if k < 3 or split:
            at = pl.multiple_of(at + p * cut[k + 1], 16)
        return pltpu.make_async_remote_copy(
            src_ref=w_ref.at[c, pl.ds(at, cut[k + 1])],
            dst_ref=recv[k].at[c, o - 1],
            send_sem=send_sem.at[c, k, o - 1],
            recv_sem=recv_sem.at[c, k, o - 1],
            device_id=device(k, p),
            device_id_type=MESH,
        )

    def gather_copy(c, k, o):
        here = s_ref.at[c, pl.ds(start_of(k + 1), cut[k + 1])]
        return pltpu.make_async_remote_copy(
            src_ref=here,
            dst_ref=here,
            send_sem=send_sem.at[c, 4 + k, o - 1],
            recv_sem=recv_sem.at[c, 4 + k, o - 1],
            device_id=device(k, peer(k, o)),
            device_id_type=MESH,
        )

    def out_copy(c):
        which, row, col = places[c]
        dst = g_refs[which].at[pl.ds(row, TILE), pl.ds(col, TILE)]
        return pltpu.make_async_copy(s_ref.at[c], dst, out_sem.at[c])

    def add(c, k):
        at = start_of(k + 1)
        dst = w_ref if k < 3 else s_ref
        step = math.gcd(cut[k + 1], 64)

        def body(i, _):
            r = pl.multiple_of(at + i * step, 16)
            total = w_ref[c, pl.ds(r, step)].astype(F32)
            for o in range(1, sizes[k]):
                total = total + recv[k][
                    c, o - 1, pl.ds(pl.multiple_of(i * step, 16), step)
                ].astype(F32)
            dst[c, pl.ds(r, step)] = total.astype(BF16)
            return 0

        lax.fori_loop(0, cut[k + 1] // step, body, 0)

    stages = [("s", k) for k in range(4)] + [("g", k) for k in (3, 2, 1, 0) if k < 3 or split]
    copies = {"s": scatter_copy, "g": gather_copy}

    def finish(c, n):
        kind, k = stages[n]
        for o in range(1, sizes[k]):
            copies[kind](c, k, o).wait_recv()
        if kind == "s":
            add(c, k)
        if n + 1 < len(stages):
            kind, k = stages[n + 1]
            for o in range(1, sizes[k]):
                copies[kind](c, k, o).start()

    last = LAG * (len(stages) - 1) + AHEAD

    def turn(t, _):
        for n in range(len(loads)):

            @pl.when(t == due[n])
            def _():
                loads[n].wait()

        @pl.when(t < chunks - 1)
        def _():
            left = l_ref[pick(t, left_at)]
            right = m_ref[pick(t, right_at)]
            w_ref[t] = outer(left, right).astype(BF16)
            ones = jnp.ones((16, T), BF16)
            t_ref[pl.ds(pick(t, right_at), 1)] = dot(ones, right)[:1]

        @pl.when(t == rest.weights_at)
        def _():
            move.start()

        rest.step(t, piece_ref)

        @pl.when(t == chunks - 1)
        def _():
            w_ref[chunks - 1, pl.ds(used, t_ref.shape[0])] = t_ref[...].astype(BF16)

        @pl.when((t >= 1) & (t <= chunks))
        def _():
            for o in range(1, sizes[0]):
                scatter_copy(t - 1, 0, o).start()

        for n in range(len(stages) - 1, -1, -1):
            c = t - AHEAD - LAG * n

            @pl.when((c >= 0) & (c < chunks))
            def _():
                finish(c, n)

        for c in range(chunks):

            @pl.when(t == c + last)
            def _():
                out_copy(c).start()

        return 0

    lax.fori_loop(0, chunks + last, turn, 0)

    def drain(c, _):
        for kind, k in stages:
            for o in range(1, sizes[k]):
                copies[kind](c, k, o).wait_send()
        return 0

    lax.fori_loop(0, chunks, drain, 0)
    move.wait()
    rest.drain()
    for c in range(chunks):
        out_copy(c).wait()


def sum_everywhere(products, rest, taps, used, S, F, sizes, cid):
    arrays, lefts, rights = [], [], []
    places, left_at, right_at, shapes = [], [], [], []

    def slots_of(pieces, slots):
        found = []
        for array, width in pieces:
            which = None
            if array is not None:
                which = next((n for n, a in enumerate(arrays) if a is array), None)
                if which is None:
                    which = len(arrays)
                    arrays.append(array)
            for col in range(0, width, TILE):
                if (which, col) not in slots:
                    slots.append((which, col))
                found.append(slots.index((which, col)))
        return found

    for n, (left, right) in enumerate(products):
        a, b = slots_of(left, lefts), slots_of(right, rights)
        shapes.append((len(a) * TILE, len(b) * TILE))
        for i, u in enumerate(a):
            for j, v in enumerate(b):
                places.append((n, i * TILE, j * TILE))
                left_at.append(u)
                right_at.append(v)
    places.append((len(products), 0, 0))
    shapes.append((TILE, TILE))
    T = min(a.shape[0] for a in arrays)
    R = rest["stem_linear"].shape[0]
    mels = rest["columns"].shape[1] // 4
    chunks = len(places)
    cut = [TILE]
    for n in sizes:
        cut.append(cut[-1] // n)
    if cut[4] % 16:
        cut[4] = cut[3]
    most = max(sizes) - 1
    spec = pl.BlockSpec(memory_space=pl.ANY)
    sums = len(rights) + 5
    sums += -sums % 16
    slots = jax.ShapeDtypeStruct((S, T // S, 2 * mels), F32)
    taps = tuple(right_at[n] for n in taps) + (len(rights),)
    plan = (
        places,
        left_at,
        right_at,
        lefts,
        rights,
        len(arrays) + len(REST),
        len(shapes) + 1,
        taps,
        T,
    )
    return pl.pallas_call(
        functools.partial(sum_kernel, sizes, F, used, plan),
        in_specs=[spec] * (len(arrays) + len(REST)),
        out_specs=[spec] * (len(shapes) + 1),
        out_shape=[jax.ShapeDtypeStruct(v, BF16) for v in shapes] + [slots],
        scratch_shapes=[
            pltpu.VMEM((len(lefts), T, TILE), BF16),
            pltpu.VMEM((len(rights), T, TILE), BF16),
            pltpu.VMEM((sums, TILE), F32),
        ]
        + [pltpu.VMEM((chunks, TILE, TILE), BF16)] * 2
        + [pltpu.VMEM((chunks, sizes[k] - 1, cut[k + 1], TILE), BF16) for k in range(4)]
        + [pltpu.VMEM(rest[name].shape, rest[name].dtype) for name in REST]
        + [
            pltpu.VMEM((R + 16, TILE), BF16),
            pltpu.VMEM((2, 16, TILE), BF16),
            pltpu.VMEM((2, 16, TILE), BF16),
            pltpu.VMEM((R, 2 * TILE), BF16),
            pltpu.VMEM((R, 2 * mels), F32),
            pltpu.VMEM((R + 8, 2 * mels), F32),
            pltpu.VMEM((R, 2 * mels), F32),
            pltpu.VMEM(slots.shape, F32),
        ]
        + [
            pltpu.SemaphoreType.DMA((chunks, 8, most)),
            pltpu.SemaphoreType.DMA((chunks, 8, most)),
            pltpu.SemaphoreType.DMA((len(lefts) + len(rights) + len(REST),)),
            pltpu.SemaphoreType.DMA((chunks,)),
            pltpu.SemaphoreType.DMA((2,)),
            pltpu.SemaphoreType.DMA((2,)),
        ]
        + move_sems(S),
        compiler_params=pltpu.CompilerParams(
            collective_id=cid, has_side_effects=True, vmem_limit_bytes=67043328
        ),
    )(*arrays, *[rest[name] for name in REST])


def on_device(
    mel_frames,
    window_count,
    stem_weight,
    stem_bias,
    reduce_weight,
    reduce_bias,
    first_gain,
    first_shift,
    query_weight,
    query_bias,
    key_weight,
    value_weight,
    value_bias,
    output_weight,
    output_bias,
    second_gain,
    second_shift,
    hidden_weight,
    hidden_bias,
    return_weight,
    return_bias,
    cotangent,
):
    S, piece_frames, mels = mel_frames.shape
    piece = cotangent.shape[1]
    D = stem_weight.shape[2]
    hd = D // HEADS
    scale = hd ** (-0.5)
    F = lax.axis_size("frame")
    G = F // S
    T = S * piece
    R = -(-(T + 2) // 128) * 128
    f = lax.axis_index("frame")
    s = f // G
    r = f % G
    alive = s < window_count[0]

    def gather_window(x):
        parts = []
        out = jnp.zeros((S * x.shape[1], x.shape[2]), x.dtype)
        for t in range(S):
            part = lax.dynamic_index_in_dim(x, (f + t) % S, 0, keepdims=False)
            perm = [(p, ((p % S + t) % S) * G + p // S) for p in range(F)]
            got = lax.ppermute(part, "frame", perm)
            j = (s - t) % S
            out = lax.dynamic_update_slice(out, got, (j * x.shape[1], 0))
        return out

    down = [(i, i + 1) for i in range(F) if (i + 1) % G != 0]
    up = [(i + 1, i) for i in range(F) if (i + 1) % G != 0]

    def with_halo(x):
        before = lax.ppermute(x[T - 1 : T], "frame", down)
        after = lax.ppermute(x[0:1], "frame", up)
        gap = jnp.zeros((R - T - 2, x.shape[1]), x.dtype)
        return jnp.concatenate([x, after, gap, before], axis=0)

    mel = gather_window(mel_frames.reshape(S, piece, 2 * mels))
    mel = with_halo(mel)
    odd_before = jnp.roll(mel[:, mels:], 1, axis=0)
    even_after = jnp.roll(mel[:, :mels], -1, axis=0)
    columns = jnp.concatenate([odd_before, mel, even_after], axis=1)
    stem_matrix = stem_weight.reshape(3 * mels, D)
    gap = jnp.zeros((mels, D), BF16)
    stem_pair = jnp.concatenate(
        [
            jnp.concatenate([stem_matrix, gap], axis=0),
            jnp.concatenate([gap, stem_matrix], axis=0),
        ],
        axis=1,
    )
    stem_bias2 = jnp.concatenate([stem_bias, stem_bias])
    stem_linear = dot(columns, stem_pair) + stem_bias2
    row = lax.broadcasted_iota(jnp.int32, (R, 1), 0)
    valid = (row < T) | ((row == T) & (r < G - 1)) | ((row == R - 1) & (r > 0))
    stem_active = jnp.where(valid, gelu(stem_linear), 0.0).astype(BF16)

    odd_active_before = jnp.roll(stem_active[:, D:], 1, axis=0)[:T]
    conv_columns = jnp.concatenate([odd_active_before, stem_active[:T]], axis=1)
    reduce_matrix = reduce_weight.reshape(3 * D, D)
    conv_linear = dot(conv_columns, reduce_matrix) + reduce_bias
    stream = gelu(conv_linear) + positions_of(r * T, T, D)
    xhat1, r1 = norm_parts(stream)
    first_normed = (xhat1 * first_gain + first_shift).astype(BF16)
    query = (dot(first_normed, query_weight) + query_bias).astype(BF16)
    key = dot(first_normed, key_weight).astype(BF16)
    value = (dot(first_normed, value_weight) + value_bias).astype(BF16)
    key = jnp.pad(key, ((0, -T % 16), (0, 0)))
    value = jnp.pad(value, ((0, -T % 16), (0, 0)))
    query_ext = jnp.pad(query, ((0, R - T), (0, 0)))
    block = 256 if R % 256 == 0 else 128
    probs, attended_wide, key_all, value_all, cot = attn_fwd(
        query_ext, key, value, cotangent, scale, HEADS, block, F, T
    )
    cot = cot.reshape(T, D)
    cot = jnp.where(alive, cot, jnp.zeros_like(cot))
    attended = attended_wide[:T].astype(BF16)
    mixed = stream + dot(attended, output_weight) + output_bias
    xhat2, r2 = norm_parts(mixed)
    second_normed = (xhat2 * second_gain + second_shift).astype(BF16)
    hidden_linear = dot(second_normed, hidden_weight) + hidden_bias
    hidden_cdf, hidden_pdf = phi_parts(hidden_linear)
    hidden_active = (hidden_linear * hidden_cdf).astype(BF16)
    layer = mixed + dot(hidden_active, return_weight) + return_bias
    layer = jnp.where(alive, layer, 0.0).astype(BF16)

    slope = hidden_cdf + hidden_linear * hidden_pdf
    hidden_grad = (slope * dot_t(cot, return_weight)).astype(BF16)
    inner, second_gain_grad, second_shift_grad = norm_pull(
        xhat2, r2, second_gain, dot_t(hidden_grad, hidden_weight)
    )
    mixed_grad = cot.astype(F32) + inner
    branch_grad = mixed_grad.astype(BF16)

    attended_grad = jnp.pad(dot_t(branch_grad, output_weight).astype(BF16), ((0, R - T), (0, 0)))
    query_wide, key_grad, value_grad, layer_output = attn_bwd(
        query_ext,
        attended_grad,
        attended_wide,
        key_all,
        value_all,
        probs,
        layer.reshape(S, piece, D),
        scale,
        HEADS,
        block,
        F,
    )
    key_grad, value_grad = key_grad[:T], value_grad[:T]
    sizes = (2, F // 2, F // 2, lax.axis_size("dp") // (F // 2))
    used = 3 * mels + -3 * mels % 16
    none = jnp.zeros((mels, 2 * D), BF16)
    taps = [
        stem_pair[mels : 3 * mels],
        jnp.concatenate([stem_pair[3 * mels :], none], axis=0),
        jnp.concatenate([none, stem_pair[:mels]], axis=0),
    ]
    rest = {
        "query": query_weight,
        "key": key_weight,
        "value": value_weight,
        "xhat": xhat1,
        "r": jnp.broadcast_to(r1, (T, 128)),
        "gain": jnp.broadcast_to(first_gain, (8, D)),
        "mixed": mixed_grad,
        "conv_linear": conv_linear,
        "reduce": reduce_matrix,
        "stem_linear": stem_linear,
        "stem_taps": jnp.stack(taps),
        "columns": columns,
        "second": jnp.where(
            lax.broadcasted_iota(jnp.int32, (8, 1), 0) == 0, second_gain_grad, second_shift_grad
        ),
    }
    FF = hidden_weight.shape[1]
    wide = FF // D
    one = [(first_normed, D)]
    *terms, mel_slots = sum_everywhere(
        [
            ([(hidden_active, FF)], [(cot, D)]),
            ([(second_normed, D)], [(hidden_grad, FF)]),
            ([(attended, D)], [(branch_grad, D)]),
            (one, [(query_wide, D)]),
            (one, [(key_grad, D)]),
            (one, [(value_grad, D)]),
            ([(odd_active_before, D), (stem_active, 2 * D)], [(None, D)]),
        ],
        rest,
        (2 * wide + 1, 2 * wide + 2, 2 * wide + 3, 2 * wide + 4),
        used,
        S,
        F,
        sizes,
        0,
    )
    mel_gradient = mel_slots.reshape(S, piece_frames, mels)
    return_w, hidden_w, output_w, query_w, key_w, value_w, reduce_w, short = [
        v.astype(F32) for v in terms
    ]
    stem_w = short[: 3 * mels]
    sums = short[used:]
    small = wide + 6
    return (
        layer_output,
        mel_gradient,
        stem_w.reshape(3, mels, D),
        sums[small],
        reduce_w.reshape(3, D, D),
        sums[wide + 5],
        sums[small + 1],
        sums[small + 2],
        query_w,
        sums[wide + 2],
        key_w,
        value_w,
        sums[wide + 4],
        output_w,
        sums[wide + 1],
        sums[small + 3],
        sums[small + 4],
        hidden_w,
        sums[1 : wide + 1].reshape(FF),
        return_w,
        sums[0],
    )


def solution(mesh):
    cut = P("dp", "frame", None)
    return jax.shard_map(
        on_device,
        mesh=mesh,
        in_specs=(cut, P("dp")) + (P(),) * 19 + (cut,),
        out_specs=(cut, cut) + (P(),) * 19,
        check_vma=False,
    )
```

```python
import functools
import math

import jax
import jax.numpy as jnp
from jax import lax
from jax.experimental import pallas as pl
from jax.experimental.pallas import tpu as pltpu
from jax.sharding import PartitionSpec as P

HEADS = 8
EPS = 1e-05
F32 = jnp.float32
BF16 = jnp.bfloat16
PHI_SLOPE = 0.28
PHI_POLY = (
    0.1167294156016242,
    0.06622785593379492,
    0.27197610469464767,
    -0.24067367858721922,
    0.3920693507793772,
    -0.10632905941542621,
)


def phi_parts(v):
    size = jnp.abs(v)
    t = 1.0 / (1.0 + PHI_SLOPE * size)
    bell = jnp.exp(-0.5 * v * v)
    poly = PHI_POLY[5]
    for c in PHI_POLY[4::-1]:
        poly = poly * t + c
    tail = poly * t * bell
    cdf = jnp.where(v >= 0, 1.0 - tail, tail)
    return cdf, bell * (1.0 / math.sqrt(2.0 * math.pi))


def gelu(v):
    cdf, _ = phi_parts(v)
    return v * cdf


def gelu_slope(v):
    cdf, pdf = phi_parts(v)
    return cdf + v * pdf


def dot(left, right):
    return jnp.dot(left, right, preferred_element_type=F32)


def dot_t(left, right):
    return lax.dot_general(left, right, (((1,), (1,)), ((), ())), preferred_element_type=F32)


def outer(left, right):
    return lax.dot_general(left, right, (((0,), (0,)), ((), ())), preferred_element_type=F32)


def column_total(x):
    return jnp.sum(x.astype(F32), axis=0)


def norm_parts(x):
    centred = x - jnp.mean(x, axis=-1, keepdims=True)
    r = lax.rsqrt(jnp.mean(centred * centred, axis=-1, keepdims=True) + EPS)
    return centred * r, r


def norm_pull(xhat, r, gain, dy):
    dh = dy * gain
    inner = r * (
        dh
        - jnp.mean(dh, axis=-1, keepdims=True)
        - xhat * jnp.mean(dh * xhat, axis=-1, keepdims=True)
    )
    return inner, column_total(dy * xhat), column_total(dy)


def positions_of(first, count, width):
    half = width // 2
    step = math.log(10000.0) / (half - 1)
    rate = jnp.exp(-step * jnp.arange(half, dtype=F32))[None, :]
    fine = math.gcd(count, 16)
    coarse = count // fine
    a = (first + fine * jnp.arange(coarse, dtype=jnp.int32)).astype(F32)[:, None] * rate
    b = jnp.arange(fine, dtype=jnp.int32).astype(F32)[:, None] * rate
    sa, ca = jnp.sin(a)[:, None, :], jnp.cos(a)[:, None, :]
    sb, cb = jnp.sin(b)[None, :, :], jnp.cos(b)[None, :, :]
    both = jnp.concatenate([sa * cb + ca * sb, ca * cb - sa * sb], axis=2)
    return both.reshape(count, width)


def half_mask(shape, h, hd):
    lane = lax.broadcasted_iota(jnp.int32, shape, 1)
    return (lane >= h*hd) & (lane < (h+1)*hd)

MESH = pl.DeviceIdType.MESH


def group_peer(G, o):
    fr = lax.axis_index("frame")
    return (lax.axis_index("dp"), fr // G * G + lax.rem(lax.rem(fr, G) + o, G))


def greet(F):
    barrier = pltpu.get_barrier_semaphore()
    for o in range(1, F):
        pl.semaphore_signal(barrier, inc=1, device_id=group_peer(F, o), device_id_type=MESH)


def meet(F):
    greet(F)
    pl.semaphore_wait(pltpu.get_barrier_semaphore(), F - 1)


class Move:
    def __init__(self, gather, F, src, dst, sems):
        self.src, self.dst = src, dst
        self.send, self.recv, self.own = sems
        self.S = src.shape[0]
        S, G = self.S, F // src.shape[0]
        self.dp, self.fr = lax.axis_index("dp"), lax.axis_index("frame")
        over = [a * G + self.fr // S for a in range(S)]
        back = [lax.rem(self.fr, G) * S + a for a in range(S)]
        self.to, self.sender = (over, back) if gather else (back, over)
        self.place = lax.rem(self.fr, S) if gather else self.fr // G

    def far(self, a):
        return pltpu.make_async_remote_copy(
            src_ref=self.src.at[a],
            dst_ref=self.dst.at[self.place],
            send_sem=self.send.at[a],
            recv_sem=self.recv.at[self.place],
            device_id=(self.dp, self.to[a]),
            device_id_type=MESH,
        )

    def near(self, a):
        return pltpu.make_async_copy(self.src.at[a], self.dst.at[self.place], self.own.at[a])

    def start(self):
        for a in range(self.S):

            @pl.when(self.to[a] != self.fr)
            def _():
                self.far(a).start()

            @pl.when(self.to[a] == self.fr)
            def _():
                self.near(a).start()

    def wait(self):
        for a in range(self.S):

            @pl.when(self.to[a] != self.fr)
            def _():
                self.far(a).wait_send()

            @pl.when(self.to[a] == self.fr)
            def _():
                self.near(a).wait()

            @pl.when(self.sender[a] != self.fr)
            def _():
                landed = self.dst.at[a]
                pltpu.make_async_copy(landed, landed, self.recv.at[a]).wait()


def move_sems(S):
    return [pltpu.SemaphoreType.DMA((S,))] * 3


def lanes_of(pair):
    return pl.ds(pl.multiple_of(pair * 128, 128), 128)


def mel_kernel(F, m_ref, e_ref, d_ref, h_ref, edge_send, edge_recv, edge_own, *sems):
    S = m_ref.shape[0]
    G = F // S
    dp, fr = lax.axis_index("dp"), lax.axis_index("frame")
    r = lax.rem(fr, G)
    meet(F)
    move = Move(True, F, m_ref, d_ref, sems)
    ends = []
    for a in range(S):
        last = (lax.rem(fr, S) == S - 1) & (fr + 1 < F)
        ends.append((a, 0, last, a * G + (fr + 1) // S))
        first = (lax.rem(fr, S) == 0) & (fr > 0)
        ends.append((a, 1, first, a * G + fr // S - 1))

    def far(a, k, to):
        return pltpu.make_async_remote_copy(
            src_ref=e_ref.at[a, k],
            dst_ref=h_ref.at[k],
            send_sem=edge_send.at[k, a],
            recv_sem=edge_recv.at[k],
            device_id=(dp, to),
            device_id_type=MESH,
        )

    def near(a, k):
        return pltpu.make_async_copy(e_ref.at[a, k], h_ref.at[k], edge_own.at[k])

    for a, k, holds, to in ends:

        @pl.when(holds & (to != fr))
        def _():
            far(a, k, to).start()

        @pl.when(holds & (to == fr))
        def _():
            near(a, k).start()

    move.start()
    for a, k, holds, to in ends:

        @pl.when(holds & (to != fr))
        def _():
            far(a, k, to).wait_send()

        @pl.when(holds & (to == fr))
        def _():
            near(a, k).wait()

    for k, wanted, sender in ((0, r > 0, r * S - 1), (1, r < G - 1, (r + 1) * S)):

        @pl.when(wanted & (sender != fr))
        def _():
            landed = h_ref.at[k]
            pltpu.make_async_copy(landed, landed, edge_recv.at[k]).wait()

    move.wait()


def gather_mel(pairs, F):
    S, piece, width = pairs.shape
    edges = jnp.stack([pairs[:, piece - 8 :], pairs[:, :8]], axis=1)
    far = pl.BlockSpec(memory_space=pl.ANY)
    return pl.pallas_call(
        functools.partial(mel_kernel, F),
        in_specs=[far, far],
        out_specs=[far, far],
        out_shape=[
            jax.ShapeDtypeStruct(pairs.shape, pairs.dtype),
            jax.ShapeDtypeStruct((2, 8, width), pairs.dtype),
        ],
        scratch_shapes=[
            pltpu.SemaphoreType.DMA((2, S)),
            pltpu.SemaphoreType.DMA((2,)),
            pltpu.SemaphoreType.DMA((2,)),
        ]
        + move_sems(S),
        compiler_params=pltpu.CompilerParams(
            collective_id=3, has_side_effects=True, vmem_limit_bytes=1 << 20
        ),
    )(pairs, edges)


def fwd_kernel(
    scale,
    hd,
    F,
    G,
    T,
    pairs,
    q_ref,
    k_own,
    v_own,
    c_ref,
    p_ref,
    o_ref,
    b_ref,
    k_all,
    v_all,
    d_ref,
    s_ref,
    k_buf,
    v_buf,
    send_sem,
    recv_sem,
    own_sem,
    out_sem,
    *sems,
):
    per = 128 // hd
    pair, i = pl.program_id(0), pl.program_id(1)
    rows = k_own.shape[0]
    both = ((k_own, k_buf), (v_own, v_buf))
    kept = ((k_buf, k_all), (v_buf, v_all))

    def own_copy(n, p):
        src, dst = both[n]
        return pltpu.make_async_copy(
            src.at[:, lanes_of(p)], dst.at[pl.ds(0, rows), lanes_of(p)], own_sem.at[n, p]
        )

    def keep(n, p):
        src, dst = kept[n]
        return pltpu.make_async_copy(
            src.at[:, lanes_of(p)], dst.at[:, lanes_of(p)], out_sem.at[n, p]
        )

    def copy_to(n, p, o):
        src, dst = both[n]
        return pltpu.make_async_remote_copy(
            src_ref=src.at[:, lanes_of(p)],
            dst_ref=dst.at[pl.ds((G - o) * rows, rows), lanes_of(p)],
            send_sem=send_sem.at[n, p, o - 1],
            recv_sem=recv_sem.at[n, p, o - 1],
            device_id=group_peer(G, o),
            device_id_type=MESH,
        )

    @pl.when((pair == 0) & (i == 0))
    def _():
        for p in range(pairs):
            for n in range(2):
                own_copy(n, p).start()
        meet(F)
        for p in range(pairs):
            for n in range(2):
                for o in range(1, G):
                    copy_to(n, p, o).start()
        Move(True, F, c_ref, d_ref, sems).start()

    @pl.when(i == 0)
    def _():
        for n in range(2):
            own_copy(n, pair).wait()
            for o in range(1, G):
                copy_to(n, pair, o).wait_recv()
            keep(n, pair).start()

    k = k_buf[:, lanes_of(pair)]
    vt = v_buf[:, lanes_of(pair)].T
    outs = []
    for h in range(per):
        q = q_ref[...]
        q = jnp.where(half_mask(q.shape, h, hd), q, jnp.zeros_like(q))
        s_ref[h] = lax.dot_general(k, q, (((1,), (1,)), ((), ())), preferred_element_type=F32)
    for h in range(per):
        s = s_ref[h]
        if rows != T:
            at = lax.rem(lax.broadcasted_iota(jnp.int32, s.shape, 0), rows)
            s = jnp.where(at < T, s, -1e30)
        m = jnp.max(s, axis=0, keepdims=True)
        e = jnp.exp((s - m) * scale)
        l = jnp.sum(e, axis=0, keepdims=True)
        p = (e * (1.0 / l)).astype(BF16)
        p_ref[h] = p
        outs.append(jnp.dot(vt[h * hd : (h + 1) * hd], p, preferred_element_type=F32))
    out = jnp.concatenate(outs, axis=0).T
    o_ref[...] = out
    b_ref[...] = out.astype(BF16)

    @pl.when((pair == pairs - 1) & (i == pl.num_programs(1) - 1))
    def _():
        for p in range(pairs):
            for n in range(2):
                keep(n, p).wait()
                for o in range(1, G):
                    copy_to(n, p, o).wait_send()
        Move(True, F, c_ref, d_ref, sems).wait()


def attn_fwd(q, k, v, slots, scale, heads, QB, F, T):
    G = F // slots.shape[0]
    R, D = q.shape
    N = k.shape[0] * G
    hd = D // heads
    per = 128 // hd
    pairs = D // 128
    far = pl.BlockSpec(memory_space=pl.ANY)
    sems = pltpu.SemaphoreType.DMA((2, pairs, G - 1))
    return pl.pallas_call(
        functools.partial(fwd_kernel, scale, hd, F, G, T, pairs),
        grid=(pairs, R // QB),
        in_specs=[pl.BlockSpec((QB, 128), lambda p, i: (i, p)), far, far, far],
        out_specs=[
            pl.BlockSpec((per, N, QB), lambda p, i: (p, 0, i)),
            pl.BlockSpec((QB, 128), lambda p, i: (i, p)),
            pl.BlockSpec((QB, 128), lambda p, i: (i, p)),
            far,
            far,
            far,
        ],
        out_shape=[
            jax.ShapeDtypeStruct((heads, N, R), BF16),
            jax.ShapeDtypeStruct((R, D), F32),
            jax.ShapeDtypeStruct((R, D), BF16),
            jax.ShapeDtypeStruct((N, D), BF16),
            jax.ShapeDtypeStruct((N, D), BF16),
            jax.ShapeDtypeStruct(slots.shape, slots.dtype),
        ],
        scratch_shapes=[
            pltpu.VMEM((per, N, QB), F32),
            pltpu.VMEM((N, D), BF16),
            pltpu.VMEM((N, D), BF16),
            sems,
            sems,
            pltpu.SemaphoreType.DMA((2, pairs)),
            pltpu.SemaphoreType.DMA((2, pairs)),
        ]
        + move_sems(slots.shape[0]),
        compiler_params=pltpu.CompilerParams(
            collective_id=1, has_side_effects=True, vmem_limit_bytes=60 << 20
        ),
    )(q, k, v, slots)


def bwd_kernel(
    scale,
    hd,
    F,
    G,
    pairs,
    q_ref,
    do_ref,
    o_ref,
    k_ref,
    v_ref,
    p_ref,
    y_ref,
    dq_ref,
    dk_ref,
    dv_ref,
    z_ref,
    dp_ref,
    kt_ref,
    acc_ref,
    got_ref,
    send_sem,
    recv_sem,
    *sems,
):
    per = 128 // hd
    pair, i = pl.program_id(0), pl.program_id(1)
    slot = lax.rem(pair, 2)
    rows = dk_ref.shape[0]

    def copy_to(n, p, o):
        return pltpu.make_async_remote_copy(
            src_ref=acc_ref.at[lax.rem(p, 2), n, pl.ds(o * rows, rows)],
            dst_ref=got_ref.at[p, n, o - 1],
            send_sem=send_sem.at[n, p, o - 1],
            recv_sem=recv_sem.at[n, p, o - 1],
            device_id=group_peer(G, o),
            device_id_type=MESH,
        )

    every = [(n, o) for n in range(2) for o in range(1, G)]

    @pl.when((pair == 0) & (i == 0))
    def _():
        meet(F)
        Move(False, F, y_ref, z_ref, sems).start()

    @pl.when((pair >= 2) & (i == 0))
    def _():
        for n, o in every:
            copy_to(n, pair - 2, o).wait_send()

    @pl.when(i == 0)
    def _():
        kt_ref[...] = k_ref[...].T
        acc_ref[slot] = jnp.zeros(acc_ref.shape[1:], F32)

    do = do_ref[...]
    q = q_ref[...]
    v = v_ref[...]
    prod = (do.astype(F32) * o_ref[...]).T
    for h in range(per):
        doh = jnp.where(half_mask(do.shape, h, hd), do, jnp.zeros_like(do))
        dp_ref[h] = lax.dot_general(v, doh, (((1,), (1,)), ((), ())), preferred_element_type=F32)
    dqs = []
    for h in range(per):
        doh = jnp.where(half_mask(do.shape, h, hd), do, jnp.zeros_like(do))
        qh = jnp.where(half_mask(q.shape, h, hd), q, jnp.zeros_like(q))
        delta = jnp.sum(prod[h * hd : (h + 1) * hd], axis=0, keepdims=True)
        p = p_ref[h]
        ds = (p.astype(F32) * (dp_ref[h] - delta)).astype(BF16)
        acc_ref[slot, 1] += jnp.dot(p, doh, preferred_element_type=F32)
        acc_ref[slot, 0] += jnp.dot(ds, qh, preferred_element_type=F32)
        dqs.append(jnp.dot(kt_ref[h * hd : (h + 1) * hd], ds, preferred_element_type=F32))
    dq_ref[...] = (jnp.concatenate(dqs, axis=0) * scale).T.astype(BF16)

    def finish(p):
        for n, o in every:
            copy_to(n, p, o).wait_recv()
        for n, out, factor in ((0, dk_ref, scale), (1, dv_ref, 1.0)):
            total = acc_ref[lax.rem(p, 2), n, pl.ds(0, rows)]
            for o in range(1, G):
                total = total + got_ref[p, n, o - 1]
            out[:, lanes_of(p)] = (total * factor).astype(BF16)

    ends = i == pl.num_programs(1) - 1

    @pl.when(ends & (pair >= 1))
    def _():
        finish(pair - 1)

    @pl.when(ends)
    def _():
        for n, o in every:
            copy_to(n, pair, o).start()

    @pl.when(ends & (pair == pairs - 1))
    def _():
        finish(pair)
        for p in range(max(pairs - 2, 0), pairs):
            for n, o in every:
                copy_to(n, p, o).wait_send()
        Move(False, F, y_ref, z_ref, sems).wait()


def attn_bwd(q, do, o, k, v, p, pieces, scale, heads, QB, F):
    G = F // pieces.shape[0]
    far = pl.BlockSpec(memory_space=pl.ANY)
    R, D = q.shape
    N = k.shape[0]
    hd = D // heads
    per = 128 // hd
    pairs = D // 128
    row = pl.BlockSpec((QB, 128), lambda p, i: (i, p))
    key = pl.BlockSpec((N, 128), lambda p, i: (0, p))
    near = pl.BlockSpec(memory_space=pltpu.VMEM)
    sems = pltpu.SemaphoreType.DMA((2, pairs, G - 1))
    own = jax.ShapeDtypeStruct((N // G, D), BF16)
    return pl.pallas_call(
        functools.partial(bwd_kernel, scale, hd, F, G, pairs),
        grid=(pairs, R // QB),
        in_specs=[row, row, row, key, key, pl.BlockSpec((per, N, QB), lambda p, i: (p, 0, i)), far],
        out_specs=[row, near, near, far],
        out_shape=[
            jax.ShapeDtypeStruct((R, D), BF16),
            own,
            own,
            jax.ShapeDtypeStruct(pieces.shape, pieces.dtype),
        ],
        scratch_shapes=[
            pltpu.VMEM((per, N, QB), F32),
            pltpu.VMEM((128, N), BF16),
            pltpu.VMEM((2, 2, N, 128), F32),
            pltpu.VMEM((pairs, 2, G - 1, N // G, 128), F32),
            sems,
            sems,
        ]
        + move_sems(pieces.shape[0]),
        compiler_params=pltpu.CompilerParams(
            collective_id=2, has_side_effects=True, vmem_limit_bytes=60 << 20
        ),
    )(q, do, o, k, v, p, pieces)


TILE = 512
LAG = 3
AHEAD = 3


def pick(c, values):
    out = values[0]
    for n in range(1, len(values)):
        if values[n] != values[n - 1]:
            out = jnp.where(c >= n, values[n], out)
    return out


class Rest:
    FIRST = 5

    def __init__(self, G, T, taps, m_ref, t_ref, w_ref, data, scratch, sems):
        self.m, self.t, self.w = m_ref, t_ref, w_ref
        self.data = data
        self.ext, self.edge, self.halo, self.sg, self.y0, self.y1, self.y2 = scratch
        self.send, self.recv = sems
        self.G, self.T, self.taps = G, T, taps
        self.R = self.sg.shape[0]
        self.row = lax.rem(lax.axis_index("frame"), G)
        self.size = 256 if self.R % 256 == 0 else 128
        self.token_blocks = [(a, min(a + 256, T)) for a in range(0, T, 256)]
        self.edges_at = self.FIRST + len(self.token_blocks)
        self.halo_at = self.edges_at + 2
        self.stem_at = self.halo_at + 1
        self.mel_at = self.stem_at + self.R // self.size
        self.weights_at = self.mel_at + 1
        self.halo[...] = jnp.zeros_like(self.halo)

    def due(self, name):
        if name in ("reduce", "stem_linear", "stem_taps"):
            return self.stem_at
        if name in ("columns", "second_gain", "second_shift"):
            return self.weights_at
        return self.FIRST

    def tokens(self, n):
        a, b = self.token_blocks[n]
        q, k, v, conv, base = self.taps
        data, rows = self.data, pl.ds(a, b - a)
        dy = (
            dot_t(self.m[q, rows], data["query"][...])
            + dot_t(self.m[k, rows], data["key"][...])
            + dot_t(self.m[v, rows], data["value"][...])
        )
        xhat, r = norm_parts(data["stream"][rows])
        dh = dy * data["gain"][...]
        inner = r * (
            dh
            - jnp.mean(dh, axis=-1, keepdims=True)
            - xhat * jnp.mean(dh * xhat, axis=-1, keepdims=True)
        )
        self.t[base + 1 : base + 2] += jnp.sum(dy * xhat, axis=0, keepdims=True)
        self.t[base + 2 : base + 3] += jnp.sum(dy, axis=0, keepdims=True)
        grad = gelu_slope(data["conv_linear"][rows]) * (data["mixed"][rows] + inner)
        grad = grad.astype(BF16)
        self.m[conv, rows] = grad
        self.ext[rows] = grad
        if n == 0:
            self.edge[1] = grad[:16]
            self.ext[pl.ds(self.R, 16)] = grad[:16]
        if b == self.T:
            self.edge[0] = grad[b - a - 16 :]

    def edge_copy(self, n):
        return pltpu.make_async_remote_copy(
            src_ref=self.edge.at[n],
            dst_ref=self.halo.at[n],
            send_sem=self.send.at[n],
            recv_sem=self.recv.at[n],
            device_id=group_peer(self.G, 1 if n == 0 else self.G - 1),
            device_id_type=MESH,
        )

    def has(self, n):
        return self.row < self.G - 1 if n == 0 else self.row > 0

    def send_edges(self):
        for n in range(2):

            @pl.when(self.has(n))
            def _():
                self.edge_copy(n).start()

    def fill_halo(self):
        for n in range(2):

            @pl.when(self.has(1 - n))
            def _():
                landed = self.halo.at[n]
                pltpu.make_async_copy(landed, landed, self.recv.at[n]).wait()

        at = self.T // 16 * 16
        rows = pl.ds(at, self.R - at)
        own = self.ext[rows].astype(F32)
        place = lax.broadcasted_iota(jnp.int32, own.shape, 0) + at
        before = self.halo[0].astype(F32)[15:16]
        after = self.halo[1].astype(F32)[:1]
        own = jnp.where(place < self.T, own, 0.0)
        own = jnp.where(place == self.T, after, own)
        own = jnp.where(place == self.R - 1, before, own)
        self.ext[rows] = own.astype(BF16)

    def stem(self, n):
        data, a = self.data, n * self.size
        D = self.ext.shape[1]
        rows = pl.ds(a, self.size)
        pair = dot_t(self.ext[rows], data["reduce"][pl.ds(D, 2 * D)])
        third = dot_t(self.ext[pl.ds(a, self.size + 16)], data["reduce"][pl.ds(0, D)])
        third = third[1 : self.size + 1]
        active = jnp.concatenate([pair[:, :D], pair[:, D:] + third], axis=1)
        place = lax.broadcasted_iota(jnp.int32, active.shape, 0) + a
        high = self.T + jnp.where(self.row < self.G - 1, 1, 0)
        low = self.R - jnp.where(self.row > 0, 1, 0)
        grad = gelu_slope(data["stem_linear"][rows]) * active
        grad = jnp.where((place < high) | (place >= low), grad, 0.0).astype(BF16)
        self.sg[rows] = grad
        self.y0[rows] = dot_t(grad, data["stem_taps"][0])
        y1 = dot_t(grad, data["stem_taps"][1])
        self.y1[pl.ds(a + 8, self.size)] = y1
        if a + self.size == self.R:
            self.y1[pl.ds(0, 8)] = y1[self.size - 8 :]
        self.y2[rows] = dot_t(grad, data["stem_taps"][2])

    def mel(self, out):
        T = self.T
        total = self.y0[pl.ds(0, T)] + self.y1[pl.ds(7, T)] + self.y2[pl.ds(1, T)]
        n = out.shape[1]
        for j in range(out.shape[0]):
            out[j] = total[j * n : (j + 1) * n]

    def weights(self):
        base = self.taps[-1]
        D = self.ext.shape[1]
        own = self.sg[pl.ds(0, self.T)]
        wide = outer(self.data["columns"][pl.ds(0, self.T)], own)
        mels = wide.shape[0] // 4
        sums = dot(jnp.ones((16, self.T), BF16), own)[:1]
        self.w[self.w.shape[0] - 1, pl.ds(0, 3 * mels)] = (
            wide[: 3 * mels, :D] + wide[mels:, D:]
        ).astype(BF16)
        self.t[base : base + 1] = sums[:, :D] + sums[:, D:]
        self.t[base + 3 : base + 4] = self.data["second_gain"][...]
        self.t[base + 4 : base + 5] = self.data["second_shift"][...]

    def step(self, t, out):
        todo = [(self.FIRST + n, functools.partial(self.tokens, n)) for n in range(len(self.token_blocks))]
        todo.append((self.edges_at, self.send_edges))
        todo.append((self.halo_at, self.fill_halo))
        todo += [
            (self.stem_at + n, functools.partial(self.stem, n)) for n in range(self.R // self.size)
        ]
        todo.append((self.mel_at, functools.partial(self.mel, out)))
        todo.append((self.weights_at, self.weights))
        for at, work in todo:
            pl.when(t == at)(work)

    def drain(self):
        for n in range(2):

            @pl.when(self.has(n))
            def _():
                self.edge_copy(n).wait_send()


REST = (
    "query",
    "key",
    "value",
    "stream",
    "gain",
    "mixed",
    "conv_linear",
    "reduce",
    "stem_linear",
    "stem_taps",
    "columns",
    "second_gain",
    "second_shift",
)


def sum_kernel(sizes, F, used, plan, *refs):
    places, left_at, right_at, lefts, rights, n_in, n_out, taps, T = plan
    extra = len(REST)
    in_refs, rest_refs = refs[: n_in - extra], refs[n_in - extra : n_in]
    g_refs, slot_ref = refs[n_in : n_in + n_out - 1], refs[n_in + n_out - 1]
    refs = refs[n_in + n_out :]
    l_ref, m_ref, t_ref, w_ref, s_ref, r0, r1, r2, r3 = refs[:9]
    kept, work = refs[9 : 9 + extra], refs[9 + extra : 16 + extra]
    piece_ref, send_sem, recv_sem, load_sem, out_sem, edge_send, edge_recv, *sems = refs[16 + extra :]
    t_ref[...] = jnp.zeros_like(t_ref)
    w_ref[len(places) - 1] = jnp.zeros(w_ref.shape[1:], BF16)
    G = F // slot_ref.shape[0]
    rest = Rest(
        G, T, taps, m_ref, t_ref, w_ref, dict(zip(REST, kept)), work, (edge_send, edge_recv)
    )
    recv = (r0, r1, r2, r3)
    chunks = len(places)
    Y = sizes[2]
    dp = lax.axis_index("dp")
    fr = lax.axis_index("frame")
    z = dp // Y
    y = lax.rem(dp, Y)
    x = fr // 2
    core = lax.rem(fr, 2)
    first = core == 0
    me = (core, jnp.where(first, x, y), jnp.where(first, y, x), z)

    loads, due = [], []
    for buf, sources, at in ((l_ref, lefts, left_at), (m_ref, rights, right_at)):
        for n, (which, col) in enumerate(sources):
            if which is None:
                continue
            src = in_refs[which].at[pl.ds(0, T), pl.ds(col, TILE)]
            loads.append(pltpu.make_async_copy(src, buf.at[n], load_sem.at[len(loads)]))
            first_use = at.index(n)
            due.append(min(first_use, rest.FIRST) if at is right_at and n in taps[:3] else first_use)
    for name, src, dst in zip(REST, rest_refs, kept):
        loads.append(pltpu.make_async_copy(src, dst, load_sem.at[len(loads)]))
        due.append(rest.due(name))
    for n in sorted(range(len(loads)), key=lambda n: (due[n], n)):
        loads[n].start()

    def device(kind, p):
        if kind == 0:
            return (dp, x * 2 + p)
        if kind == 3:
            return (p * Y + y, fr)
        along_x = first if kind == 1 else jnp.logical_not(first)
        return (z * Y + jnp.where(along_x, y, p), jnp.where(along_x, p, x) * 2 + core)

    def peer(k, o):
        return lax.rem(me[k] + o, sizes[k])

    pairs = [(k, o) for k in range(4) for o in range(1, sizes[k])]
    barrier = pltpu.get_barrier_semaphore()
    for k, o in pairs:
        pl.semaphore_signal(barrier, inc=1, device_id=device(k, peer(k, o)), device_id_type=MESH)
    greet(F)
    pl.semaphore_wait(barrier, len(pairs) + F - 1)
    move = Move(False, F, piece_ref, slot_ref, sems)

    cut = [TILE]
    for k in range(4):
        cut.append(cut[-1] // sizes[k])
    split = cut[4] % 16 == 0
    if not split:
        cut[4] = cut[3]

    def start_of(level):
        at = 0
        for k in range(level):
            if k < 3 or split:
                at = at + me[k] * cut[k + 1]
        return pl.multiple_of(at, 16) if level else 0

    def scatter_copy(c, k, o):
        p = peer(k, o)
        at = start_of(k)
        if k < 3 or split:
            at = pl.multiple_of(at + p * cut[k + 1], 16)
        return pltpu.make_async_remote_copy(
            src_ref=w_ref.at[c, pl.ds(at, cut[k + 1])],
            dst_ref=recv[k].at[c, o - 1],
            send_sem=send_sem.at[c, k, o - 1],
            recv_sem=recv_sem.at[c, k, o - 1],
            device_id=device(k, p),
            device_id_type=MESH,
        )

    def gather_copy(c, k, o):
        here = s_ref.at[c, pl.ds(start_of(k + 1), cut[k + 1])]
        return pltpu.make_async_remote_copy(
            src_ref=here,
            dst_ref=here,
            send_sem=send_sem.at[c, 4 + k, o - 1],
            recv_sem=recv_sem.at[c, 4 + k, o - 1],
            device_id=device(k, peer(k, o)),
            device_id_type=MESH,
        )

    def out_copy(c):
        which, row, col = places[c]
        dst = g_refs[which].at[pl.ds(row, TILE), pl.ds(col, TILE)]
        return pltpu.make_async_copy(s_ref.at[c], dst, out_sem.at[c])

    def add(c, k):
        at = start_of(k + 1)
        dst = w_ref if k < 3 else s_ref
        step = math.gcd(cut[k + 1], 64)

        def body(i, _):
            r = pl.multiple_of(at + i * step, 16)
            total = w_ref[c, pl.ds(r, step)].astype(F32)
            for o in range(1, sizes[k]):
                total = total + recv[k][
                    c, o - 1, pl.ds(pl.multiple_of(i * step, 16), step)
                ].astype(F32)
            dst[c, pl.ds(r, step)] = total.astype(BF16)
            return 0

        lax.fori_loop(0, cut[k + 1] // step, body, 0)

    stages = [("s", k) for k in range(4)] + [("g", k) for k in (3, 2, 1, 0) if k < 3 or split]
    copies = {"s": scatter_copy, "g": gather_copy}

    def finish(c, n):
        kind, k = stages[n]
        for o in range(1, sizes[k]):
            copies[kind](c, k, o).wait_recv()
        if kind == "s":
            add(c, k)
        if n + 1 < len(stages):
            kind, k = stages[n + 1]
            for o in range(1, sizes[k]):
                copies[kind](c, k, o).start()

    last = LAG * (len(stages) - 1) + AHEAD

    def turn(t, _):
        for n in range(len(loads)):

            @pl.when(t == due[n])
            def _():
                loads[n].wait()

        @pl.when(t < chunks - 1)
        def _():
            left = l_ref[pick(t, left_at)]
            right = m_ref[pick(t, right_at)]
            w_ref[t] = outer(left, right).astype(BF16)
            ones = jnp.ones((16, T), BF16)
            t_ref[pl.ds(pick(t, right_at), 1)] = dot(ones, right)[:1]

        @pl.when(t == rest.weights_at)
        def _():
            move.start()

        rest.step(t, piece_ref)

        @pl.when(t == chunks - 1)
        def _():
            w_ref[chunks - 1, pl.ds(used, t_ref.shape[0])] = t_ref[...].astype(BF16)

        @pl.when((t >= 1) & (t <= chunks))
        def _():
            for o in range(1, sizes[0]):
                scatter_copy(t - 1, 0, o).start()

        for n in range(len(stages) - 1, -1, -1):
            c = t - AHEAD - LAG * n

            @pl.when((c >= 0) & (c < chunks))
            def _():
                finish(c, n)

        for c in range(chunks):

            @pl.when(t == c + last)
            def _():
                out_copy(c).start()

        return 0

    lax.fori_loop(0, chunks + last, turn, 0)

    def drain(c, _):
        for kind, k in stages:
            for o in range(1, sizes[k]):
                copies[kind](c, k, o).wait_send()
        return 0

    lax.fori_loop(0, chunks, drain, 0)
    move.wait()
    rest.drain()
    for c in range(chunks):
        out_copy(c).wait()


def sum_everywhere(products, rest, taps, used, S, F, sizes, cid):
    arrays, lefts, rights = [], [], []
    places, left_at, right_at, shapes = [], [], [], []

    def slots_of(pieces, slots):
        found = []
        for array, width in pieces:
            which = None
            if array is not None:
                which = next((n for n, a in enumerate(arrays) if a is array), None)
                if which is None:
                    which = len(arrays)
                    arrays.append(array)
            for col in range(0, width, TILE):
                if (which, col) not in slots:
                    slots.append((which, col))
                found.append(slots.index((which, col)))
        return found

    for n, (left, right) in enumerate(products):
        a, b = slots_of(left, lefts), slots_of(right, rights)
        shapes.append((len(a) * TILE, len(b) * TILE))
        for i, u in enumerate(a):
            for j, v in enumerate(b):
                places.append((n, i * TILE, j * TILE))
                left_at.append(u)
                right_at.append(v)
    places.append((len(products), 0, 0))
    shapes.append((TILE, TILE))
    T = min(a.shape[0] for a in arrays)
    R = rest["stem_linear"].shape[0]
    mels = rest["columns"].shape[1] // 4
    chunks = len(places)
    cut = [TILE]
    for n in sizes:
        cut.append(cut[-1] // n)
    if cut[4] % 16:
        cut[4] = cut[3]
    most = max(sizes) - 1
    spec = pl.BlockSpec(memory_space=pl.ANY)
    sums = len(rights) + 5
    sums += -sums % 16
    slots = jax.ShapeDtypeStruct((S, T // S, 2 * mels), F32)
    taps = tuple(right_at[n] for n in taps) + (len(rights),)
    plan = (
        places,
        left_at,
        right_at,
        lefts,
        rights,
        len(arrays) + len(REST),
        len(shapes) + 1,
        taps,
        T,
    )
    return pl.pallas_call(
        functools.partial(sum_kernel, sizes, F, used, plan),
        in_specs=[spec] * (len(arrays) + len(REST)),
        out_specs=[spec] * (len(shapes) + 1),
        out_shape=[jax.ShapeDtypeStruct(v, BF16) for v in shapes] + [slots],
        scratch_shapes=[
            pltpu.VMEM((len(lefts), T, TILE), BF16),
            pltpu.VMEM((len(rights), T, TILE), BF16),
            pltpu.VMEM((sums, TILE), F32),
        ]
        + [pltpu.VMEM((chunks, TILE, TILE), BF16)] * 2
        + [pltpu.VMEM((chunks, sizes[k] - 1, cut[k + 1], TILE), BF16) for k in range(4)]
        + [pltpu.VMEM(rest[name].shape, rest[name].dtype) for name in REST]
        + [
            pltpu.VMEM((R + 16, TILE), BF16),
            pltpu.VMEM((2, 16, TILE), BF16),
            pltpu.VMEM((2, 16, TILE), BF16),
            pltpu.VMEM((R, 2 * TILE), BF16),
            pltpu.VMEM((R, 2 * mels), F32),
            pltpu.VMEM((R + 8, 2 * mels), F32),
            pltpu.VMEM((R, 2 * mels), F32),
            pltpu.VMEM(slots.shape, F32),
        ]
        + [
            pltpu.SemaphoreType.DMA((chunks, 8, most)),
            pltpu.SemaphoreType.DMA((chunks, 8, most)),
            pltpu.SemaphoreType.DMA((len(lefts) + len(rights) + len(REST),)),
            pltpu.SemaphoreType.DMA((chunks,)),
            pltpu.SemaphoreType.DMA((2,)),
            pltpu.SemaphoreType.DMA((2,)),
        ]
        + move_sems(S),
        compiler_params=pltpu.CompilerParams(
            collective_id=cid, has_side_effects=True, vmem_limit_bytes=67043328
        ),
    )(*arrays, *[rest[name] for name in REST])


def widen_kernel(parts, count, *refs):
    ins, outs = refs[:count], refs[count : 2 * count + 1]
    b_ref, f_ref, load_sem, out_sem = refs[2 * count + 1 :]
    loads, stores = [], []
    for n, (which, row, col, places) in enumerate(parts):
        rows = pl.ds(row, TILE)
        cols = pl.ds(col, TILE)
        loads.append(
            pltpu.make_async_copy(ins[which].at[rows, cols], b_ref.at[n], load_sem.at[n])
        )
        here = []
        for out, at, first, size in places:
            target = outs[out].at[pl.ds(at, size), cols]
            source = f_ref.at[n, pl.ds(first, size)]
            here.append(pltpu.make_async_copy(source, target, out_sem.at[n, len(here)]))
        stores.append(here)
    for load in loads:
        load.start()
    for n, load in enumerate(loads):
        load.wait()

        def body(i, _):
            rows = pl.ds(pl.multiple_of(i * 64, 64), 64)
            f_ref[n, rows] = b_ref[n, rows].astype(F32)
            return 0

        lax.fori_loop(0, TILE // 64, body, 0)
        for store in stores[n]:
            store.start()
    for here in stores:
        for store in here:
            store.wait()


def widen(arrays, used, sums):
    parts = []
    last = len(arrays) - 1
    for n, a in enumerate(arrays):
        for row in range(0, a.shape[0], TILE):
            for col in range(0, a.shape[1], TILE):
                places = [(n, row, 0, TILE)]
                if n == last:
                    places = [(n, 0, 0, used[0]), (n + 1, 0, used[1], sums)]
                parts.append((n, row, col, places))
    shapes = [a.shape for a in arrays[:-1]] + [(used[0], TILE), (sums, TILE)]
    far = pl.BlockSpec(memory_space=pl.ANY)
    return pl.pallas_call(
        functools.partial(widen_kernel, parts, len(arrays)),
        in_specs=[far] * len(arrays),
        out_specs=[far] * len(shapes),
        out_shape=[jax.ShapeDtypeStruct(v, F32) for v in shapes],
        scratch_shapes=[
            pltpu.VMEM((len(parts), TILE, TILE), BF16),
            pltpu.VMEM((len(parts), TILE, TILE), F32),
            pltpu.SemaphoreType.DMA((len(parts),)),
            pltpu.SemaphoreType.DMA((len(parts), 2)),
        ],
        compiler_params=pltpu.CompilerParams(vmem_limit_bytes=67043328),
    )(*arrays)


def on_device(
    mel_frames,
    window_count,
    stem_weight,
    stem_bias,
    reduce_weight,
    reduce_bias,
    first_gain,
    first_shift,
    query_weight,
    query_bias,
    key_weight,
    value_weight,
    value_bias,
    output_weight,
    output_bias,
    second_gain,
    second_shift,
    hidden_weight,
    hidden_bias,
    return_weight,
    return_bias,
    cotangent,
):
    S, piece_frames, mels = mel_frames.shape
    piece = cotangent.shape[1]
    D = stem_weight.shape[2]
    hd = D // HEADS
    scale = hd ** (-0.5)
    F = lax.axis_size("frame")
    G = F // S
    T = S * piece
    R = -(-(T + 2) // 128) * 128
    f = lax.axis_index("frame")
    s = f // G
    r = f % G
    alive = s < window_count[0]

    own, beside = gather_mel(mel_frames.reshape(S, piece, 2 * mels), F)
    before = jnp.where(r > 0, beside[0, -1:], jnp.zeros((1, 2 * mels), BF16))
    after = jnp.where(r < G - 1, beside[1, :1], jnp.zeros((1, 2 * mels), BF16))
    gap = jnp.zeros((R - T - 2, 2 * mels), BF16)
    mel = jnp.concatenate([own.reshape(T, 2 * mels), after, gap, before], axis=0)
    odd_before = jnp.roll(mel[:, mels:], 1, axis=0)
    even_after = jnp.roll(mel[:, :mels], -1, axis=0)
    columns = jnp.concatenate([odd_before, mel, even_after], axis=1)
    stem_matrix = stem_weight.reshape(3 * mels, D)
    gap = jnp.zeros((mels, D), BF16)
    stem_pair = jnp.concatenate(
        [
            jnp.concatenate([stem_matrix, gap], axis=0),
            jnp.concatenate([gap, stem_matrix], axis=0),
        ],
        axis=1,
    )
    stem_bias2 = jnp.concatenate([stem_bias, stem_bias])
    stem_linear = dot(columns, stem_pair) + stem_bias2
    row = lax.broadcasted_iota(jnp.int32, (R, 1), 0)
    valid = (row < T) | ((row == T) & (r < G - 1)) | ((row == R - 1) & (r > 0))
    stem_active = jnp.where(valid, gelu(stem_linear), 0.0).astype(BF16)

    odd_active_before = jnp.roll(stem_active[:, D:], 1, axis=0)[:T]
    conv_columns = jnp.concatenate([odd_active_before, stem_active[:T]], axis=1)
    reduce_matrix = reduce_weight.reshape(3 * D, D)
    conv_linear = dot(conv_columns, reduce_matrix) + reduce_bias
    stream = gelu(conv_linear) + positions_of(r * T, T, D)
    xhat1, r1 = norm_parts(stream)
    first_normed = jnp.pad((xhat1 * first_gain + first_shift).astype(BF16), ((0, R - T), (0, 0)))
    query_ext = (dot(first_normed, query_weight) + query_bias).astype(BF16)
    key = dot(first_normed[:T], key_weight).astype(BF16)
    value = (dot(first_normed[:T], value_weight) + value_bias).astype(BF16)
    key = jnp.pad(key, ((0, -T % 16), (0, 0)))
    value = jnp.pad(value, ((0, -T % 16), (0, 0)))
    block = 256 if R % 256 == 0 else 128
    probs, attended_wide, attended, key_all, value_all, cot = attn_fwd(
        query_ext, key, value, cotangent, scale, HEADS, block, F, T
    )
    cot = cot.reshape(T, D)
    cot = jnp.where(alive, cot, jnp.zeros_like(cot))
    mixed = stream + dot(attended[:T], output_weight) + output_bias
    xhat2, r2 = norm_parts(mixed)
    second_normed = (xhat2 * second_gain + second_shift).astype(BF16)
    hidden_linear = dot(second_normed, hidden_weight) + hidden_bias
    hidden_cdf, hidden_pdf = phi_parts(hidden_linear)
    hidden_active = (hidden_linear * hidden_cdf).astype(BF16)
    layer = mixed + dot(hidden_active, return_weight) + return_bias
    layer = jnp.where(alive, layer, 0.0).astype(BF16)

    slope = hidden_cdf + hidden_linear * hidden_pdf
    hidden_grad = (slope * dot_t(cot, return_weight)).astype(BF16)
    inner, second_gain_grad, second_shift_grad = norm_pull(
        xhat2, r2, second_gain, dot_t(hidden_grad, hidden_weight)
    )
    mixed_grad = cot.astype(F32) + inner
    branch_grad = jnp.pad(mixed_grad.astype(BF16), ((0, R - T), (0, 0)))

    attended_grad = dot_t(branch_grad, output_weight).astype(BF16)
    query_wide, key_grad, value_grad, layer_output = attn_bwd(
        query_ext,
        attended_grad,
        attended_wide,
        key_all,
        value_all,
        probs,
        layer.reshape(S, piece, D),
        scale,
        HEADS,
        block,
        F,
    )
    key_grad, value_grad = key_grad[:T], value_grad[:T]
    sizes = (2, F // 2, F // 2, lax.axis_size("dp") // (F // 2))
    used = 3 * mels + -3 * mels % 16
    none = jnp.zeros((mels, 2 * D), BF16)
    taps = [
        stem_pair[mels : 3 * mels],
        jnp.concatenate([stem_pair[3 * mels :], none], axis=0),
        jnp.concatenate([none, stem_pair[:mels]], axis=0),
    ]
    rest = {
        "query": query_weight,
        "key": key_weight,
        "value": value_weight,
        "stream": stream,
        "gain": first_gain.reshape(1, D),
        "mixed": mixed_grad,
        "conv_linear": conv_linear,
        "reduce": reduce_matrix,
        "stem_linear": stem_linear,
        "stem_taps": jnp.stack(taps),
        "columns": columns,
        "second_gain": second_gain_grad.reshape(1, D),
        "second_shift": second_shift_grad.reshape(1, D),
    }
    FF = hidden_weight.shape[1]
    wide = FF // D
    one = [(first_normed, D)]
    *terms, mel_slots = sum_everywhere(
        [
            ([(hidden_active, FF)], [(cot, D)]),
            ([(second_normed, D)], [(hidden_grad, FF)]),
            ([(attended, D)], [(branch_grad, D)]),
            (one, [(query_wide, D)]),
            (one, [(key_grad, D)]),
            (one, [(value_grad, D)]),
            ([(odd_active_before, D), (stem_active, 2 * D)], [(None, D)]),
        ],
        rest,
        (2 * wide + 1, 2 * wide + 2, 2 * wide + 3, 2 * wide + 4),
        used,
        S,
        F,
        sizes,
        0,
    )
    mel_gradient = mel_slots.reshape(S, piece_frames, mels)
    rows = wide + 11
    rows += -rows % 16
    return_w, hidden_w, output_w, query_w, key_w, value_w, reduce_w, stem_w, sums = widen(
        terms, (3 * mels, used), rows
    )
    small = wide + 6
    return (
        layer_output,
        mel_gradient,
        stem_w.reshape(3, mels, D),
        sums[small],
        reduce_w.reshape(3, D, D),
        sums[wide + 5],
        sums[small + 1],
        sums[small + 2],
        query_w,
        sums[wide + 2],
        key_w,
        value_w,
        sums[wide + 4],
        output_w,
        sums[wide + 1],
        sums[small + 3],
        sums[small + 4],
        hidden_w,
        sums[1 : wide + 1].reshape(FF),
        return_w,
        sums[0],
    )


def solution(mesh):
    cut = P("dp", "frame", None)
    return jax.shard_map(
        on_device,
        mesh=mesh,
        in_specs=(cut, P("dp")) + (P(),) * 19 + (cut,),
        out_specs=(cut, cut) + (P(),) * 19,
        check_vma=False,
    )
```

```python
import functools
import math

import jax
import jax.numpy as jnp
from jax import lax
from jax.experimental import pallas as pl
from jax.experimental.pallas import tpu as pltpu
from jax.sharding import PartitionSpec as P

HEADS = 8
EPS = 1e-05
F32 = jnp.float32
BF16 = jnp.bfloat16
PHI_SLOPE = 0.28
PHI_POLY = (
    0.1167294156016242,
    0.06622785593379492,
    0.27197610469464767,
    -0.24067367858721922,
    0.3920693507793772,
    -0.10632905941542621,
)


def phi_parts(v):
    size = jnp.abs(v)
    t = 1.0 / (1.0 + PHI_SLOPE * size)
    bell = jnp.exp(-0.5 * v * v)
    poly = PHI_POLY[5]
    for c in PHI_POLY[4::-1]:
        poly = poly * t + c
    tail = poly * t * bell
    cdf = jnp.where(v >= 0, 1.0 - tail, tail)
    return cdf, bell * (1.0 / math.sqrt(2.0 * math.pi))


def gelu(v):
    cdf, _ = phi_parts(v)
    return v * cdf


def gelu_slope(v):
    cdf, pdf = phi_parts(v)
    return cdf + v * pdf


def dot(left, right):
    return jnp.dot(left, right, preferred_element_type=F32)


def dot_t(left, right):
    return lax.dot_general(left, right, (((1,), (1,)), ((), ())), preferred_element_type=F32)


def outer(left, right):
    return lax.dot_general(left, right, (((0,), (0,)), ((), ())), preferred_element_type=F32)


def column_total(x):
    return jnp.sum(x.astype(F32), axis=0)


def norm_parts(x):
    centred = x - jnp.mean(x, axis=-1, keepdims=True)
    r = lax.rsqrt(jnp.mean(centred * centred, axis=-1, keepdims=True) + EPS)
    return centred * r, r


def norm_pull(xhat, r, gain, dy):
    dh = dy * gain
    inner = r * (
        dh
        - jnp.mean(dh, axis=-1, keepdims=True)
        - xhat * jnp.mean(dh * xhat, axis=-1, keepdims=True)
    )
    return inner, column_total(dy * xhat), column_total(dy)


def positions_of(first, count, width):
    half = width // 2
    step = math.log(10000.0) / (half - 1)
    rate = jnp.exp(-step * jnp.arange(half, dtype=F32))[None, :]
    fine = math.gcd(count, 16)
    coarse = count // fine
    a = (first + fine * jnp.arange(coarse, dtype=jnp.int32)).astype(F32)[:, None] * rate
    b = jnp.arange(fine, dtype=jnp.int32).astype(F32)[:, None] * rate
    sa, ca = jnp.sin(a)[:, None, :], jnp.cos(a)[:, None, :]
    sb, cb = jnp.sin(b)[None, :, :], jnp.cos(b)[None, :, :]
    both = jnp.concatenate([sa * cb + ca * sb, ca * cb - sa * sb], axis=2)
    return both.reshape(count, width)


def half_mask(shape, h, hd):
    lane = lax.broadcasted_iota(jnp.int32, shape, 1)
    return (lane >= h*hd) & (lane < (h+1)*hd)

MESH = pl.DeviceIdType.MESH


def group_peer(G, o):
    fr = lax.axis_index("frame")
    return (lax.axis_index("dp"), fr // G * G + lax.rem(lax.rem(fr, G) + o, G))


def greet(F):
    barrier = pltpu.get_barrier_semaphore()
    for o in range(1, F):
        pl.semaphore_signal(barrier, inc=1, device_id=group_peer(F, o), device_id_type=MESH)


def meet(F):
    greet(F)
    pl.semaphore_wait(pltpu.get_barrier_semaphore(), F - 1)


class Move:
    def __init__(self, gather, F, src, dst, sems):
        self.src, self.dst = src, dst
        self.send, self.recv, self.own = sems
        self.S = src.shape[0]
        S, G = self.S, F // src.shape[0]
        self.dp, self.fr = lax.axis_index("dp"), lax.axis_index("frame")
        over = [a * G + self.fr // S for a in range(S)]
        back = [lax.rem(self.fr, G) * S + a for a in range(S)]
        self.to, self.sender = (over, back) if gather else (back, over)
        self.place = lax.rem(self.fr, S) if gather else self.fr // G

    def far(self, a):
        return pltpu.make_async_remote_copy(
            src_ref=self.src.at[a],
            dst_ref=self.dst.at[self.place],
            send_sem=self.send.at[a],
            recv_sem=self.recv.at[self.place],
            device_id=(self.dp, self.to[a]),
            device_id_type=MESH,
        )

    def near(self, a):
        return pltpu.make_async_copy(self.src.at[a], self.dst.at[self.place], self.own.at[a])

    def start(self):
        for a in range(self.S):

            @pl.when(self.to[a] != self.fr)
            def _():
                self.far(a).start()

            @pl.when(self.to[a] == self.fr)
            def _():
                self.near(a).start()

    def wait(self):
        for a in range(self.S):

            @pl.when(self.to[a] != self.fr)
            def _():
                self.far(a).wait_send()

            @pl.when(self.to[a] == self.fr)
            def _():
                self.near(a).wait()

            @pl.when(self.sender[a] != self.fr)
            def _():
                landed = self.dst.at[a]
                pltpu.make_async_copy(landed, landed, self.recv.at[a]).wait()


def move_sems(S):
    return [pltpu.SemaphoreType.DMA((S,))] * 3


def lanes_of(pair):
    return pl.ds(pl.multiple_of(pair * 128, 128), 128)


def mel_kernel(F, m_ref, e_ref, d_ref, h_ref, edge_send, edge_recv, edge_own, *sems):
    S = m_ref.shape[0]
    G = F // S
    dp, fr = lax.axis_index("dp"), lax.axis_index("frame")
    r = lax.rem(fr, G)
    meet(F)
    move = Move(True, F, m_ref, d_ref, sems)
    ends = []
    for a in range(S):
        last = (lax.rem(fr, S) == S - 1) & (fr + 1 < F)
        ends.append((a, 0, last, a * G + (fr + 1) // S))
        first = (lax.rem(fr, S) == 0) & (fr > 0)
        ends.append((a, 1, first, a * G + fr // S - 1))

    def far(a, k, to):
        return pltpu.make_async_remote_copy(
            src_ref=e_ref.at[a, k],
            dst_ref=h_ref.at[k],
            send_sem=edge_send.at[k, a],
            recv_sem=edge_recv.at[k],
            device_id=(dp, to),
            device_id_type=MESH,
        )

    def near(a, k):
        return pltpu.make_async_copy(e_ref.at[a, k], h_ref.at[k], edge_own.at[k])

    for a, k, holds, to in ends:

        @pl.when(holds & (to != fr))
        def _():
            far(a, k, to).start()

        @pl.when(holds & (to == fr))
        def _():
            near(a, k).start()

    move.start()
    for a, k, holds, to in ends:

        @pl.when(holds & (to != fr))
        def _():
            far(a, k, to).wait_send()

        @pl.when(holds & (to == fr))
        def _():
            near(a, k).wait()

    for k, wanted, sender in ((0, r > 0, r * S - 1), (1, r < G - 1, (r + 1) * S)):

        @pl.when(wanted & (sender != fr))
        def _():
            landed = h_ref.at[k]
            pltpu.make_async_copy(landed, landed, edge_recv.at[k]).wait()

    move.wait()


def gather_mel(pairs, F):
    S, piece, width = pairs.shape
    edges = jnp.stack([pairs[:, piece - 8 :], pairs[:, :8]], axis=1)
    far = pl.BlockSpec(memory_space=pl.ANY)
    return pl.pallas_call(
        functools.partial(mel_kernel, F),
        in_specs=[far, far],
        out_specs=[far, far],
        out_shape=[
            jax.ShapeDtypeStruct(pairs.shape, pairs.dtype),
            jax.ShapeDtypeStruct((2, 8, width), pairs.dtype),
        ],
        scratch_shapes=[
            pltpu.SemaphoreType.DMA((2, S)),
            pltpu.SemaphoreType.DMA((2,)),
            pltpu.SemaphoreType.DMA((2,)),
        ]
        + move_sems(S),
        compiler_params=pltpu.CompilerParams(
            collective_id=3, has_side_effects=True, vmem_limit_bytes=1 << 20
        ),
    )(pairs, edges)


def fwd_kernel(
    scale,
    hd,
    F,
    G,
    T,
    pairs,
    q_ref,
    k_own,
    v_own,
    c_ref,
    p_ref,
    o_ref,
    b_ref,
    k_all,
    v_all,
    d_ref,
    s_ref,
    k_buf,
    v_buf,
    send_sem,
    recv_sem,
    own_sem,
    out_sem,
    *sems,
):
    per = 128 // hd
    pair, i = pl.program_id(0), pl.program_id(1)
    rows = k_own.shape[0]
    both = ((k_own, k_buf), (v_own, v_buf))
    kept = ((k_buf, k_all), (v_buf, v_all))

    def own_copy(n, p):
        src, dst = both[n]
        return pltpu.make_async_copy(
            src.at[:, lanes_of(p)], dst.at[pl.ds(0, rows), lanes_of(p)], own_sem.at[n, p]
        )

    def keep(n, p):
        src, dst = kept[n]
        return pltpu.make_async_copy(
            src.at[:, lanes_of(p)], dst.at[:, lanes_of(p)], out_sem.at[n, p]
        )

    def copy_to(n, p, o):
        src, dst = both[n]
        return pltpu.make_async_remote_copy(
            src_ref=src.at[:, lanes_of(p)],
            dst_ref=dst.at[pl.ds((G - o) * rows, rows), lanes_of(p)],
            send_sem=send_sem.at[n, p, o - 1],
            recv_sem=recv_sem.at[n, p, o - 1],
            device_id=group_peer(G, o),
            device_id_type=MESH,
        )

    @pl.when((pair == 0) & (i == 0))
    def _():
        for p in range(pairs):
            for n in range(2):
                own_copy(n, p).start()
        meet(F)
        for p in range(pairs):
            for n in range(2):
                for o in range(1, G):
                    copy_to(n, p, o).start()
        Move(True, F, c_ref, d_ref, sems).start()

    @pl.when(i == 0)
    def _():
        for n in range(2):
            own_copy(n, pair).wait()
            for o in range(1, G):
                copy_to(n, pair, o).wait_recv()
            keep(n, pair).start()

    k = k_buf[:, lanes_of(pair)]
    vt = v_buf[:, lanes_of(pair)].T
    outs = []
    for h in range(per):
        q = q_ref[...]
        q = jnp.where(half_mask(q.shape, h, hd), q, jnp.zeros_like(q))
        s_ref[h] = lax.dot_general(k, q, (((1,), (1,)), ((), ())), preferred_element_type=F32)
    for h in range(per):
        s = s_ref[h]
        if rows != T:
            at = lax.rem(lax.broadcasted_iota(jnp.int32, s.shape, 0), rows)
            s = jnp.where(at < T, s, -1e30)
        m = jnp.max(s, axis=0, keepdims=True)
        e = jnp.exp((s - m) * scale)
        l = jnp.sum(e, axis=0, keepdims=True)
        p = (e * (1.0 / l)).astype(BF16)
        p_ref[h] = p
        outs.append(jnp.dot(vt[h * hd : (h + 1) * hd], p, preferred_element_type=F32))
    out = jnp.concatenate(outs, axis=0).T
    o_ref[...] = out
    b_ref[...] = out.astype(BF16)

    @pl.when((pair == pairs - 1) & (i == pl.num_programs(1) - 1))
    def _():
        for p in range(pairs):
            for n in range(2):
                keep(n, p).wait()
                for o in range(1, G):
                    copy_to(n, p, o).wait_send()
        Move(True, F, c_ref, d_ref, sems).wait()


def attn_fwd(q, k, v, slots, scale, heads, QB, F, T):
    G = F // slots.shape[0]
    R, D = q.shape
    N = k.shape[0] * G
    hd = D // heads
    per = 128 // hd
    pairs = D // 128
    far = pl.BlockSpec(memory_space=pl.ANY)
    sems = pltpu.SemaphoreType.DMA((2, pairs, G - 1))
    return pl.pallas_call(
        functools.partial(fwd_kernel, scale, hd, F, G, T, pairs),
        grid=(pairs, R // QB),
        in_specs=[pl.BlockSpec((QB, 128), lambda p, i: (i, p)), far, far, far],
        out_specs=[
            pl.BlockSpec((per, N, QB), lambda p, i: (p, 0, i)),
            pl.BlockSpec((QB, 128), lambda p, i: (i, p)),
            pl.BlockSpec((QB, 128), lambda p, i: (i, p)),
            far,
            far,
            far,
        ],
        out_shape=[
            jax.ShapeDtypeStruct((heads, N, R), BF16),
            jax.ShapeDtypeStruct((R, D), F32),
            jax.ShapeDtypeStruct((R, D), BF16),
            jax.ShapeDtypeStruct((N, D), BF16),
            jax.ShapeDtypeStruct((N, D), BF16),
            jax.ShapeDtypeStruct(slots.shape, slots.dtype),
        ],
        scratch_shapes=[
            pltpu.VMEM((per, N, QB), F32),
            pltpu.VMEM((N, D), BF16),
            pltpu.VMEM((N, D), BF16),
            sems,
            sems,
            pltpu.SemaphoreType.DMA((2, pairs)),
            pltpu.SemaphoreType.DMA((2, pairs)),
        ]
        + move_sems(slots.shape[0]),
        compiler_params=pltpu.CompilerParams(
            collective_id=1, has_side_effects=True, vmem_limit_bytes=60 << 20
        ),
    )(q, k, v, slots)


def bwd_kernel(
    scale,
    hd,
    F,
    G,
    pairs,
    q_ref,
    do_ref,
    o_ref,
    k_ref,
    v_ref,
    p_ref,
    y_ref,
    dq_ref,
    dk_ref,
    dv_ref,
    z_ref,
    dp_ref,
    kt_ref,
    acc_ref,
    got_ref,
    send_sem,
    recv_sem,
    *sems,
):
    per = 128 // hd
    pair, i = pl.program_id(0), pl.program_id(1)
    slot = lax.rem(pair, 2)
    rows = dk_ref.shape[0]

    def copy_to(n, p, o):
        return pltpu.make_async_remote_copy(
            src_ref=acc_ref.at[lax.rem(p, 2), n, pl.ds(o * rows, rows)],
            dst_ref=got_ref.at[p, n, o - 1],
            send_sem=send_sem.at[n, p, o - 1],
            recv_sem=recv_sem.at[n, p, o - 1],
            device_id=group_peer(G, o),
            device_id_type=MESH,
        )

    every = [(n, o) for n in range(2) for o in range(1, G)]

    @pl.when((pair == 0) & (i == 0))
    def _():
        meet(F)
        Move(False, F, y_ref, z_ref, sems).start()

    @pl.when((pair >= 2) & (i == 0))
    def _():
        for n, o in every:
            copy_to(n, pair - 2, o).wait_send()

    @pl.when(i == 0)
    def _():
        kt_ref[...] = k_ref[...].T
        acc_ref[slot] = jnp.zeros(acc_ref.shape[1:], F32)

    do = do_ref[...]
    q = q_ref[...]
    v = v_ref[...]
    prod = (do.astype(F32) * o_ref[...]).T
    for h in range(per):
        doh = jnp.where(half_mask(do.shape, h, hd), do, jnp.zeros_like(do))
        dp_ref[h] = lax.dot_general(v, doh, (((1,), (1,)), ((), ())), preferred_element_type=F32)
    dqs = []
    for h in range(per):
        doh = jnp.where(half_mask(do.shape, h, hd), do, jnp.zeros_like(do))
        qh = jnp.where(half_mask(q.shape, h, hd), q, jnp.zeros_like(q))
        delta = jnp.sum(prod[h * hd : (h + 1) * hd], axis=0, keepdims=True)
        p = p_ref[h]
        ds = (p.astype(F32) * (dp_ref[h] - delta)).astype(BF16)
        acc_ref[slot, 1] += jnp.dot(p, doh, preferred_element_type=F32)
        acc_ref[slot, 0] += jnp.dot(ds, qh, preferred_element_type=F32)
        dqs.append(jnp.dot(kt_ref[h * hd : (h + 1) * hd], ds, preferred_element_type=F32))
    dq_ref[...] = (jnp.concatenate(dqs, axis=0) * scale).T.astype(BF16)

    def finish(p):
        for n, o in every:
            copy_to(n, p, o).wait_recv()
        for n, out, factor in ((0, dk_ref, scale), (1, dv_ref, 1.0)):
            total = acc_ref[lax.rem(p, 2), n, pl.ds(0, rows)]
            for o in range(1, G):
                total = total + got_ref[p, n, o - 1]
            out[:, lanes_of(p)] = (total * factor).astype(BF16)

    ends = i == pl.num_programs(1) - 1

    @pl.when(ends & (pair >= 1))
    def _():
        finish(pair - 1)

    @pl.when(ends)
    def _():
        for n, o in every:
            copy_to(n, pair, o).start()

    @pl.when(ends & (pair == pairs - 1))
    def _():
        finish(pair)
        for p in range(max(pairs - 2, 0), pairs):
            for n, o in every:
                copy_to(n, p, o).wait_send()
        Move(False, F, y_ref, z_ref, sems).wait()


def attn_bwd(q, do, o, k, v, p, pieces, scale, heads, QB, F):
    G = F // pieces.shape[0]
    far = pl.BlockSpec(memory_space=pl.ANY)
    R, D = q.shape
    N = k.shape[0]
    hd = D // heads
    per = 128 // hd
    pairs = D // 128
    row = pl.BlockSpec((QB, 128), lambda p, i: (i, p))
    key = pl.BlockSpec((N, 128), lambda p, i: (0, p))
    near = pl.BlockSpec(memory_space=pltpu.VMEM)
    sems = pltpu.SemaphoreType.DMA((2, pairs, G - 1))
    own = jax.ShapeDtypeStruct((N // G, D), BF16)
    return pl.pallas_call(
        functools.partial(bwd_kernel, scale, hd, F, G, pairs),
        grid=(pairs, R // QB),
        in_specs=[row, row, row, key, key, pl.BlockSpec((per, N, QB), lambda p, i: (p, 0, i)), far],
        out_specs=[row, near, near, far],
        out_shape=[
            jax.ShapeDtypeStruct((R, D), BF16),
            own,
            own,
            jax.ShapeDtypeStruct(pieces.shape, pieces.dtype),
        ],
        scratch_shapes=[
            pltpu.VMEM((per, N, QB), F32),
            pltpu.VMEM((128, N), BF16),
            pltpu.VMEM((2, 2, N, 128), F32),
            pltpu.VMEM((pairs, 2, G - 1, N // G, 128), F32),
            sems,
            sems,
        ]
        + move_sems(pieces.shape[0]),
        compiler_params=pltpu.CompilerParams(
            collective_id=2, has_side_effects=True, vmem_limit_bytes=60 << 20
        ),
    )(q, do, o, k, v, p, pieces)


TILE = 512
LAG = 3
AHEAD = 2


def pick(c, values):
    out = values[0]
    for n in range(1, len(values)):
        if values[n] != values[n - 1]:
            out = jnp.where(c >= n, values[n], out)
    return out


class Rest:
    FIRST = 5

    def __init__(self, G, T, taps, m_ref, t_ref, w_ref, data, scratch, sems):
        self.m, self.t, self.w = m_ref, t_ref, w_ref
        self.data = data
        self.ext, self.edge, self.halo, self.sg, self.y0, self.y1, self.y2 = scratch
        self.send, self.recv = sems
        self.G, self.T, self.taps = G, T, taps
        self.R = self.sg.shape[0]
        self.row = lax.rem(lax.axis_index("frame"), G)
        self.size = 256 if self.R % 256 == 0 else 128
        self.token_blocks = [(a, min(a + 256, T)) for a in range(0, T, 256)]
        self.edges_at = self.FIRST + len(self.token_blocks)
        self.halo_at = self.edges_at + 2
        self.stem_at = self.halo_at + 1
        self.mel_at = self.stem_at + self.R // self.size
        self.weights_at = self.mel_at + 1
        self.halo[...] = jnp.zeros_like(self.halo)

    def due(self, name):
        if name in ("reduce", "stem_linear", "stem_taps"):
            return self.stem_at
        if name in ("columns", "second_gain", "second_shift"):
            return self.weights_at
        return self.FIRST

    def tokens(self, n):
        a, b = self.token_blocks[n]
        q, k, v, conv, base = self.taps
        data, rows = self.data, pl.ds(a, b - a)
        dy = (
            dot_t(self.m[q, rows], data["query"][...])
            + dot_t(self.m[k, rows], data["key"][...])
            + dot_t(self.m[v, rows], data["value"][...])
        )
        xhat, r = norm_parts(data["stream"][rows])
        dh = dy * data["gain"][...]
        inner = r * (
            dh
            - jnp.mean(dh, axis=-1, keepdims=True)
            - xhat * jnp.mean(dh * xhat, axis=-1, keepdims=True)
        )
        self.t[base + 1 : base + 2] += jnp.sum(dy * xhat, axis=0, keepdims=True)
        self.t[base + 2 : base + 3] += jnp.sum(dy, axis=0, keepdims=True)
        grad = gelu_slope(data["conv_linear"][rows]) * (data["mixed"][rows] + inner)
        grad = grad.astype(BF16)
        self.m[conv, rows] = grad
        self.ext[rows] = grad
        if n == 0:
            self.edge[1] = grad[:16]
            self.ext[pl.ds(self.R, 16)] = grad[:16]
        if b == self.T:
            self.edge[0] = grad[b - a - 16 :]

    def edge_copy(self, n):
        return pltpu.make_async_remote_copy(
            src_ref=self.edge.at[n],
            dst_ref=self.halo.at[n],
            send_sem=self.send.at[n],
            recv_sem=self.recv.at[n],
            device_id=group_peer(self.G, 1 if n == 0 else self.G - 1),
            device_id_type=MESH,
        )

    def has(self, n):
        return self.row < self.G - 1 if n == 0 else self.row > 0

    def send_edges(self):
        for n in range(2):

            @pl.when(self.has(n))
            def _():
                self.edge_copy(n).start()

    def fill_halo(self):
        for n in range(2):

            @pl.when(self.has(1 - n))
            def _():
                landed = self.halo.at[n]
                pltpu.make_async_copy(landed, landed, self.recv.at[n]).wait()

        at = self.T // 16 * 16
        rows = pl.ds(at, self.R - at)
        own = self.ext[rows].astype(F32)
        place = lax.broadcasted_iota(jnp.int32, own.shape, 0) + at
        before = self.halo[0].astype(F32)[15:16]
        after = self.halo[1].astype(F32)[:1]
        own = jnp.where(place < self.T, own, 0.0)
        own = jnp.where(place == self.T, after, own)
        own = jnp.where(place == self.R - 1, before, own)
        self.ext[rows] = own.astype(BF16)

    def stem(self, n):
        data, a = self.data, n * self.size
        D = self.ext.shape[1]
        rows = pl.ds(a, self.size)
        pair = dot_t(self.ext[rows], data["reduce"][pl.ds(D, 2 * D)])
        third = dot_t(self.ext[pl.ds(a, self.size + 16)], data["reduce"][pl.ds(0, D)])
        third = third[1 : self.size + 1]
        active = jnp.concatenate([pair[:, :D], pair[:, D:] + third], axis=1)
        place = lax.broadcasted_iota(jnp.int32, active.shape, 0) + a
        high = self.T + jnp.where(self.row < self.G - 1, 1, 0)
        low = self.R - jnp.where(self.row > 0, 1, 0)
        grad = gelu_slope(data["stem_linear"][rows]) * active
        grad = jnp.where((place < high) | (place >= low), grad, 0.0).astype(BF16)
        self.sg[rows] = grad
        self.y0[rows] = dot_t(grad, data["stem_taps"][0])
        y1 = dot_t(grad, data["stem_taps"][1])
        self.y1[pl.ds(a + 8, self.size)] = y1
        if a + self.size == self.R:
            self.y1[pl.ds(0, 8)] = y1[self.size - 8 :]
        self.y2[rows] = dot_t(grad, data["stem_taps"][2])

    def mel(self, out):
        T = self.T
        total = self.y0[pl.ds(0, T)] + self.y1[pl.ds(7, T)] + self.y2[pl.ds(1, T)]
        n = out.shape[1]
        for j in range(out.shape[0]):
            out[j] = total[j * n : (j + 1) * n]

    def weights(self):
        base = self.taps[-1]
        D = self.ext.shape[1]
        own = self.sg[pl.ds(0, self.T)]
        wide = outer(self.data["columns"][pl.ds(0, self.T)], own)
        mels = wide.shape[0] // 4
        sums = dot(jnp.ones((16, self.T), BF16), own)[:1]
        self.w[self.w.shape[0] - 1, pl.ds(0, 3 * mels)] = (
            wide[: 3 * mels, :D] + wide[mels:, D:]
        ).astype(BF16)
        self.t[base : base + 1] = sums[:, :D] + sums[:, D:]
        self.t[base + 3 : base + 4] = self.data["second_gain"][...]
        self.t[base + 4 : base + 5] = self.data["second_shift"][...]

    def step(self, t, out):
        todo = [(self.FIRST + n, functools.partial(self.tokens, n)) for n in range(len(self.token_blocks))]
        todo.append((self.edges_at, self.send_edges))
        todo.append((self.halo_at, self.fill_halo))
        todo += [
            (self.stem_at + n, functools.partial(self.stem, n)) for n in range(self.R // self.size)
        ]
        todo.append((self.mel_at, functools.partial(self.mel, out)))
        todo.append((self.weights_at, self.weights))
        for at, work in todo:
            pl.when(t == at)(work)

    def drain(self):
        for n in range(2):

            @pl.when(self.has(n))
            def _():
                self.edge_copy(n).wait_send()


REST = (
    "query",
    "key",
    "value",
    "stream",
    "gain",
    "mixed",
    "conv_linear",
    "reduce",
    "stem_linear",
    "stem_taps",
    "columns",
    "second_gain",
    "second_shift",
)


def sum_kernel(sizes, F, used, plan, *refs):
    places, left_at, right_at, lefts, rights, n_in, n_out, taps, T = plan
    extra = len(REST)
    in_refs, rest_refs = refs[: n_in - extra], refs[n_in - extra : n_in]
    g_refs, slot_ref = refs[n_in : n_in + n_out - 1], refs[n_in + n_out - 1]
    refs = refs[n_in + n_out :]
    l_ref, m_ref, t_ref, w_ref, s_ref, r0, r1, r2, r3 = refs[:9]
    kept, work = refs[9 : 9 + extra], refs[9 + extra : 16 + extra]
    piece_ref, send_sem, recv_sem, load_sem, out_sem, edge_send, edge_recv, *sems = refs[16 + extra :]
    t_ref[...] = jnp.zeros_like(t_ref)
    w_ref[len(places) - 1] = jnp.zeros(w_ref.shape[1:], BF16)
    G = F // slot_ref.shape[0]
    rest = Rest(
        G, T, taps, m_ref, t_ref, w_ref, dict(zip(REST, kept)), work, (edge_send, edge_recv)
    )
    recv = (r0, r1, r2, r3)
    chunks = len(places)
    Y = sizes[2]
    dp = lax.axis_index("dp")
    fr = lax.axis_index("frame")
    z = dp // Y
    y = lax.rem(dp, Y)
    x = fr // 2
    core = lax.rem(fr, 2)
    first = core == 0
    me = (core, jnp.where(first, x, y), jnp.where(first, y, x), z)

    loads, due = [], []
    for buf, sources, at in ((l_ref, lefts, left_at), (m_ref, rights, right_at)):
        for n, (which, col) in enumerate(sources):
            if which is None:
                continue
            src = in_refs[which].at[pl.ds(0, T), pl.ds(col, TILE)]
            loads.append(pltpu.make_async_copy(src, buf.at[n], load_sem.at[len(loads)]))
            first_use = at.index(n)
            due.append(min(first_use, rest.FIRST) if at is right_at and n in taps[:3] else first_use)
    for name, src, dst in zip(REST, rest_refs, kept):
        loads.append(pltpu.make_async_copy(src, dst, load_sem.at[len(loads)]))
        due.append(rest.due(name))
    for n in sorted(range(len(loads)), key=lambda n: (due[n], n)):
        loads[n].start()

    def device(kind, p):
        if kind == 0:
            return (dp, x * 2 + p)
        if kind == 3:
            return (p * Y + y, fr)
        along_x = first if kind == 1 else jnp.logical_not(first)
        return (z * Y + jnp.where(along_x, y, p), jnp.where(along_x, p, x) * 2 + core)

    def peer(k, o):
        return lax.rem(me[k] + o, sizes[k])

    pairs = [(k, o) for k in range(4) for o in range(1, sizes[k])]
    barrier = pltpu.get_barrier_semaphore()
    for k, o in pairs:
        pl.semaphore_signal(barrier, inc=1, device_id=device(k, peer(k, o)), device_id_type=MESH)
    greet(F)
    pl.semaphore_wait(barrier, len(pairs) + F - 1)
    move = Move(False, F, piece_ref, slot_ref, sems)

    cut = [TILE]
    for k in range(4):
        cut.append(cut[-1] // sizes[k])
    split = cut[4] % 16 == 0
    if not split:
        cut[4] = cut[3]

    def start_of(level):
        at = 0
        for k in range(level):
            if k < 3 or split:
                at = at + me[k] * cut[k + 1]
        return pl.multiple_of(at, 16) if level else 0

    def scatter_copy(c, k, o):
        p = peer(k, o)
        at = start_of(k)
        if k < 3 or split:
            at = pl.multiple_of(at + p * cut[k + 1], 16)
        return pltpu.make_async_remote_copy(
            src_ref=w_ref.at[c, pl.ds(at, cut[k + 1])],
            dst_ref=recv[k].at[c, o - 1],
            send_sem=send_sem.at[c, k, o - 1],
            recv_sem=recv_sem.at[c, k, o - 1],
            device_id=device(k, p),
            device_id_type=MESH,
        )

    def gather_copy(c, k, o):
        here = s_ref.at[c, pl.ds(start_of(k + 1), cut[k + 1])]
        return pltpu.make_async_remote_copy(
            src_ref=here,
            dst_ref=here,
            send_sem=send_sem.at[c, 4 + k, o - 1],
            recv_sem=recv_sem.at[c, 4 + k, o - 1],
            device_id=device(k, peer(k, o)),
            device_id_type=MESH,
        )

    def out_copy(c):
        which, row, col = places[c]
        dst = g_refs[which].at[pl.ds(row, TILE), pl.ds(col, TILE)]
        return pltpu.make_async_copy(s_ref.at[c], dst, out_sem.at[c])

    def add(c, k):
        at = start_of(k + 1)
        dst = w_ref if k < 3 else s_ref
        step = math.gcd(cut[k + 1], 64)

        def body(i, _):
            r = pl.multiple_of(at + i * step, 16)
            total = w_ref[c, pl.ds(r, step)].astype(F32)
            for o in range(1, sizes[k]):
                total = total + recv[k][
                    c, o - 1, pl.ds(pl.multiple_of(i * step, 16), step)
                ].astype(F32)
            dst[c, pl.ds(r, step)] = total.astype(BF16)
            return 0

        lax.fori_loop(0, cut[k + 1] // step, body, 0)

    stages = [("s", k) for k in range(4)] + [("g", k) for k in (3, 2, 1, 0) if k < 3 or split]
    copies = {"s": scatter_copy, "g": gather_copy}

    def finish(c, n):
        kind, k = stages[n]
        for o in range(1, sizes[k]):
            copies[kind](c, k, o).wait_recv()
        if kind == "s":
            add(c, k)
        if n + 1 < len(stages):
            kind, k = stages[n + 1]
            for o in range(1, sizes[k]):
                copies[kind](c, k, o).start()

    turns = [AHEAD]
    for n in range(1, len(stages)):
        turns.append(turns[-1] + (LAG if stages[n][1] else LAG - 1))
    last = turns[-1]

    def turn(t, _):
        for n in range(len(loads)):

            @pl.when(t == due[n])
            def _():
                loads[n].wait()

        @pl.when(t < chunks - 1)
        def _():
            left = l_ref[pick(t, left_at)]
            right = m_ref[pick(t, right_at)]
            w_ref[t] = outer(left, right).astype(BF16)
            ones = jnp.ones((16, T), BF16)
            t_ref[pl.ds(pick(t, right_at), 1)] = dot(ones, right)[:1]

        @pl.when(t == rest.weights_at)
        def _():
            move.start()

        rest.step(t, piece_ref)

        @pl.when(t == chunks - 1)
        def _():
            w_ref[chunks - 1, pl.ds(used, t_ref.shape[0])] = t_ref[...].astype(BF16)

        @pl.when((t >= 1) & (t <= chunks))
        def _():
            for o in range(1, sizes[0]):
                scatter_copy(t - 1, 0, o).start()

        for n in range(len(stages) - 1, -1, -1):
            c = t - turns[n]

            @pl.when((c >= 0) & (c < chunks))
            def _():
                finish(c, n)

        for c in range(chunks):

            @pl.when(t == c + last)
            def _():
                out_copy(c).start()

        return 0

    lax.fori_loop(0, chunks + last, turn, 0)

    def drain(c, _):
        for kind, k in stages:
            for o in range(1, sizes[k]):
                copies[kind](c, k, o).wait_send()
        return 0

    lax.fori_loop(0, chunks, drain, 0)
    move.wait()
    rest.drain()
    for c in range(chunks):
        out_copy(c).wait()


def sum_everywhere(products, rest, taps, used, S, F, sizes, cid):
    arrays, lefts, rights = [], [], []
    places, left_at, right_at, shapes = [], [], [], []

    def slots_of(pieces, slots):
        found = []
        for array, width in pieces:
            which = None
            if array is not None:
                which = next((n for n, a in enumerate(arrays) if a is array), None)
                if which is None:
                    which = len(arrays)
                    arrays.append(array)
            for col in range(0, width, TILE):
                if (which, col) not in slots:
                    slots.append((which, col))
                found.append(slots.index((which, col)))
        return found

    for n, (left, right) in enumerate(products):
        a, b = slots_of(left, lefts), slots_of(right, rights)
        shapes.append((len(a) * TILE, len(b) * TILE))
        for i, u in enumerate(a):
            for j, v in enumerate(b):
                places.append((n, i * TILE, j * TILE))
                left_at.append(u)
                right_at.append(v)
    places.append((len(products), 0, 0))
    shapes.append((TILE, TILE))
    T = min(a.shape[0] for a in arrays)
    R = rest["stem_linear"].shape[0]
    mels = rest["columns"].shape[1] // 4
    chunks = len(places)
    cut = [TILE]
    for n in sizes:
        cut.append(cut[-1] // n)
    if cut[4] % 16:
        cut[4] = cut[3]
    most = max(sizes) - 1
    spec = pl.BlockSpec(memory_space=pl.ANY)
    sums = len(rights) + 5
    sums += -sums % 16
    slots = jax.ShapeDtypeStruct((S, T // S, 2 * mels), F32)
    taps = tuple(right_at[n] for n in taps) + (len(rights),)
    plan = (
        places,
        left_at,
        right_at,
        lefts,
        rights,
        len(arrays) + len(REST),
        len(shapes) + 1,
        taps,
        T,
    )
    return pl.pallas_call(
        functools.partial(sum_kernel, sizes, F, used, plan),
        in_specs=[spec] * (len(arrays) + len(REST)),
        out_specs=[spec] * (len(shapes) + 1),
        out_shape=[jax.ShapeDtypeStruct(v, BF16) for v in shapes] + [slots],
        scratch_shapes=[
            pltpu.VMEM((len(lefts), T, TILE), BF16),
            pltpu.VMEM((len(rights), T, TILE), BF16),
            pltpu.VMEM((sums, TILE), F32),
        ]
        + [pltpu.VMEM((chunks, TILE, TILE), BF16)] * 2
        + [pltpu.VMEM((chunks, sizes[k] - 1, cut[k + 1], TILE), BF16) for k in range(4)]
        + [pltpu.VMEM(rest[name].shape, rest[name].dtype) for name in REST]
        + [
            pltpu.VMEM((R + 16, TILE), BF16),
            pltpu.VMEM((2, 16, TILE), BF16),
            pltpu.VMEM((2, 16, TILE), BF16),
            pltpu.VMEM((R, 2 * TILE), BF16),
            pltpu.VMEM((R, 2 * mels), F32),
            pltpu.VMEM((R + 8, 2 * mels), F32),
            pltpu.VMEM((R, 2 * mels), F32),
            pltpu.VMEM(slots.shape, F32),
        ]
        + [
            pltpu.SemaphoreType.DMA((chunks, 8, most)),
            pltpu.SemaphoreType.DMA((chunks, 8, most)),
            pltpu.SemaphoreType.DMA((len(lefts) + len(rights) + len(REST),)),
            pltpu.SemaphoreType.DMA((chunks,)),
            pltpu.SemaphoreType.DMA((2,)),
            pltpu.SemaphoreType.DMA((2,)),
        ]
        + move_sems(S),
        compiler_params=pltpu.CompilerParams(
            collective_id=cid, has_side_effects=True, vmem_limit_bytes=67043328
        ),
    )(*arrays, *[rest[name] for name in REST])


def widen_kernel(parts, count, *refs):
    ins, outs = refs[:count], refs[count : 2 * count + 1]
    b_ref, f_ref, load_sem, out_sem = refs[2 * count + 1 :]
    loads, stores = [], []
    for n, (which, row, col, places) in enumerate(parts):
        rows = pl.ds(row, TILE)
        cols = pl.ds(col, TILE)
        loads.append(
            pltpu.make_async_copy(ins[which].at[rows, cols], b_ref.at[n], load_sem.at[n])
        )
        here = []
        for out, at, first, size in places:
            target = outs[out].at[pl.ds(at, size), cols]
            source = f_ref.at[n, pl.ds(first, size)]
            here.append(pltpu.make_async_copy(source, target, out_sem.at[n, len(here)]))
        stores.append(here)
    for load in loads:
        load.start()
    for n, load in enumerate(loads):
        load.wait()

        def body(i, _):
            rows = pl.ds(pl.multiple_of(i * 64, 64), 64)
            f_ref[n, rows] = b_ref[n, rows].astype(F32)
            return 0

        lax.fori_loop(0, TILE // 64, body, 0)
        for store in stores[n]:
            store.start()
    for here in stores:
        for store in here:
            store.wait()


def widen(arrays, used, sums):
    parts = []
    last = len(arrays) - 1
    for n, a in enumerate(arrays):
        for row in range(0, a.shape[0], TILE):
            for col in range(0, a.shape[1], TILE):
                places = [(n, row, 0, TILE)]
                if n == last:
                    places = [(n, 0, 0, used[0]), (n + 1, 0, used[1], sums)]
                parts.append((n, row, col, places))
    shapes = [a.shape for a in arrays[:-1]] + [(used[0], TILE), (sums, TILE)]
    far = pl.BlockSpec(memory_space=pl.ANY)
    return pl.pallas_call(
        functools.partial(widen_kernel, parts, len(arrays)),
        in_specs=[far] * len(arrays),
        out_specs=[far] * len(shapes),
        out_shape=[jax.ShapeDtypeStruct(v, F32) for v in shapes],
        scratch_shapes=[
            pltpu.VMEM((len(parts), TILE, TILE), BF16),
            pltpu.VMEM((len(parts), TILE, TILE), F32),
            pltpu.SemaphoreType.DMA((len(parts),)),
            pltpu.SemaphoreType.DMA((len(parts), 2)),
        ],
        compiler_params=pltpu.CompilerParams(vmem_limit_bytes=67043328),
    )(*arrays)


def on_device(
    mel_frames,
    window_count,
    stem_weight,
    stem_bias,
    reduce_weight,
    reduce_bias,
    first_gain,
    first_shift,
    query_weight,
    query_bias,
    key_weight,
    value_weight,
    value_bias,
    output_weight,
    output_bias,
    second_gain,
    second_shift,
    hidden_weight,
    hidden_bias,
    return_weight,
    return_bias,
    cotangent,
):
    S, piece_frames, mels = mel_frames.shape
    piece = cotangent.shape[1]
    D = stem_weight.shape[2]
    hd = D // HEADS
    scale = hd ** (-0.5)
    F = lax.axis_size("frame")
    G = F // S
    T = S * piece
    R = -(-(T + 2) // 128) * 128
    f = lax.axis_index("frame")
    s = f // G
    r = f % G
    alive = s < window_count[0]

    own, beside = gather_mel(mel_frames.reshape(S, piece, 2 * mels), F)
    before = jnp.where(r > 0, beside[0, -1:], jnp.zeros((1, 2 * mels), BF16))
    after = jnp.where(r < G - 1, beside[1, :1], jnp.zeros((1, 2 * mels), BF16))
    gap = jnp.zeros((R - T - 2, 2 * mels), BF16)
    mel = jnp.concatenate([own.reshape(T, 2 * mels), after, gap, before], axis=0)
    odd_before = jnp.roll(mel[:, mels:], 1, axis=0)
    even_after = jnp.roll(mel[:, :mels], -1, axis=0)
    columns = jnp.concatenate([odd_before, mel, even_after], axis=1)
    stem_matrix = stem_weight.reshape(3 * mels, D)
    gap = jnp.zeros((mels, D), BF16)
    stem_pair = jnp.concatenate(
        [
            jnp.concatenate([stem_matrix, gap], axis=0),
            jnp.concatenate([gap, stem_matrix], axis=0),
        ],
        axis=1,
    )
    stem_bias2 = jnp.concatenate([stem_bias, stem_bias])
    stem_linear = dot(columns, stem_pair) + stem_bias2
    row = lax.broadcasted_iota(jnp.int32, (R, 1), 0)
    valid = (row < T) | ((row == T) & (r < G - 1)) | ((row == R - 1) & (r > 0))
    stem_active = jnp.where(valid, gelu(stem_linear), 0.0).astype(BF16)

    odd_active_before = jnp.roll(stem_active[:, D:], 1, axis=0)[:T]
    conv_columns = jnp.concatenate([odd_active_before, stem_active[:T]], axis=1)
    reduce_matrix = reduce_weight.reshape(3 * D, D)
    conv_linear = dot(conv_columns, reduce_matrix) + reduce_bias
    stream = gelu(conv_linear) + positions_of(r * T, T, D)
    xhat1, r1 = norm_parts(stream)
    first_normed = (xhat1 * first_gain + first_shift).astype(BF16)
    tail = ((0, R - T), (0, 0))
    query_ext = (dot(jnp.pad(first_normed, tail), query_weight) + query_bias).astype(BF16)
    key = dot(first_normed, key_weight).astype(BF16)
    value = (dot(first_normed, value_weight) + value_bias).astype(BF16)
    key = jnp.pad(key, ((0, -T % 16), (0, 0)))
    value = jnp.pad(value, ((0, -T % 16), (0, 0)))
    block = 256 if R % 256 == 0 else 128
    probs, attended_wide, attended, key_all, value_all, cot = attn_fwd(
        query_ext, key, value, cotangent, scale, HEADS, block, F, T
    )
    cot = cot.reshape(T, D)
    cot = jnp.where(alive, cot, jnp.zeros_like(cot))
    mixed = stream + dot(attended[:T], output_weight) + output_bias
    xhat2, r2 = norm_parts(mixed)
    second_normed = (xhat2 * second_gain + second_shift).astype(BF16)
    hidden_linear = dot(second_normed, hidden_weight) + hidden_bias
    hidden_cdf, hidden_pdf = phi_parts(hidden_linear)
    hidden_active = (hidden_linear * hidden_cdf).astype(BF16)
    layer = mixed + dot(hidden_active, return_weight) + return_bias
    layer = jnp.where(alive, layer, 0.0).astype(BF16)

    slope = hidden_cdf + hidden_linear * hidden_pdf
    hidden_grad = (slope * dot_t(cot, return_weight)).astype(BF16)
    inner, second_gain_grad, second_shift_grad = norm_pull(
        xhat2, r2, second_gain, dot_t(hidden_grad, hidden_weight)
    )
    mixed_grad = cot.astype(F32) + inner
    branch_grad = mixed_grad.astype(BF16)

    attended_grad = dot_t(jnp.pad(branch_grad, tail), output_weight).astype(BF16)
    query_wide, key_grad, value_grad, layer_output = attn_bwd(
        query_ext,
        attended_grad,
        attended_wide,
        key_all,
        value_all,
        probs,
        layer.reshape(S, piece, D),
        scale,
        HEADS,
        block,
        F,
    )
    key_grad, value_grad = key_grad[:T], value_grad[:T]
    sizes = (2, F // 2, F // 2, lax.axis_size("dp") // (F // 2))
    used = 3 * mels + -3 * mels % 16
    none = jnp.zeros((mels, 2 * D), BF16)
    taps = [
        stem_pair[mels : 3 * mels],
        jnp.concatenate([stem_pair[3 * mels :], none], axis=0),
        jnp.concatenate([none, stem_pair[:mels]], axis=0),
    ]
    rest = {
        "query": query_weight,
        "key": key_weight,
        "value": value_weight,
        "stream": stream,
        "gain": first_gain.reshape(1, D),
        "mixed": mixed_grad,
        "conv_linear": conv_linear,
        "reduce": reduce_matrix,
        "stem_linear": stem_linear,
        "stem_taps": jnp.stack(taps),
        "columns": columns,
        "second_gain": second_gain_grad.reshape(1, D),
        "second_shift": second_shift_grad.reshape(1, D),
    }
    FF = hidden_weight.shape[1]
    wide = FF // D
    one = [(first_normed, D)]
    *terms, mel_slots = sum_everywhere(
        [
            ([(hidden_active, FF)], [(cot, D)]),
            ([(second_normed, D)], [(hidden_grad, FF)]),
            ([(attended, D)], [(branch_grad, D)]),
            (one, [(query_wide, D)]),
            (one, [(key_grad, D)]),
            (one, [(value_grad, D)]),
            ([(odd_active_before, D), (stem_active, 2 * D)], [(None, D)]),
        ],
        rest,
        (2 * wide + 1, 2 * wide + 2, 2 * wide + 3, 2 * wide + 4),
        used,
        S,
        F,
        sizes,
        0,
    )
    mel_gradient = mel_slots.reshape(S, piece_frames, mels)
    rows = wide + 11
    rows += -rows % 16
    return_w, hidden_w, output_w, query_w, key_w, value_w, reduce_w, stem_w, sums = widen(
        terms, (3 * mels, used), rows
    )
    small = wide + 6
    return (
        layer_output,
        mel_gradient,
        stem_w.reshape(3, mels, D),
        sums[small],
        reduce_w.reshape(3, D, D),
        sums[wide + 5],
        sums[small + 1],
        sums[small + 2],
        query_w,
        sums[wide + 2],
        key_w,
        value_w,
        sums[wide + 4],
        output_w,
        sums[wide + 1],
        sums[small + 3],
        sums[small + 4],
        hidden_w,
        sums[1 : wide + 1].reshape(FF),
        return_w,
        sums[0],
    )


def solution(mesh):
    cut = P("dp", "frame", None)
    return jax.shard_map(
        on_device,
        mesh=mesh,
        in_specs=(cut, P("dp")) + (P(),) * 19 + (cut,),
        out_specs=(cut, cut) + (P(),) * 19,
        check_vma=False,
    )
```

```python
import functools
import math

import jax
import jax.numpy as jnp
from jax import lax
from jax.experimental import pallas as pl
from jax.experimental.pallas import tpu as pltpu
from jax.sharding import PartitionSpec as P

HEADS = 8
EPS = 1e-05
F32 = jnp.float32
BF16 = jnp.bfloat16
PHI_SLOPE = 0.28
PHI_POLY = (
    0.1167294156016242,
    0.06622785593379492,
    0.27197610469464767,
    -0.24067367858721922,
    0.3920693507793772,
    -0.10632905941542621,
)


def phi_parts(v):
    size = jnp.abs(v)
    t = 1.0 / (1.0 + PHI_SLOPE * size)
    bell = jnp.exp(-0.5 * v * v)
    poly = PHI_POLY[5]
    for c in PHI_POLY[4::-1]:
        poly = poly * t + c
    tail = poly * t * bell
    cdf = jnp.where(v >= 0, 1.0 - tail, tail)
    return cdf, bell * (1.0 / math.sqrt(2.0 * math.pi))


def gelu(v):
    cdf, _ = phi_parts(v)
    return v * cdf


def gelu_slope(v):
    cdf, pdf = phi_parts(v)
    return cdf + v * pdf


def dot(left, right):
    return jnp.dot(left, right, preferred_element_type=F32)


def dot_t(left, right):
    return lax.dot_general(left, right, (((1,), (1,)), ((), ())), preferred_element_type=F32)


def outer(left, right):
    return lax.dot_general(left, right, (((0,), (0,)), ((), ())), preferred_element_type=F32)


def column_total(x):
    return jnp.sum(x.astype(F32), axis=0)


def norm_parts(x):
    centred = x - jnp.mean(x, axis=-1, keepdims=True)
    r = lax.rsqrt(jnp.mean(centred * centred, axis=-1, keepdims=True) + EPS)
    return centred * r, r


def norm_pull(xhat, r, gain, dy):
    dh = dy * gain
    inner = r * (
        dh
        - jnp.mean(dh, axis=-1, keepdims=True)
        - xhat * jnp.mean(dh * xhat, axis=-1, keepdims=True)
    )
    return inner, column_total(dy * xhat), column_total(dy)


def positions_of(first, count, width):
    half = width // 2
    step = math.log(10000.0) / (half - 1)
    rate = jnp.exp(-step * jnp.arange(half, dtype=F32))[None, :]
    fine = math.gcd(count, 16)
    coarse = count // fine
    a = (first + fine * jnp.arange(coarse, dtype=jnp.int32)).astype(F32)[:, None] * rate
    b = jnp.arange(fine, dtype=jnp.int32).astype(F32)[:, None] * rate
    sa, ca = jnp.sin(a)[:, None, :], jnp.cos(a)[:, None, :]
    sb, cb = jnp.sin(b)[None, :, :], jnp.cos(b)[None, :, :]
    both = jnp.concatenate([sa * cb + ca * sb, ca * cb - sa * sb], axis=2)
    return both.reshape(count, width)


def half_mask(shape, h, hd):
    lane = lax.broadcasted_iota(jnp.int32, shape, 1)
    return (lane >= h*hd) & (lane < (h+1)*hd)

MESH = pl.DeviceIdType.MESH


def group_peer(G, o):
    fr = lax.axis_index("frame")
    return (lax.axis_index("dp"), fr // G * G + lax.rem(lax.rem(fr, G) + o, G))


def greet(F):
    barrier = pltpu.get_barrier_semaphore()
    for o in range(1, F):
        pl.semaphore_signal(barrier, inc=1, device_id=group_peer(F, o), device_id_type=MESH)


def meet(F):
    greet(F)
    pl.semaphore_wait(pltpu.get_barrier_semaphore(), F - 1)


class Move:
    def __init__(self, gather, F, src, dst, sems):
        self.src, self.dst = src, dst
        self.send, self.recv, self.own = sems
        self.S = src.shape[0]
        S, G = self.S, F // src.shape[0]
        self.dp, self.fr = lax.axis_index("dp"), lax.axis_index("frame")
        over = [a * G + self.fr // S for a in range(S)]
        back = [lax.rem(self.fr, G) * S + a for a in range(S)]
        self.to, self.sender = (over, back) if gather else (back, over)
        self.place = lax.rem(self.fr, S) if gather else self.fr // G

    def far(self, a):
        return pltpu.make_async_remote_copy(
            src_ref=self.src.at[a],
            dst_ref=self.dst.at[self.place],
            send_sem=self.send.at[a],
            recv_sem=self.recv.at[self.place],
            device_id=(self.dp, self.to[a]),
            device_id_type=MESH,
        )

    def near(self, a):
        return pltpu.make_async_copy(self.src.at[a], self.dst.at[self.place], self.own.at[a])

    def start(self):
        for a in range(self.S):

            @pl.when(self.to[a] != self.fr)
            def _():
                self.far(a).start()

            @pl.when(self.to[a] == self.fr)
            def _():
                self.near(a).start()

    def wait(self):
        for a in range(self.S):

            @pl.when(self.to[a] != self.fr)
            def _():
                self.far(a).wait_send()

            @pl.when(self.to[a] == self.fr)
            def _():
                self.near(a).wait()

            @pl.when(self.sender[a] != self.fr)
            def _():
                landed = self.dst.at[a]
                pltpu.make_async_copy(landed, landed, self.recv.at[a]).wait()


def move_sems(S):
    return [pltpu.SemaphoreType.DMA((S,))] * 3


def lanes_of(pair):
    return pl.ds(pl.multiple_of(pair * 128, 128), 128)


def mel_kernel(F, m_ref, e_ref, d_ref, h_ref, edge_send, edge_recv, edge_own, *sems):
    S = m_ref.shape[0]
    G = F // S
    dp, fr = lax.axis_index("dp"), lax.axis_index("frame")
    r = lax.rem(fr, G)
    meet(F)
    move = Move(True, F, m_ref, d_ref, sems)
    ends = []
    for a in range(S):
        last = (lax.rem(fr, S) == S - 1) & (fr + 1 < F)
        ends.append((a, 0, last, a * G + (fr + 1) // S))
        first = (lax.rem(fr, S) == 0) & (fr > 0)
        ends.append((a, 1, first, a * G + fr // S - 1))

    def far(a, k, to):
        return pltpu.make_async_remote_copy(
            src_ref=e_ref.at[a, k],
            dst_ref=h_ref.at[k],
            send_sem=edge_send.at[k, a],
            recv_sem=edge_recv.at[k],
            device_id=(dp, to),
            device_id_type=MESH,
        )

    def near(a, k):
        return pltpu.make_async_copy(e_ref.at[a, k], h_ref.at[k], edge_own.at[k])

    for a, k, holds, to in ends:

        @pl.when(holds & (to != fr))
        def _():
            far(a, k, to).start()

        @pl.when(holds & (to == fr))
        def _():
            near(a, k).start()

    move.start()
    for a, k, holds, to in ends:

        @pl.when(holds & (to != fr))
        def _():
            far(a, k, to).wait_send()

        @pl.when(holds & (to == fr))
        def _():
            near(a, k).wait()

    for k, wanted, sender in ((0, r > 0, r * S - 1), (1, r < G - 1, (r + 1) * S)):

        @pl.when(wanted & (sender != fr))
        def _():
            landed = h_ref.at[k]
            pltpu.make_async_copy(landed, landed, edge_recv.at[k]).wait()

    move.wait()


def gather_mel(pairs, F):
    S, piece, width = pairs.shape
    edges = jnp.stack([pairs[:, piece - 8 :], pairs[:, :8]], axis=1)
    far = pl.BlockSpec(memory_space=pl.ANY)
    return pl.pallas_call(
        functools.partial(mel_kernel, F),
        in_specs=[far, far],
        out_specs=[far, far],
        out_shape=[
            jax.ShapeDtypeStruct(pairs.shape, pairs.dtype),
            jax.ShapeDtypeStruct((2, 8, width), pairs.dtype),
        ],
        scratch_shapes=[
            pltpu.SemaphoreType.DMA((2, S)),
            pltpu.SemaphoreType.DMA((2,)),
            pltpu.SemaphoreType.DMA((2,)),
        ]
        + move_sems(S),
        compiler_params=pltpu.CompilerParams(
            collective_id=3, has_side_effects=True, vmem_limit_bytes=1 << 20
        ),
    )(pairs, edges)


def fwd_kernel(
    scale,
    hd,
    F,
    G,
    T,
    pairs,
    q_ref,
    k_own,
    v_own,
    c_ref,
    p_ref,
    o_ref,
    b_ref,
    k_all,
    v_all,
    d_ref,
    s_ref,
    k_buf,
    v_buf,
    send_sem,
    recv_sem,
    own_sem,
    out_sem,
    *sems,
):
    per = 128 // hd
    pair, i = pl.program_id(0), pl.program_id(1)
    rows = k_own.shape[0]
    both = ((k_own, k_buf), (v_own, v_buf))
    kept = ((k_buf, k_all), (v_buf, v_all))

    def own_copy(n, p):
        src, dst = both[n]
        return pltpu.make_async_copy(
            src.at[:, lanes_of(p)], dst.at[pl.ds(0, rows), lanes_of(p)], own_sem.at[n, p]
        )

    def keep(n, p):
        src, dst = kept[n]
        return pltpu.make_async_copy(
            src.at[:, lanes_of(p)], dst.at[:, lanes_of(p)], out_sem.at[n, p]
        )

    def copy_to(n, p, o):
        src, dst = both[n]
        return pltpu.make_async_remote_copy(
            src_ref=src.at[:, lanes_of(p)],
            dst_ref=dst.at[pl.ds((G - o) * rows, rows), lanes_of(p)],
            send_sem=send_sem.at[n, p, o - 1],
            recv_sem=recv_sem.at[n, p, o - 1],
            device_id=group_peer(G, o),
            device_id_type=MESH,
        )

    @pl.when((pair == 0) & (i == 0))
    def _():
        for p in range(pairs):
            for n in range(2):
                own_copy(n, p).start()
        meet(F)
        for p in range(pairs):
            for n in range(2):
                for o in range(1, G):
                    copy_to(n, p, o).start()
        Move(True, F, c_ref, d_ref, sems).start()

    @pl.when(i == 0)
    def _():
        for n in range(2):
            own_copy(n, pair).wait()
            for o in range(1, G):
                copy_to(n, pair, o).wait_recv()
            keep(n, pair).start()

    k = k_buf[:, lanes_of(pair)]
    vt = v_buf[:, lanes_of(pair)].T
    outs = []
    for h in range(per):
        q = q_ref[...]
        q = jnp.where(half_mask(q.shape, h, hd), q, jnp.zeros_like(q))
        s_ref[h] = lax.dot_general(k, q, (((1,), (1,)), ((), ())), preferred_element_type=F32)
    for h in range(per):
        s = s_ref[h]
        if rows != T:
            at = lax.rem(lax.broadcasted_iota(jnp.int32, s.shape, 0), rows)
            s = jnp.where(at < T, s, -1e30)
        m = jnp.max(s, axis=0, keepdims=True)
        e = jnp.exp((s - m) * scale)
        l = jnp.sum(e, axis=0, keepdims=True)
        p = (e * (1.0 / l)).astype(BF16)
        p_ref[h] = p
        outs.append(jnp.dot(vt[h * hd : (h + 1) * hd], p, preferred_element_type=F32))
    out = jnp.concatenate(outs, axis=0).T
    o_ref[...] = out
    b_ref[...] = out.astype(BF16)

    @pl.when((pair == pairs - 1) & (i == pl.num_programs(1) - 1))
    def _():
        for p in range(pairs):
            for n in range(2):
                keep(n, p).wait()
                for o in range(1, G):
                    copy_to(n, p, o).wait_send()
        Move(True, F, c_ref, d_ref, sems).wait()


def attn_fwd(q, k, v, slots, scale, heads, QB, F, T):
    G = F // slots.shape[0]
    R, D = q.shape
    N = k.shape[0] * G
    hd = D // heads
    per = 128 // hd
    pairs = D // 128
    far = pl.BlockSpec(memory_space=pl.ANY)
    sems = pltpu.SemaphoreType.DMA((2, pairs, G - 1))
    return pl.pallas_call(
        functools.partial(fwd_kernel, scale, hd, F, G, T, pairs),
        grid=(pairs, R // QB),
        in_specs=[pl.BlockSpec((QB, 128), lambda p, i: (i, p)), far, far, far],
        out_specs=[
            pl.BlockSpec((per, N, QB), lambda p, i: (p, 0, i)),
            pl.BlockSpec((QB, 128), lambda p, i: (i, p)),
            pl.BlockSpec((QB, 128), lambda p, i: (i, p)),
            far,
            far,
            far,
        ],
        out_shape=[
            jax.ShapeDtypeStruct((heads, N, R), BF16),
            jax.ShapeDtypeStruct((R, D), F32),
            jax.ShapeDtypeStruct((R, D), BF16),
            jax.ShapeDtypeStruct((N, D), BF16),
            jax.ShapeDtypeStruct((N, D), BF16),
            jax.ShapeDtypeStruct(slots.shape, slots.dtype),
        ],
        scratch_shapes=[
            pltpu.VMEM((per, N, QB), F32),
            pltpu.VMEM((N, D), BF16),
            pltpu.VMEM((N, D), BF16),
            sems,
            sems,
            pltpu.SemaphoreType.DMA((2, pairs)),
            pltpu.SemaphoreType.DMA((2, pairs)),
        ]
        + move_sems(slots.shape[0]),
        compiler_params=pltpu.CompilerParams(
            collective_id=1, has_side_effects=True, vmem_limit_bytes=60 << 20
        ),
    )(q, k, v, slots)


def bwd_kernel(
    scale,
    hd,
    F,
    G,
    pairs,
    q_ref,
    do_ref,
    o_ref,
    k_ref,
    v_ref,
    p_ref,
    y_ref,
    dq_ref,
    dk_ref,
    dv_ref,
    z_ref,
    dp_ref,
    kt_ref,
    acc_ref,
    got_ref,
    send_sem,
    recv_sem,
    *sems,
):
    per = 128 // hd
    pair, i = pl.program_id(0), pl.program_id(1)
    slot = lax.rem(pair, 2)
    rows = dk_ref.shape[0]

    def copy_to(n, p, o):
        return pltpu.make_async_remote_copy(
            src_ref=acc_ref.at[lax.rem(p, 2), n, pl.ds(o * rows, rows)],
            dst_ref=got_ref.at[p, n, o - 1],
            send_sem=send_sem.at[n, p, o - 1],
            recv_sem=recv_sem.at[n, p, o - 1],
            device_id=group_peer(G, o),
            device_id_type=MESH,
        )

    every = [(n, o) for n in range(2) for o in range(1, G)]

    @pl.when((pair == 0) & (i == 0))
    def _():
        meet(F)
        Move(False, F, y_ref, z_ref, sems).start()

    @pl.when((pair >= 2) & (i == 0))
    def _():
        for n, o in every:
            copy_to(n, pair - 2, o).wait_send()

    @pl.when(i == 0)
    def _():
        kt_ref[...] = k_ref[...].T
        acc_ref[slot] = jnp.zeros(acc_ref.shape[1:], F32)

    do = do_ref[...]
    q = q_ref[...]
    v = v_ref[...]
    prod = (do.astype(F32) * o_ref[...]).T
    for h in range(per):
        doh = jnp.where(half_mask(do.shape, h, hd), do, jnp.zeros_like(do))
        dp_ref[h] = lax.dot_general(v, doh, (((1,), (1,)), ((), ())), preferred_element_type=F32)
    dqs = []
    for h in range(per):
        doh = jnp.where(half_mask(do.shape, h, hd), do, jnp.zeros_like(do))
        qh = jnp.where(half_mask(q.shape, h, hd), q, jnp.zeros_like(q))
        delta = jnp.sum(prod[h * hd : (h + 1) * hd], axis=0, keepdims=True)
        p = p_ref[h]
        ds = (p.astype(F32) * (dp_ref[h] - delta)).astype(BF16)
        acc_ref[slot, 1] += jnp.dot(p, doh, preferred_element_type=F32)
        acc_ref[slot, 0] += jnp.dot(ds, qh, preferred_element_type=F32)
        dqs.append(jnp.dot(kt_ref[h * hd : (h + 1) * hd], ds, preferred_element_type=F32))
    dq_ref[...] = (jnp.concatenate(dqs, axis=0) * scale).T.astype(BF16)

    def finish(p):
        for n, o in every:
            copy_to(n, p, o).wait_recv()
        for n, out, factor in ((0, dk_ref, scale), (1, dv_ref, 1.0)):
            total = acc_ref[lax.rem(p, 2), n, pl.ds(0, rows)]
            for o in range(1, G):
                total = total + got_ref[p, n, o - 1]
            out[:, lanes_of(p)] = (total * factor).astype(BF16)

    ends = i == pl.num_programs(1) - 1

    @pl.when(ends & (pair >= 1))
    def _():
        finish(pair - 1)

    @pl.when(ends)
    def _():
        for n, o in every:
            copy_to(n, pair, o).start()

    @pl.when(ends & (pair == pairs - 1))
    def _():
        finish(pair)
        for p in range(max(pairs - 2, 0), pairs):
            for n, o in every:
                copy_to(n, p, o).wait_send()
        Move(False, F, y_ref, z_ref, sems).wait()


def attn_bwd(q, do, o, k, v, p, pieces, scale, heads, QB, F):
    G = F // pieces.shape[0]
    far = pl.BlockSpec(memory_space=pl.ANY)
    R, D = q.shape
    N = k.shape[0]
    hd = D // heads
    per = 128 // hd
    pairs = D // 128
    row = pl.BlockSpec((QB, 128), lambda p, i: (i, p))
    key = pl.BlockSpec((N, 128), lambda p, i: (0, p))
    near = pl.BlockSpec(memory_space=pltpu.VMEM)
    sems = pltpu.SemaphoreType.DMA((2, pairs, G - 1))
    own = jax.ShapeDtypeStruct((N // G, D), BF16)
    return pl.pallas_call(
        functools.partial(bwd_kernel, scale, hd, F, G, pairs),
        grid=(pairs, R // QB),
        in_specs=[row, row, row, key, key, pl.BlockSpec((per, N, QB), lambda p, i: (p, 0, i)), far],
        out_specs=[row, near, near, far],
        out_shape=[
            jax.ShapeDtypeStruct((R, D), BF16),
            own,
            own,
            jax.ShapeDtypeStruct(pieces.shape, pieces.dtype),
        ],
        scratch_shapes=[
            pltpu.VMEM((per, N, QB), F32),
            pltpu.VMEM((128, N), BF16),
            pltpu.VMEM((2, 2, N, 128), F32),
            pltpu.VMEM((pairs, 2, G - 1, N // G, 128), F32),
            sems,
            sems,
        ]
        + move_sems(pieces.shape[0]),
        compiler_params=pltpu.CompilerParams(
            collective_id=2, has_side_effects=True, vmem_limit_bytes=60 << 20
        ),
    )(q, do, o, k, v, p, pieces)


TILE = 512
LAG = 3
AHEAD = 2


def pick(c, values):
    out = values[0]
    for n in range(1, len(values)):
        if values[n] != values[n - 1]:
            out = jnp.where(c >= n, values[n], out)
    return out


class Rest:
    FIRST = 5

    def __init__(self, G, T, taps, m_ref, t_ref, w_ref, data, scratch, sems):
        self.m, self.t, self.w = m_ref, t_ref, w_ref
        self.data = data
        self.ext, self.edge, self.halo, self.sg, self.y0, self.y1, self.y2 = scratch
        self.send, self.recv = sems
        self.G, self.T, self.taps = G, T, taps
        self.R = self.sg.shape[0]
        self.row = lax.rem(lax.axis_index("frame"), G)
        self.size = 256 if self.R % 256 == 0 else 128
        self.token_blocks = [(a, min(a + 256, T)) for a in range(0, T, 256)]
        self.edges_at = self.FIRST + len(self.token_blocks)
        self.halo_at = self.edges_at + 2
        self.stem_at = self.halo_at + 1
        self.mel_at = self.stem_at + self.R // self.size
        self.weights_at = self.mel_at + 1
        self.halo[...] = jnp.zeros_like(self.halo)

    def due(self, name):
        if name in ("reduce", "stem_linear", "stem_taps"):
            return self.stem_at
        if name in ("columns", "second_gain", "second_shift"):
            return self.weights_at
        return self.FIRST

    def tokens(self, n):
        a, b = self.token_blocks[n]
        q, k, v, conv, base = self.taps
        data, rows = self.data, pl.ds(a, b - a)
        dy = (
            dot_t(self.m[q, rows], data["query"][...])
            + dot_t(self.m[k, rows], data["key"][...])
            + dot_t(self.m[v, rows], data["value"][...])
        )
        xhat, r = norm_parts(data["stream"][rows])
        dh = dy * data["gain"][...]
        inner = r * (
            dh
            - jnp.mean(dh, axis=-1, keepdims=True)
            - xhat * jnp.mean(dh * xhat, axis=-1, keepdims=True)
        )
        self.t[base + 1 : base + 2] += jnp.sum(dy * xhat, axis=0, keepdims=True)
        self.t[base + 2 : base + 3] += jnp.sum(dy, axis=0, keepdims=True)
        grad = gelu_slope(data["conv_linear"][rows]) * (data["mixed"][rows] + inner)
        grad = grad.astype(BF16)
        self.m[conv, rows] = grad
        self.ext[rows] = grad
        if n == 0:
            self.edge[1] = grad[:16]
            self.ext[pl.ds(self.R, 16)] = grad[:16]
        if b == self.T:
            self.edge[0] = grad[b - a - 16 :]

    def edge_copy(self, n):
        return pltpu.make_async_remote_copy(
            src_ref=self.edge.at[n],
            dst_ref=self.halo.at[n],
            send_sem=self.send.at[n],
            recv_sem=self.recv.at[n],
            device_id=group_peer(self.G, 1 if n == 0 else self.G - 1),
            device_id_type=MESH,
        )

    def has(self, n):
        return self.row < self.G - 1 if n == 0 else self.row > 0

    def send_edges(self):
        for n in range(2):

            @pl.when(self.has(n))
            def _():
                self.edge_copy(n).start()

    def fill_halo(self):
        for n in range(2):

            @pl.when(self.has(1 - n))
            def _():
                landed = self.halo.at[n]
                pltpu.make_async_copy(landed, landed, self.recv.at[n]).wait()

        at = self.T // 16 * 16
        rows = pl.ds(at, self.R - at)
        own = self.ext[rows].astype(F32)
        place = lax.broadcasted_iota(jnp.int32, own.shape, 0) + at
        before = self.halo[0].astype(F32)[15:16]
        after = self.halo[1].astype(F32)[:1]
        own = jnp.where(place < self.T, own, 0.0)
        own = jnp.where(place == self.T, after, own)
        own = jnp.where(place == self.R - 1, before, own)
        self.ext[rows] = own.astype(BF16)

    def stem(self, n):
        data, a = self.data, n * self.size
        D = self.ext.shape[1]
        rows = pl.ds(a, self.size)
        pair = dot_t(self.ext[rows], data["reduce"][pl.ds(D, 2 * D)])
        third = dot_t(self.ext[pl.ds(a, self.size + 16)], data["reduce"][pl.ds(0, D)])
        third = third[1 : self.size + 1]
        active = jnp.concatenate([pair[:, :D], pair[:, D:] + third], axis=1)
        place = lax.broadcasted_iota(jnp.int32, active.shape, 0) + a
        high = self.T + jnp.where(self.row < self.G - 1, 1, 0)
        low = self.R - jnp.where(self.row > 0, 1, 0)
        grad = gelu_slope(data["stem_linear"][rows]) * active
        grad = jnp.where((place < high) | (place >= low), grad, 0.0).astype(BF16)
        self.sg[rows] = grad
        self.y0[rows] = dot_t(grad, data["stem_taps"][0])
        y1 = dot_t(grad, data["stem_taps"][1])
        self.y1[pl.ds(a + 8, self.size)] = y1
        if a + self.size == self.R:
            self.y1[pl.ds(0, 8)] = y1[self.size - 8 :]
        self.y2[rows] = dot_t(grad, data["stem_taps"][2])

    def mel(self, out):
        T = self.T
        total = self.y0[pl.ds(0, T)] + self.y1[pl.ds(7, T)] + self.y2[pl.ds(1, T)]
        n = out.shape[1]
        for j in range(out.shape[0]):
            out[j] = total[j * n : (j + 1) * n]

    def weights(self):
        base = self.taps[-1]
        D = self.ext.shape[1]
        own = self.sg[pl.ds(0, self.T)]
        wide = outer(self.data["columns"][pl.ds(0, self.T)], own)
        mels = wide.shape[0] // 4
        sums = dot(jnp.ones((16, self.T), BF16), own)[:1]
        self.w[self.w.shape[0] - 1, pl.ds(0, 3 * mels)] = (
            wide[: 3 * mels, :D] + wide[mels:, D:]
        ).astype(BF16)
        self.t[base : base + 1] = sums[:, :D] + sums[:, D:]
        self.t[base + 3 : base + 4] = self.data["second_gain"][...]
        self.t[base + 4 : base + 5] = self.data["second_shift"][...]

    def step(self, t, out):
        todo = [(self.FIRST + n, functools.partial(self.tokens, n)) for n in range(len(self.token_blocks))]
        todo.append((self.edges_at, self.send_edges))
        todo.append((self.halo_at, self.fill_halo))
        todo += [
            (self.stem_at + n, functools.partial(self.stem, n)) for n in range(self.R // self.size)
        ]
        todo.append((self.mel_at, functools.partial(self.mel, out)))
        todo.append((self.weights_at, self.weights))
        for at, work in todo:
            pl.when(t == at)(work)

    def drain(self):
        for n in range(2):

            @pl.when(self.has(n))
            def _():
                self.edge_copy(n).wait_send()


REST = (
    "query",
    "key",
    "value",
    "stream",
    "gain",
    "mixed",
    "conv_linear",
    "reduce",
    "stem_linear",
    "stem_taps",
    "columns",
    "second_gain",
    "second_shift",
)


def sum_kernel(sizes, F, used, plan, *refs):
    places, left_at, right_at, lefts, rights, n_in, n_out, taps, T = plan
    extra = len(REST)
    in_refs, rest_refs = refs[: n_in - extra], refs[n_in - extra : n_in]
    g_refs, slot_ref = refs[n_in : n_in + n_out - 1], refs[n_in + n_out - 1]
    refs = refs[n_in + n_out :]
    l_ref, m_ref, t_ref, w_ref, s_ref, r0, r1, r2, r3 = refs[:9]
    kept, work = refs[9 : 9 + extra], refs[9 + extra : 16 + extra]
    piece_ref, send_sem, recv_sem, load_sem, out_sem, edge_send, edge_recv, *sems = refs[16 + extra :]
    t_ref[...] = jnp.zeros_like(t_ref)
    w_ref[len(places) - 1] = jnp.zeros(w_ref.shape[1:], BF16)
    G = F // slot_ref.shape[0]
    rest = Rest(
        G, T, taps, m_ref, t_ref, w_ref, dict(zip(REST, kept)), work, (edge_send, edge_recv)
    )
    recv = (r0, r1, r2, r3)
    chunks = len(places)
    Y = sizes[2]
    dp = lax.axis_index("dp")
    fr = lax.axis_index("frame")
    z = dp // Y
    y = lax.rem(dp, Y)
    x = fr // 2
    core = lax.rem(fr, 2)
    first = core == 0
    me = (core, jnp.where(first, x, y), jnp.where(first, y, x), z)

    loads, due = [], []
    for buf, sources, at in ((l_ref, lefts, left_at), (m_ref, rights, right_at)):
        for n, (which, col) in enumerate(sources):
            if which is None:
                continue
            src = in_refs[which].at[pl.ds(0, T), pl.ds(col, TILE)]
            loads.append(pltpu.make_async_copy(src, buf.at[n], load_sem.at[len(loads)]))
            first_use = at.index(n)
            due.append(min(first_use, rest.FIRST) if at is right_at and n in taps[:3] else first_use)
    for name, src, dst in zip(REST, rest_refs, kept):
        loads.append(pltpu.make_async_copy(src, dst, load_sem.at[len(loads)]))
        due.append(rest.due(name))
    for n in sorted(range(len(loads)), key=lambda n: (due[n], n)):
        loads[n].start()

    def device(kind, p):
        if kind == 0:
            return (dp, x * 2 + p)
        if kind == 3:
            return (p * Y + y, fr)
        along_x = first if kind == 1 else jnp.logical_not(first)
        return (z * Y + jnp.where(along_x, y, p), jnp.where(along_x, p, x) * 2 + core)

    def peer(k, o):
        return lax.rem(me[k] + o, sizes[k])

    pairs = [(k, o) for k in range(4) for o in range(1, sizes[k])]
    barrier = pltpu.get_barrier_semaphore()
    for k, o in pairs:
        pl.semaphore_signal(barrier, inc=1, device_id=device(k, peer(k, o)), device_id_type=MESH)
    greet(F)
    pl.semaphore_wait(barrier, len(pairs) + F - 1)
    move = Move(False, F, piece_ref, slot_ref, sems)

    cut = [TILE]
    for k in range(4):
        cut.append(cut[-1] // sizes[k])
    split = cut[4] % 16 == 0
    if not split:
        cut[4] = cut[3]

    def start_of(level):
        at = 0
        for k in range(level):
            if k < 3 or split:
                at = at + me[k] * cut[k + 1]
        return pl.multiple_of(at, 16) if level else 0

    def scatter_copy(c, k, o):
        p = peer(k, o)
        at = start_of(k)
        if k < 3 or split:
            at = pl.multiple_of(at + p * cut[k + 1], 16)
        return pltpu.make_async_remote_copy(
            src_ref=w_ref.at[c, pl.ds(at, cut[k + 1])],
            dst_ref=recv[k].at[c, o - 1],
            send_sem=send_sem.at[c, k, o - 1],
            recv_sem=recv_sem.at[c, k, o - 1],
            device_id=device(k, p),
            device_id_type=MESH,
        )

    def gather_copy(c, k, o):
        here = s_ref.at[c, pl.ds(start_of(k + 1), cut[k + 1])]
        return pltpu.make_async_remote_copy(
            src_ref=here,
            dst_ref=here,
            send_sem=send_sem.at[c, 4 + k, o - 1],
            recv_sem=recv_sem.at[c, 4 + k, o - 1],
            device_id=device(k, peer(k, o)),
            device_id_type=MESH,
        )

    def out_copy(c):
        which, row, col = places[c]
        dst = g_refs[which].at[pl.ds(row, TILE), pl.ds(col, TILE)]
        return pltpu.make_async_copy(s_ref.at[c], dst, out_sem.at[c])

    def add(c, k):
        at = start_of(k + 1)
        dst = w_ref if k < 3 else s_ref
        step = math.gcd(cut[k + 1], 64)

        def body(i, _):
            r = pl.multiple_of(at + i * step, 16)
            total = w_ref[c, pl.ds(r, step)].astype(F32)
            for o in range(1, sizes[k]):
                total = total + recv[k][
                    c, o - 1, pl.ds(pl.multiple_of(i * step, 16), step)
                ].astype(F32)
            dst[c, pl.ds(r, step)] = total.astype(BF16)
            return 0

        lax.fori_loop(0, cut[k + 1] // step, body, 0)

    stages = [("s", k) for k in range(4)] + [("g", k) for k in (3, 2, 1, 0) if k < 3 or split]
    copies = {"s": scatter_copy, "g": gather_copy}

    def finish(c, n):
        kind, k = stages[n]
        for o in range(1, sizes[k]):
            copies[kind](c, k, o).wait_recv()
        if kind == "s":
            add(c, k)
        if n + 1 < len(stages):
            kind, k = stages[n + 1]
            for o in range(1, sizes[k]):
                copies[kind](c, k, o).start()

    turns = [AHEAD]
    for n in range(1, len(stages)):
        turns.append(turns[-1] + (LAG if stages[n][1] else LAG - 1))
    last = turns[-1]

    def turn(t, _):
        for n in range(len(loads)):

            @pl.when(t == due[n])
            def _():
                loads[n].wait()

        @pl.when(t < chunks - 1)
        def _():
            left = l_ref[pick(t, left_at)]
            right = m_ref[pick(t, right_at)]
            w_ref[t] = outer(left, right).astype(BF16)
            ones = jnp.ones((16, T), BF16)
            t_ref[pl.ds(pick(t, right_at), 1)] = dot(ones, right)[:1]

        @pl.when(t == rest.weights_at)
        def _():
            move.start()

        rest.step(t, piece_ref)

        @pl.when(t == chunks - 1)
        def _():
            w_ref[chunks - 1, pl.ds(used, t_ref.shape[0])] = t_ref[...].astype(BF16)

        @pl.when((t >= 1) & (t <= chunks))
        def _():
            for o in range(1, sizes[0]):
                scatter_copy(t - 1, 0, o).start()

        for n in range(len(stages) - 1, -1, -1):
            c = t - turns[n]

            @pl.when((c >= 0) & (c < chunks))
            def _():
                finish(c, n)

        for c in range(chunks):

            @pl.when(t == c + last)
            def _():
                out_copy(c).start()

        return 0

    lax.fori_loop(0, chunks + last, turn, 0)

    def drain(c, _):
        for kind, k in stages:
            for o in range(1, sizes[k]):
                copies[kind](c, k, o).wait_send()
        return 0

    lax.fori_loop(0, chunks, drain, 0)
    move.wait()
    rest.drain()
    for c in range(chunks):
        out_copy(c).wait()


def sum_everywhere(products, rest, taps, used, S, F, sizes, cid):
    arrays, lefts, rights = [], [], []
    places, left_at, right_at, shapes = [], [], [], []

    def slots_of(pieces, slots):
        found = []
        for array, width in pieces:
            which = None
            if array is not None:
                which = next((n for n, a in enumerate(arrays) if a is array), None)
                if which is None:
                    which = len(arrays)
                    arrays.append(array)
            for col in range(0, width, TILE):
                if (which, col) not in slots:
                    slots.append((which, col))
                found.append(slots.index((which, col)))
        return found

    for n, (left, right) in enumerate(products):
        a, b = slots_of(left, lefts), slots_of(right, rights)
        shapes.append((len(a) * TILE, len(b) * TILE))
        for i, u in enumerate(a):
            for j, v in enumerate(b):
                places.append((n, i * TILE, j * TILE))
                left_at.append(u)
                right_at.append(v)
    places.append((len(products), 0, 0))
    shapes.append((TILE, TILE))
    T = min(a.shape[0] for a in arrays)
    R = rest["stem_linear"].shape[0]
    mels = rest["columns"].shape[1] // 4
    chunks = len(places)
    cut = [TILE]
    for n in sizes:
        cut.append(cut[-1] // n)
    if cut[4] % 16:
        cut[4] = cut[3]
    most = max(sizes) - 1
    spec = pl.BlockSpec(memory_space=pl.ANY)
    sums = len(rights) + 5
    sums += -sums % 16
    slots = jax.ShapeDtypeStruct((S, T // S, 2 * mels), F32)
    taps = tuple(right_at[n] for n in taps) + (len(rights),)
    plan = (
        places,
        left_at,
        right_at,
        lefts,
        rights,
        len(arrays) + len(REST),
        len(shapes) + 1,
        taps,
        T,
    )
    return pl.pallas_call(
        functools.partial(sum_kernel, sizes, F, used, plan),
        in_specs=[spec] * (len(arrays) + len(REST)),
        out_specs=[spec] * (len(shapes) + 1),
        out_shape=[jax.ShapeDtypeStruct(v, BF16) for v in shapes] + [slots],
        scratch_shapes=[
            pltpu.VMEM((len(lefts), T, TILE), BF16),
            pltpu.VMEM((len(rights), T, TILE), BF16),
            pltpu.VMEM((sums, TILE), F32),
        ]
        + [pltpu.VMEM((chunks, TILE, TILE), BF16)] * 2
        + [pltpu.VMEM((chunks, sizes[k] - 1, cut[k + 1], TILE), BF16) for k in range(4)]
        + [pltpu.VMEM(rest[name].shape, rest[name].dtype) for name in REST]
        + [
            pltpu.VMEM((R + 16, TILE), BF16),
            pltpu.VMEM((2, 16, TILE), BF16),
            pltpu.VMEM((2, 16, TILE), BF16),
            pltpu.VMEM((R, 2 * TILE), BF16),
            pltpu.VMEM((R, 2 * mels), F32),
            pltpu.VMEM((R + 8, 2 * mels), F32),
            pltpu.VMEM((R, 2 * mels), F32),
            pltpu.VMEM(slots.shape, F32),
        ]
        + [
            pltpu.SemaphoreType.DMA((chunks, 8, most)),
            pltpu.SemaphoreType.DMA((chunks, 8, most)),
            pltpu.SemaphoreType.DMA((len(lefts) + len(rights) + len(REST),)),
            pltpu.SemaphoreType.DMA((chunks,)),
            pltpu.SemaphoreType.DMA((2,)),
            pltpu.SemaphoreType.DMA((2,)),
        ]
        + move_sems(S),
        compiler_params=pltpu.CompilerParams(
            collective_id=cid, has_side_effects=True, vmem_limit_bytes=67043328
        ),
    )(*arrays, *[rest[name] for name in REST])


def widen_kernel(parts, count, *refs):
    ins, outs = refs[:count], refs[count : 2 * count + 1]
    b_ref, f_ref, load_sem, out_sem = refs[2 * count + 1 :]
    loads, stores = [], []
    for n, (which, row, col, places) in enumerate(parts):
        rows = pl.ds(row, TILE)
        cols = pl.ds(col, TILE)
        loads.append(
            pltpu.make_async_copy(ins[which].at[rows, cols], b_ref.at[n], load_sem.at[n])
        )
        here = []
        for out, at, first, size in places:
            target = outs[out].at[pl.ds(at, size), cols]
            source = f_ref.at[n, pl.ds(first, size)]
            here.append(pltpu.make_async_copy(source, target, out_sem.at[n, len(here)]))
        stores.append(here)
    for load in loads:
        load.start()
    for n, load in enumerate(loads):
        load.wait()

        def body(i, _):
            rows = pl.ds(pl.multiple_of(i * 64, 64), 64)
            f_ref[n, rows] = b_ref[n, rows].astype(F32)
            return 0

        lax.fori_loop(0, TILE // 64, body, 0)
        for store in stores[n]:
            store.start()
    for here in stores:
        for store in here:
            store.wait()


def widen(arrays, used, sums):
    parts = []
    last = len(arrays) - 1
    for n, a in enumerate(arrays):
        for row in range(0, a.shape[0], TILE):
            for col in range(0, a.shape[1], TILE):
                places = [(n, row, 0, TILE)]
                if n == last:
                    places = [(n, 0, 0, used[0]), (n + 1, 0, used[1], sums)]
                parts.append((n, row, col, places))
    shapes = [a.shape for a in arrays[:-1]] + [(used[0], TILE), (sums, TILE)]
    far = pl.BlockSpec(memory_space=pl.ANY)
    return pl.pallas_call(
        functools.partial(widen_kernel, parts, len(arrays)),
        in_specs=[far] * len(arrays),
        out_specs=[far] * len(shapes),
        out_shape=[jax.ShapeDtypeStruct(v, F32) for v in shapes],
        scratch_shapes=[
            pltpu.VMEM((len(parts), TILE, TILE), BF16),
            pltpu.VMEM((len(parts), TILE, TILE), F32),
            pltpu.SemaphoreType.DMA((len(parts),)),
            pltpu.SemaphoreType.DMA((len(parts), 2)),
        ],
        compiler_params=pltpu.CompilerParams(vmem_limit_bytes=67043328),
    )(*arrays)


def on_device(
    mel_frames,
    window_count,
    stem_weight,
    stem_bias,
    reduce_weight,
    reduce_bias,
    first_gain,
    first_shift,
    query_weight,
    query_bias,
    key_weight,
    value_weight,
    value_bias,
    output_weight,
    output_bias,
    second_gain,
    second_shift,
    hidden_weight,
    hidden_bias,
    return_weight,
    return_bias,
    cotangent,
):
    S, piece_frames, mels = mel_frames.shape
    piece = cotangent.shape[1]
    D = stem_weight.shape[2]
    hd = D // HEADS
    scale = hd ** (-0.5)
    F = lax.axis_size("frame")
    G = F // S
    T = S * piece
    R = -(-(T + 2) // 128) * 128
    f = lax.axis_index("frame")
    s = f // G
    r = f % G
    alive = s < window_count[0]

    own, beside = gather_mel(mel_frames.reshape(S, piece, 2 * mels), F)
    before = jnp.where(r > 0, beside[0, -1:], jnp.zeros((1, 2 * mels), BF16))
    after = jnp.where(r < G - 1, beside[1, :1], jnp.zeros((1, 2 * mels), BF16))
    gap = jnp.zeros((R - T - 2, 2 * mels), BF16)
    mel = jnp.concatenate([own.reshape(T, 2 * mels), after, gap, before], axis=0)
    odd_before = jnp.roll(mel[:, mels:], 1, axis=0)
    even_after = jnp.roll(mel[:, :mels], -1, axis=0)
    columns = jnp.concatenate([odd_before, mel, even_after], axis=1)
    stem_matrix = stem_weight.reshape(3 * mels, D)
    gap = jnp.zeros((mels, D), BF16)
    stem_pair = jnp.concatenate(
        [
            jnp.concatenate([stem_matrix, gap], axis=0),
            jnp.concatenate([gap, stem_matrix], axis=0),
        ],
        axis=1,
    )
    stem_bias2 = jnp.concatenate([stem_bias, stem_bias])
    stem_linear = dot(columns, stem_pair) + stem_bias2
    row = lax.broadcasted_iota(jnp.int32, (R, 1), 0)
    valid = (row < T) | ((row == T) & (r < G - 1)) | ((row == R - 1) & (r > 0))
    stem_active = jnp.where(valid, gelu(stem_linear), 0.0).astype(BF16)

    odd_active_before = jnp.roll(stem_active[:, D:], 1, axis=0)[:T]
    conv_columns = jnp.concatenate([odd_active_before, stem_active[:T]], axis=1)
    reduce_matrix = reduce_weight.reshape(3 * D, D)
    conv_linear = dot(conv_columns, reduce_matrix) + reduce_bias
    stream = gelu(conv_linear) + positions_of(r * T, T, D)
    xhat1, r1 = norm_parts(stream)
    first_normed = (xhat1 * first_gain + first_shift).astype(BF16)
    tail = ((0, R - T), (0, 0))
    query_ext = (dot(jnp.pad(first_normed, tail), query_weight) + query_bias).astype(BF16)
    key = dot(first_normed, key_weight).astype(BF16)
    value = (dot(first_normed, value_weight) + value_bias).astype(BF16)
    key = jnp.pad(key, ((0, -T % 16), (0, 0)))
    value = jnp.pad(value, ((0, -T % 16), (0, 0)))
    block = 384 if R % 384 == 0 else 128
    probs, attended_wide, attended, key_all, value_all, cot = attn_fwd(
        query_ext, key, value, cotangent, scale, HEADS, block, F, T
    )
    cot = cot.reshape(T, D)
    cot = jnp.where(alive, cot, jnp.zeros_like(cot))
    mixed = stream + dot(attended[:T], output_weight) + output_bias
    xhat2, r2 = norm_parts(mixed)
    second_normed = (xhat2 * second_gain + second_shift).astype(BF16)
    hidden_linear = dot(second_normed, hidden_weight) + hidden_bias
    hidden_cdf, hidden_pdf = phi_parts(hidden_linear)
    hidden_active = (hidden_linear * hidden_cdf).astype(BF16)
    layer = mixed + dot(hidden_active, return_weight) + return_bias
    layer = jnp.where(alive, layer, 0.0).astype(BF16)

    slope = hidden_cdf + hidden_linear * hidden_pdf
    hidden_grad = (slope * dot_t(cot, return_weight)).astype(BF16)
    inner, second_gain_grad, second_shift_grad = norm_pull(
        xhat2, r2, second_gain, dot_t(hidden_grad, hidden_weight)
    )
    mixed_grad = cot.astype(F32) + inner
    branch_grad = mixed_grad.astype(BF16)

    attended_grad = dot_t(jnp.pad(branch_grad, tail), output_weight).astype(BF16)
    query_wide, key_grad, value_grad, layer_output = attn_bwd(
        query_ext,
        attended_grad,
        attended_wide,
        key_all,
        value_all,
        probs,
        layer.reshape(S, piece, D),
        scale,
        HEADS,
        block,
        F,
    )
    key_grad, value_grad = key_grad[:T], value_grad[:T]
    sizes = (2, F // 2, F // 2, lax.axis_size("dp") // (F // 2))
    used = 3 * mels + -3 * mels % 16
    none = jnp.zeros((mels, 2 * D), BF16)
    taps = [
        stem_pair[mels : 3 * mels],
        jnp.concatenate([stem_pair[3 * mels :], none], axis=0),
        jnp.concatenate([none, stem_pair[:mels]], axis=0),
    ]
    rest = {
        "query": query_weight,
        "key": key_weight,
        "value": value_weight,
        "stream": stream,
        "gain": first_gain.reshape(1, D),
        "mixed": mixed_grad,
        "conv_linear": conv_linear,
        "reduce": reduce_matrix,
        "stem_linear": stem_linear,
        "stem_taps": jnp.stack(taps),
        "columns": columns,
        "second_gain": second_gain_grad.reshape(1, D),
        "second_shift": second_shift_grad.reshape(1, D),
    }
    FF = hidden_weight.shape[1]
    wide = FF // D
    one = [(first_normed, D)]
    *terms, mel_slots = sum_everywhere(
        [
            ([(hidden_active, FF)], [(cot, D)]),
            ([(second_normed, D)], [(hidden_grad, FF)]),
            ([(attended, D)], [(branch_grad, D)]),
            (one, [(query_wide, D)]),
            (one, [(key_grad, D)]),
            (one, [(value_grad, D)]),
            ([(odd_active_before, D), (stem_active, 2 * D)], [(None, D)]),
        ],
        rest,
        (2 * wide + 1, 2 * wide + 2, 2 * wide + 3, 2 * wide + 4),
        used,
        S,
        F,
        sizes,
        0,
    )
    mel_gradient = mel_slots.reshape(S, piece_frames, mels)
    rows = wide + 11
    rows += -rows % 16
    return_w, hidden_w, output_w, query_w, key_w, value_w, reduce_w, stem_w, sums = widen(
        terms, (3 * mels, used), rows
    )
    small = wide + 6
    return (
        layer_output,
        mel_gradient,
        stem_w.reshape(3, mels, D),
        sums[small],
        reduce_w.reshape(3, D, D),
        sums[wide + 5],
        sums[small + 1],
        sums[small + 2],
        query_w,
        sums[wide + 2],
        key_w,
        value_w,
        sums[wide + 4],
        output_w,
        sums[wide + 1],
        sums[small + 3],
        sums[small + 4],
        hidden_w,
        sums[1 : wide + 1].reshape(FF),
        return_w,
        sums[0],
    )


def solution(mesh):
    cut = P("dp", "frame", None)
    return jax.shard_map(
        on_device,
        mesh=mesh,
        in_specs=(cut, P("dp")) + (P(),) * 19 + (cut,),
        out_specs=(cut, cut) + (P(),) * 19,
        check_vma=False,
    )
```
